256 devices in a mesh: dp: 16 (over y, z_hi), mp: 16 (over x, z_lo, core).
Axes of the slice: x: 4, y: 4, z: 8 (z_hi: 4, z_lo: 2; z = z_hi * 2 + z_lo), core: 2. Of those that a mesh axis runs over, the one named last changes fastest.
Arguments:
- tokens: bfloat16 [4096, 4096], P('dp', 'mp'), may hold values from -6 to 6
- norm_gain: float32 [4096], P('mp'), may hold values from 0.75 to 7.5
- w_gate: bfloat16 [4096, 6144], P('dp', 'mp'), may hold values from -0.09375 to 0.09375
- w_up: bfloat16 [4096, 6144], P('dp', 'mp'), may hold values from -0.09375 to 0.09375
- cotangent: bfloat16 [4096, 6144], P('dp', 'mp'), may hold values from -0.09375 to 0.09375
- decay_mask: int32 [2, 4096], replicated, may hold values 0 or 1
- radius: float32 [1], replicated, may hold values from 12.8 to 38.4
Outputs:
- grad_gain: float32 [4096], P('mp')
- grad_gate: float32 [4096, 6144], P('dp', 'mp')
- grad_up: float32 [4096, 6144], P('dp', 'mp')
The draws below stay inside these ranges and needn't reach their ends.
Inputs may be any that keep to these rules, and one draw needn't show every extreme that they name: `decay_mask`: 1 marks a row that is perturbed.
All inputs are finite; a program needn't handle non-finite values.
Results may differ from the reference program's by a relative error of at most 0.024.
Values may be sent and summed in bfloat16 or wider, within the bound.
No kernel may reach another device: no remote copies, remote signals or barrier semaphores. Data moves between devices by JAX's collectives and lax.ppermute only.
A program may use at most 64 MiB of HBM per device.

```python
import math
import jax
import jax.numpy as jnp
from jax import lax

D = 4096
FF = 6144
TOK_DEV = 256
TOKENS = 4096
N_DP = 16
N_MP = 16


def draw_norm_gain(key, part):
    place = jnp.arange(D).astype(jnp.float32) / jnp.float32(max(D - 1, 1))
    base = jnp.exp(jnp.log(jnp.float32(3.0)) * place)
    noise = jnp.clip(1.0 + 0.1 * jax.random.normal(key, (D,), jnp.float32), 0.75, 1.25)
    return (base * noise).astype(jnp.float32)


def with_ends(array, stream_key, least, largest):
    index_at = [jax.random.randint(jax.random.fold_in(stream_key, axis), (), 0, length) for axis, length in enumerate(array.shape)]
    main_axis = array.shape.index(max(array.shape))
    beside = index_at[:main_axis] + [(index_at[main_axis] + 1) % array.shape[main_axis]] + index_at[main_axis + 1:]
    return array.at[tuple(index_at)].set(least).at[tuple(beside)].set(largest)


def levels(rng, dims, pieces, low, largest):
    level, own = 1.0, jax.random.fold_in(rng, 6)
    for axis_at, parts in pieces:
        heights = jnp.exp(jax.random.uniform(jax.random.fold_in(own, axis_at), (parts,), jnp.float32, low / len(pieces), largest / len(pieces)))
        level = level * jnp.repeat(heights, dims[axis_at] // parts).reshape([-1 if axis == axis_at else 1 for axis in range(len(dims))])
    return level


def centred(own_key, shape, width, limit, pieces=(), dtype=jnp.bfloat16):
    entries = width * jax.random.normal(own_key, shape, jnp.float32)
    if pieces:
        entries = entries * levels(own_key, shape, pieces, -0.22, 0.18)
    return jnp.clip(entries, -limit, limit).astype(dtype)


def setup_inputs(seed: int = 0) -> dict:
    key_of = jax.random.split(jax.random.key(seed), 8)
    return {
        "tokens": centred(key_of[0], (TOKENS, D), 1.0, 6.0, ((0, 16), (1, 16))),
        "norm_gain": draw_norm_gain(jax.random.fold_in(key_of[7], 71), 0),
        "w_gate": centred(key_of[2], (D, FF), D ** -0.5, 0.09375, ((0, 16), (1, 16))),
        "w_up": centred(key_of[3], (D, FF), D ** -0.5, 0.09375, ((0, 16), (1, 16))),
        "cotangent": centred(key_of[4], (TOKENS, FF), (TOKENS ** -0.5), 0.09375, ((0, 16), (1, 16))),
        "decay_mask": with_ends((jax.random.randint(key_of[5], (2, D), 0, 2) < 1).astype(jnp.int32), jax.random.fold_in(key_of[5], 1), 0, 1),
        "radius": jnp.clip(jnp.exp(jax.random.uniform(key_of[6], (1,), jnp.float32, math.log(12.8), math.log(38.4))), 12.8, 38.4),
    }


def activation(value):
    return jax.nn.gelu(value, approximate=True)

def pass_grads(scaled, gain_vec, mat_gate, mat_up, cotangent):
    block = FF // N_MP
    normed = (scaled * gain_vec[None, :]).astype(jnp.bfloat16)
    pre_gate = jnp.dot(normed, mat_gate, preferred_element_type=jnp.float32)
    pre_up = jnp.dot(normed, mat_up, preferred_element_type=jnp.float32)
    activated, back_fn = jax.vjp(activation, pre_gate)
    upstream = cotangent.astype(jnp.float32)
    d_up = (upstream * activated).astype(jnp.bfloat16)
    d_gate = back_fn(upstream * pre_up)[0].astype(jnp.bfloat16)

    def feature_step(index, total):
        first = (index * block).astype(jnp.int32)
        gate_cols = lax.dynamic_slice_in_dim(d_gate, first, block, 1)
        up_cols = lax.dynamic_slice_in_dim(d_up, first, block, 1)
        gate_mat = lax.dynamic_slice_in_dim(mat_gate, first, block, 1)
        up_mat = lax.dynamic_slice_in_dim(mat_up, first, block, 1)
        term = lax.dot_general(gate_cols, gate_mat, (((1,), (1,)), ((), ())), preferred_element_type=jnp.float32)
        term = term + lax.dot_general(up_cols, up_mat, (((1,), (1,)), ((), ())), preferred_element_type=jnp.float32)
        term = lax.optimization_barrier(term.astype(jnp.bfloat16)).astype(jnp.float32)
        return total + term
    d_norm = lax.fori_loop(0, N_MP, feature_step, jnp.zeros((TOKENS, D), jnp.float32))
    d_gain = lax.optimization_barrier(jnp.sum(d_norm * scaled, axis=0))
    stacked = jnp.concatenate([d_gate, d_up], axis=1)

    def token_step(index, total):
        first = (index * TOK_DEV).astype(jnp.int32)
        rows = lax.dynamic_slice_in_dim(normed, first, TOK_DEV, 0)
        grads = lax.dynamic_slice_in_dim(stacked, first, TOK_DEV, 0)
        term = lax.dot_general(rows, grads, (((0,), (0,)), ((), ())), preferred_element_type=jnp.float32)
        term = lax.optimization_barrier(term.astype(jnp.bfloat16)).astype(jnp.float32)
        return total + term
    both = lax.fori_loop(0, N_DP, token_step, jnp.zeros((D, 2 * FF), jnp.float32))
    return (d_gain, both[:, :FF], both[:, FF:])

def reference(tokens, norm_gain, w_gate, w_up, cotangent, decay_mask, radius):
    values = tokens.astype(jnp.float32)
    scaled = values * lax.rsqrt(lax.optimization_barrier(jnp.mean(values * values, axis=1, keepdims=True)) + 1e-06)
    asc_gain, asc_gate_f, asc_up_f = pass_grads(scaled, norm_gain, w_gate, w_up, cotangent)
    asc_gate = asc_gate_f.astype(jnp.bfloat16).astype(jnp.float32)
    asc_up = asc_up_f.astype(jnp.bfloat16).astype(jnp.float32)
    groups = decay_mask.astype(jnp.float32)
    gate_rows = groups[0][:, None]
    up_rows = groups[1][:, None]
    total = jnp.sum(gate_rows * asc_gate * asc_gate) + jnp.sum(up_rows * asc_up * asc_up)
    factor = radius[0] / (jnp.sqrt(total) + 1e-12)
    new_gate = (w_gate.astype(jnp.float32) + factor * gate_rows * asc_gate).astype(jnp.bfloat16)
    new_up = (w_up.astype(jnp.float32) + factor * up_rows * asc_up).astype(jnp.bfloat16)
    grad_gain, grad_gate, grad_up = pass_grads(scaled, norm_gain, new_gate, new_up, cotangent)
    return (grad_gain, grad_gate, grad_up)
```

```python
import functools
import jax
import jax.numpy as jnp
from jax import lax
from jax.experimental import pallas as pl
from jax.experimental.pallas import tpu as pltpu
from jax.sharding import PartitionSpec as P

NY, NZH, NX, NZL, NC = 4, 4, 4, 2, 2
AXES = ("dp", "mp")
BLK = 256
SUB = 96
ROWS = 2 * SUB
NB = 16
KC = 0.7978845608
KB = 0.044715
VMEM = pl.BlockSpec(memory_space=pltpu.VMEM)
SMEM = pl.BlockSpec(memory_space=pltpu.SMEM)
BF = jnp.bfloat16
F32 = jnp.float32
NT = (((1,), (1,)), ((), ()))

GROUPS = (
    ((0, 0),),
    ((0, 1), (1, 0), (3, 0)),
    ((1, 1), (3, 1), (2, 0), (2, 1)),
)


def linear(y, zh, x, zl, c):
    return ((y * NZH + zh) * NX + x) * NZL * NC + zl * NC + c


def recv(value, dy=0, dzh=0, dx=0, lz=0, lc=0):
    pairs = []
    for y in range(NY):
        for zh in range(NZH):
            for x in range(NX):
                for zl in range(NZL):
                    for c in range(NC):
                        src = linear((y + dy) % NY, (zh + dzh) % NZH, (x + dx) % NX, zl ^ lz, c ^ lc)
                        pairs.append((src, linear(y, zh, x, zl, c)))
    return lax.ppermute(value, AXES, pairs)


def sum_over(value, axes):
    for axis in axes:
        if axis == "c":
            value = value + recv(value, lc=1)
        elif axis == "zl":
            value = value + recv(value, lz=1)
        else:
            key = {"x": "dx", "y": "dy", "zh": "dzh"}[axis]
            value = value + recv(value, **{key: 1}) + recv(value, **{key: 3}) + recv(value, **{key: 2})
    return value


def call(kernel, out_shape, n_smem, n_vmem, flops, nbytes, scratch=(), out_specs=None):
    return pl.pallas_call(
        kernel,
        out_shape=out_shape,
        in_specs=[SMEM] * n_smem + [VMEM] * n_vmem,
        out_specs=jax.tree.map(lambda _: VMEM, out_shape),
        scratch_shapes=scratch,
        compiler_params=pltpu.CompilerParams(vmem_limit_bytes=48 * 1024 * 1024),
        cost_estimate=pl.CostEstimate(flops=flops, bytes_accessed=nbytes, transcendentals=0),
    )


def shape(dims, dtype):
    return jax.ShapeDtypeStruct(dims, dtype)


def token_blocks(toks, lam=None):
    at = 0
    for a in range(NX):
        for g in (0, 1):
            for group in GROUPS:
                ref = toks[at]
                at += 1
                for i, (k, l) in enumerate(group):
                    if lam is None or lam == l:
                        yield a, k, l, g, ref, i


def prep_kernel(ids, gain, mask, *refs):
    own, first, rest = refs[0:4], refs[4:7], refs[7:10]
    wabs, wp = refs[10], refs[11]
    y, zh = ids[0], ids[1]
    for j in range(NY):
        for k in range(NZH):
            if j == 0:
                blk = own[k][0:ROWS, :]
            elif k == 0:
                blk = first[j - 1][...]
            else:
                blk = rest[j - 1][k - 1]
            fb = lax.rem(y + j, NY) * NZH + lax.rem(zh + k, NZH)
            wabs[fb] = blk
            wp[fb] = (blk.astype(F32) * gain[pl.ds(fb, 1), :]).astype(BF)


def pre_kernel(lam, ids, wp, *refs):
    toks, out = refs[:-1], refs[-1]
    x, zl, c = ids[2], ids[3], ids[4]
    seen = set()
    for a, k, l, g, ref, i in token_blocks(toks, lam):
        fb = lax.rem(x + a, NX) * 4 + (zl ^ l) * 2 + (c ^ g)
        term = lax.dot_general(wp[fb], ref[i], NT, preferred_element_type=F32)
        if k in seen:
            out[k] += term
        else:
            seen.add(k)
            out[k] = term


def asc_kernel(lam, ids, gain, mask, *refs):
    parts, keep, scaled = refs[0:4], refs[4], refs[5]
    y, zl = ids[0], ids[3]
    for j in range(NY):
        for h in range(2):
            ya = lax.rem(y + j, NY)
            fb = ya * NZH + (zl ^ lam) * 2 + h
            at = ya * 2 + h
            m = mask[fb]
            blk = parts[j][h].astype(F32)
            gm = jnp.concatenate(
                [jnp.broadcast_to(m[0:1, :], (SUB, BLK)), jnp.broadcast_to(m[1:2, :], (SUB, BLK))], axis=0
            )
            blk = blk * gm
            keep[at] = blk.astype(BF)
            scaled[at] = (blk * gain[pl.ds(fb, 1), :]).astype(BF)


def pre2_kernel(lam, ids, ap, *refs):
    toks, out = refs[:-1], refs[-1]
    x, c = ids[2], ids[4]
    seen = set()
    for a, k, l, g, ref, i in token_blocks(toks, lam):
        at = lax.rem(x + a, NX) * 2 + (c ^ g)
        term = lax.dot_general(ap[at], ref[i], NT, preferred_element_type=F32)
        if k in seen:
            out[k] += term
        else:
            seen.add(k)
            out[k] = term


def hidden_grads(pre, r, cot):
    gate = pre[0:SUB] * r
    up = pre[SUB:ROWS] * r
    u = cot.astype(F32)
    inner = KC * (gate + KB * gate * gate * gate)
    t = jnp.tanh(inner)
    act = 0.5 * gate * (1.0 + t)
    slope = 0.5 * (1.0 + t) + 0.5 * gate * (1.0 - t * t) * KC * (1.0 + 3.0 * KB * gate * gate)
    return jnp.concatenate([u * up * slope * r, u * act * r], axis=0).astype(BF)


def grad1_kernel(praw0, praw1, r, *refs):
    cots, out = refs[0:4], refs[4]
    for k in range(NZH):
        out[k] = hidden_grads(praw0[k] + praw1[k], r[pl.ds(k, 1), :], cots[k][ROWS : ROWS + SUB, :])


def grad2_kernel(factor, praw0, praw1, preA0, preA1, r, *refs):
    cots, out = refs[0:4], refs[4]
    f = factor[0]
    for k in range(NZH):
        pre = praw0[k] + praw1[k] + f * (preA0[k] + preA1[k])
        out[k] = hidden_grads(pre, r[pl.ds(k, 1), :], cots[k][ROWS : ROWS + SUB, :])


def outer_terms(lam, ids, d, toks):
    x, zl, c = ids[2], ids[3], ids[4]
    sums = {}
    for a, k, l, g, ref, i in token_blocks(toks, lam):
        term = lax.dot_general(d[k], ref[i], (((1,), (0,)), ((), ())), preferred_element_type=F32)
        key = (a, g)
        if key in sums:
            n, total = sums[key]
            n, total = n + 1, total + term
        else:
            n, total = 1, term
        sums[key] = (n, total)
        if n == NZH:
            sums.pop(key)
            yield a, g, total


def order_blocks(toks, lam):
    blocks = list(token_blocks(toks, lam))
    blocks.sort(key=lambda b: (b[0], b[3]))
    return blocks


def outer1_kernel(lam, ids, d, *refs):
    toks, out = refs[:-1], refs[-1]
    y, x, c = ids[0], ids[2], ids[4]
    for a, g, total in outer_terms(lam, ids, d, toks):
        k = lax.rem(x + a - y + NY, NY)
        out[k, c ^ g] = total.astype(BF)


def outer2_kernel(lam, factor, ids, d, wabs, keep, *refs):
    toks, out, dgp = refs[:-2], refs[-2], refs[-1]
    y, x, zl, c = ids[0], ids[2], ids[3], ids[4]
    f = factor[0]
    dgp[...] = jnp.zeros_like(dgp)
    for a, g, total in outer_terms(lam, ids, d, toks):
        xa = lax.rem(x + a, NX)
        k = lax.rem(xa - y + NY, NY)
        out[k, c ^ g] = total.astype(BF)
        fb = xa * 4 + (zl ^ lam) * 2 + (c ^ g)
        w = wabs[fb].astype(F32) + f * keep[xa * 2 + (c ^ g)].astype(F32)
        dgp[pl.ds(fb, 1), :] = jnp.sum(w * total, axis=0, keepdims=True)


def final_kernel(ids, p0, p1, p2, p3, gate, up, tg, tu):
    zh = ids[1]
    for k, part in enumerate((p0, p1, p2, p3)):
        at = pl.multiple_of(lax.rem(zh + k, NZH) * SUB, SUB)
        blk = part[...].astype(F32)
        tg[pl.ds(at, SUB), :] = blk[0:SUB]
        tu[pl.ds(at, SUB), :] = blk[SUB:ROWS]
    gate[...] = tg[...].T
    up[...] = tu[...].T


def body(tokens, norm_gain, w_gate, w_up, cotangent, decay_mask, radius):
    width = NB * BLK
    dp, mp = lax.axis_index("dp"), lax.axis_index("mp")
    y, zh = dp // NZH, dp % NZH
    x, zl, c = mp // 4, (mp // 2) % 2, mp % 2
    ids = jnp.stack([y, zh, x, zl, c]).astype(jnp.int32)

    zparts = {(k, l): tokens if (k, l) == (0, 0) else recv(tokens, dzh=k, lz=l) for grp in GROUPS for k, l in grp}
    own = [jnp.stack([zparts[b] for b in grp]) for grp in GROUPS]
    toks = []
    for a in range(NX):
        mine = [v if a == 0 else recv(v, dx=a) for v in own]
        toks += mine + [recv(v, lc=1) for v in mine]

    both = jnp.stack([w_gate, w_up, cotangent])
    quarters = both.reshape(3, BLK, NZH, SUB).transpose(2, 0, 3, 1).reshape(NZH, 3 * SUB, BLK)

    def quarter(q):
        return lax.dynamic_index_in_dim(quarters, q, 0, keepdims=False)

    pieces = [quarter(zh)] + [recv(quarter((zh - k) % NZH), dzh=k) for k in range(1, NZH)]
    first = [recv(pieces[0][:ROWS], dy=j) for j in range(1, NY)]
    three = jnp.stack([p[:ROWS] for p in pieces[1:]])
    rest = [recv(three, dy=j) for j in range(1, NY)]

    values = tokens.astype(F32)
    square = jnp.sum(values * values, axis=1)[None, :]
    small = jnp.zeros((NB, BLK), F32)
    small = lax.dynamic_update_slice(small, norm_gain[None, :], (mp, 0))
    small = jnp.concatenate([small, jnp.broadcast_to(square, (8, BLK))], axis=0)
    small = sum_over(small, ("c", "zl", "x"))
    gain, square = small[:NB], small[NB:]
    squares = jnp.stack([square[0]] + [recv(square, dzh=k)[0] for k in range(1, NZH)])
    r = lax.rsqrt(squares / width + 1e-06)
    mask = decay_mask.astype(F32).reshape(2, NB, BLK).transpose(1, 0, 2)

    wshape = shape((NB, ROWS, BLK), BF)
    wabs, wp = call(prep_kernel, (wshape, wshape), 1, 12, 10**6, 4 * 10**6)(ids, gain, mask, *pieces, *first, *rest)
    pshape = shape((NZH, ROWS, BLK), F32)
    half = ROWS * width * 4 * BLK
    praw = [
        call(functools.partial(pre_kernel, l), pshape, 1, 25, half, 5 * 10**6)(ids, wp, *toks) for l in range(2)
    ]
    dshape = shape((NZH, ROWS, BLK), BF)
    d1 = call(grad1_kernel, dshape, 0, 7, 10**7, 2 * 10**6)(*praw, r, *pieces)

    oshape = shape((NY, 2, ROWS, BLK), BF)
    gains_here, masks_here, asc = [], [], []
    total = 0.0
    for l in range(2):
        base = y * NZH + (zl ^ l) * 2
        gh = lax.dynamic_slice(gain, (base, 0), (2, BLK))[:, None, :]
        mh = jnp.repeat(lax.dynamic_slice(mask, (base, 0, 0), (2, 2, BLK)), SUB, axis=1)
        gains_here.append(gh)
        out = call(functools.partial(outer1_kernel, l), oshape, 1, 25, half, 5 * 10**6)(ids, d1, *toks)
        s = out[0].astype(F32)
        for k in range(1, NY):
            s = s + recv(out[k], dy=NY - k).astype(F32)
        low = (s * gh).astype(BF)
        asc.append(low)
        wide = low.astype(F32)
        total = total + jnp.sum(mh * wide * wide)
    total = sum_over(jnp.full((8, 128), total, F32), ("c", "zl", "x", "y", "zh"))[0, 0]
    factor = (radius[0] / (jnp.sqrt(total) + 1e-12))[None]

    kept, prea = [], []
    for l in range(2):
        parts = [asc[l]] + [recv(asc[l], dy=j) for j in range(1, NY)]
        kshape = shape((8, ROWS, BLK), BF)
        keep, scaled = call(functools.partial(asc_kernel, l), (kshape, kshape), 1, 6, 10**6, 3 * 10**6)(
            ids, gain, mask, *parts
        )
        kept.append(keep)
        prea.append(call(functools.partial(pre2_kernel, l), pshape, 1, 25, half, 5 * 10**6)(ids, scaled, *toks))
    d2 = call(grad2_kernel, dshape, 1, 9, 10**7, 3 * 10**6)(factor, *praw, *prea, r, *pieces)
    sums, dgp = [], 0.0
    for l in range(2):
        out, part = call(
            functools.partial(outer2_kernel, l), (oshape, shape((NB, BLK), F32)), 2, 27, half, 7 * 10**6
        )(factor, ids, d2, wabs, kept[l], *toks)
        dgp = dgp + part
        s = out[0].astype(F32)
        for k in range(1, NY):
            s = s + recv(out[k], dy=NY - k).astype(F32)
        sums.append((s * gains_here[l]).astype(BF))
    stacked = jnp.concatenate(sums, axis=0)

    def for_zh(q):
        return lax.dynamic_index_in_dim(stacked, ((q // 2) ^ zl) * 2 + q % 2, 0, keepdims=False)

    finals = [for_zh(zh)] + [recv(for_zh((zh - k) % NZH), dzh=k) for k in range(1, NZH)]
    gshape = shape((BLK, 4 * SUB), F32)
    grad_gate, grad_up = call(
        final_kernel, (gshape, gshape), 1, 4, 10**6, 2 * 10**6, [pltpu.VMEM((4 * SUB, BLK), F32)] * 2
    )(ids, *finals)
    dg = sum_over(dgp, ("c", "zl", "x", "y", "zh"))
    grad_gain = lax.dynamic_index_in_dim(dg, mp, 0, keepdims=False)
    return grad_gain, grad_gate, grad_up


def solution(mesh):
    placed = (P("dp", "mp"), P("mp"), P("dp", "mp"), P("dp", "mp"), P("dp", "mp"), P(), P())
    return jax.shard_map(
        body,
        mesh=mesh,
        in_specs=placed,
        out_specs=(P("mp"), P("dp", "mp"), P("dp", "mp")),
        check_vma=False,
    )
```

```python
import functools
import jax
import jax.numpy as jnp
from jax import lax
from jax.experimental import pallas as pl
from jax.experimental.pallas import tpu as pltpu
from jax.sharding import Mesh, PartitionSpec as P

SIZES = (4, 4, 4, 2, 2)
NAMES = ("y", "zh", "x", "zl", "c")
DP, MP = ("y", "zh"), ("x", "zl", "c")
BLK = 256
SUB = 96
ROWS = 2 * SUB
NB = 16
PACK = BLK + 16
KC = 0.7978845608
KB = 0.044715
BF = jnp.bfloat16
F32 = jnp.float32
NT = (((1,), (1,)), ((), ()))
NN = (((1,), (0,)), ((), ()))

GROUPS = (
    ((0, 0),),
    ((0, 1), (1, 0), (3, 0)),
    ((1, 1), (3, 1), (2, 0), (2, 1)),
)
PLACE = {b: (g, i) for g, grp in enumerate(GROUPS) for i, b in enumerate(grp)}


def from_z(value, dzh, lz):
    pairs = []
    for zh in range(4):
        for zl in range(2):
            pairs.append((((zh + dzh) % 4) * 2 + (zl ^ lz), zh * 2 + zl))
    return lax.ppermute(value, ("zh", "zl"), pairs)


def other_core(value):
    return lax.ppermute(value, "c", [(0, 1), (1, 0)])


def shape(dims, dtype):
    return jax.ShapeDtypeStruct(dims, dtype)


def call(kernel, out_shape, in_specs, out_specs, grid=(), scratch=(), flops=10**6, nbytes=10**6):
    return pl.pallas_call(
        kernel,
        out_shape=out_shape,
        grid=grid,
        in_specs=in_specs,
        out_specs=out_specs,
        scratch_shapes=scratch,
        compiler_params=pltpu.CompilerParams(vmem_limit_bytes=32 * 1024 * 1024),
        cost_estimate=pl.CostEstimate(flops=flops, bytes_accessed=nbytes, transcendentals=0),
    )


SMEM = pl.BlockSpec(memory_space=pltpu.SMEM)


def whole(dims):
    return pl.BlockSpec(dims, lambda *_: (0,) * len(dims))


def by_x(dims):
    return pl.BlockSpec((1,) + dims, lambda i: (i,) + (0,) * len(dims))


def split3(value):
    hi = value.astype(BF)
    left = value - hi.astype(F32)
    mid = left.astype(BF)
    return [hi, mid, (left - mid.astype(F32)).astype(BF)]


def row(ref_rows, at):
    rows = ref_rows.astype(F32)
    return rows[at : at + 1] + rows[at + 1 : at + 2] + rows[at + 2 : at + 3]


def start_kernel(tokens, gain, w_gate, w_up, cot, pack, pieces):
    values = tokens[...].astype(F32)
    squares = jnp.sum((values * values).T, axis=0, keepdims=True)
    pack[0:BLK, :] = tokens[...]
    extra = split3(gain[...]) + split3(squares)
    tail = jnp.concatenate([e.astype(F32) for e in extra] + [jnp.zeros((10, BLK), F32)], axis=0)
    pack[BLK:PACK, :] = tail.astype(BF)
    for i, ref in enumerate((w_gate, w_up, cot)):
        turned = ref[...].astype(F32).T.astype(BF)
        for q in range(4):
            pieces[q, SUB * i : SUB * (i + 1), :] = turned[SUB * q : SUB * (q + 1), :]


def pre_kernel(parts, with_gain, ids, w, *refs):
    toks = refs[: len(parts)]
    out, sq = refs[len(parts)], refs[len(parts) + 1]
    gabs = refs[len(parts) + 2] if with_gain else None
    x, zh, zl, c = pl.program_id(0), ids[1], ids[3], ids[4]

    @pl.when(x == 0)
    def _():
        out[...] = jnp.zeros_like(out)
        sq[...] = jnp.zeros_like(sq)

    scaled, sums, squares = {}, {}, {}
    for (grp, g), ref in zip(parts, toks):
        for i, (k, l) in enumerate(GROUPS[grp]):
            tail = ref[0, i, BLK:PACK, :]
            if (l, g) not in scaled:
                gain = row(tail, 0)
                at = (zl ^ l) * 2 + (c ^ g)
                wv = w[0, at]
                scaled[l, g] = (wv.astype(F32) * gain).astype(BF)
                if gabs is not None:
                    gabs[x * 4 + at] = jnp.broadcast_to(gain, (8, BLK))
            term = lax.dot_general(scaled[l, g], ref[0, i, 0:BLK, :], NT, preferred_element_type=F32)
            sums[k] = sums[k] + term if k in sums else term
            s = row(tail, 3)
            squares[k] = squares[k] + s if k in squares else s
    for k, total in sums.items():
        out[k] += total
        sq[k] += jnp.broadcast_to(squares[k], (8, BLK))


def pre2_kernel(parts, ids, asc, mask, gabs, *refs):
    toks, out = refs[: len(parts)], refs[len(parts)]
    x, zl, c = pl.program_id(0), ids[3], ids[4]

    @pl.when(x == 0)
    def _():
        out[...] = jnp.zeros_like(out)

    scaled, sums = {}, {}
    for (grp, g), ref in zip(parts, toks):
        for i, (k, l) in enumerate(GROUPS[grp]):
            if (l, g) not in scaled:
                at = (zl ^ l) * 2 + (c ^ g)
                fb = x * 4 + at
                scaled[l, g] = (asc[0, at].astype(F32) * mask_rows(mask[fb]) * gabs[fb][0:1]).astype(BF)
            term = lax.dot_general(scaled[l, g], ref[0, i, 0:BLK, :], NT, preferred_element_type=F32)
            sums[k] = sums[k] + term if k in sums else term
    for k, total in sums.items():
        out[k] += total


def mask_rows(m):
    return jnp.concatenate(
        [jnp.broadcast_to(m[0:1, :], (SUB, BLK)), jnp.broadcast_to(m[1:2, :], (SUB, BLK))], axis=0
    )


def hidden_grads(pre, r, cot):
    gate = pre[0:SUB] * r
    up = pre[SUB:ROWS] * r
    u = cot.astype(F32)
    inner = KC * (gate + KB * gate * gate * gate)
    t = jnp.tanh(inner)
    act = 0.5 * gate * (1.0 + t)
    slope = 0.5 * (1.0 + t) + 0.5 * gate * (1.0 - t * t) * KC * (1.0 + 3.0 * KB * gate * gate)
    return jnp.concatenate([u * up * slope * r, u * act * r], axis=0).astype(BF)


def fill_grads(ids, d, pres, sqs, pieces):
    zh = ids[1]
    for k in range(4):
        pre, sq = pres(k), sqs[0][k][0:1]
        for s in sqs[1:]:
            sq = sq + s[k][0:1]
        r = lax.rsqrt(sq / (NB * BLK) + 1e-06)
        d[k] = hidden_grads(pre, r, pieces[lax.rem(zh + k, 4), ROWS : ROWS + SUB, :])


def outer_terms(parts, d, toks):
    where = {p: ref for p, ref in zip(parts, toks)}
    for l in range(2):
        for g in range(2):
            total = None
            for k in range(4):
                grp, i = PLACE[k, l]
                term = lax.dot_general(d[k], where[grp, g][0, i, 0:BLK, :], NN, preferred_element_type=F32)
                total = term if total is None else total + term
            yield l, g, total


def outer1_kernel(parts, ids, p0, p1, p2, s0, s1, s2, pieces, *refs):
    toks, out, d = refs[: len(parts)], refs[len(parts)], refs[len(parts) + 1]
    zl, c = ids[3], ids[4]

    @pl.when(pl.program_id(0) == 0)
    def _():
        fill_grads(ids, d, lambda k: p0[k] + p1[k] + p2[k], (s0, s1, s2), pieces)

    for l, g, total in outer_terms(parts, d, toks):
        out[0, (zl ^ l) * 2 + (c ^ g)] = total.astype(BF)


def outer2_kernel(parts, factor, ids, p0, p1, p2, s0, s1, s2, pieces, pa, w, asc, mask, *refs):
    toks, out, dgp, d = refs[: len(parts)], refs[len(parts)], refs[len(parts) + 1], refs[len(parts) + 2]
    x, zh, zl, c = pl.program_id(0), ids[1], ids[3], ids[4]
    f = factor[0]

    @pl.when(x == 0)
    def _():
        fill_grads(ids, d, lambda k: p0[k] + p1[k] + p2[k] + f * pa[k], (s0, s1, s2), pieces)

    for l, g, total in outer_terms(parts, d, toks):
        at = (zl ^ l) * 2 + (c ^ g)
        out[0, at] = total.astype(BF)
        fb = x * 4 + at
        wv = w[0, at].astype(F32)
        wv = wv + f * mask_rows(mask[fb]) * asc[0, at].astype(F32)
        dgp[pl.ds(fb, 1), :] = jnp.sum(wv * total, axis=0, keepdims=True)


def ascent_kernel(ids, terms, gabs, mask, asc, part):
    y = ids[0]
    acc = jnp.zeros((8, BLK), F32)
    for h in range(4):
        total = terms[0, h].astype(F32)
        for j in range(1, 4):
            total = total + terms[j, h].astype(F32)
        low = (total * gabs[y * 4 + h][0:1]).astype(BF)
        asc[h] = low
        wide = low.astype(F32)
        acc = acc + jnp.sum((mask_rows(mask[y * 4 + h]) * wide * wide).reshape(ROWS // 8, 8, BLK), axis=0)
    part[...] = acc[:, 0:128] + acc[:, 128:256]


def final_kernel(ids, gabs, sums, gate, up):
    g = gabs[ids[0] * 4 + ids[1]][0:1]
    tg = jnp.concatenate([sums[q, 0:SUB, :].astype(F32) for q in range(4)], axis=0) * g
    tu = jnp.concatenate([sums[q, SUB:ROWS, :].astype(F32) for q in range(4)], axis=0) * g
    gate[...] = tg.T
    up[...] = tu.T


def spread(value, axes):
    n = 16
    return lax.all_to_all(jnp.broadcast_to(value[None], (n,) + value.shape), axes, 0, 0, tiled=True)


def body(tokens, norm_gain, w_gate, w_up, cotangent, decay_mask, radius):
    ids = jnp.stack([lax.axis_index(n) for n in NAMES]).astype(jnp.int32)
    mask = decay_mask.astype(F32).reshape(2, NB, BLK).transpose(1, 0, 2)

    pack, pieces = call(
        start_kernel,
        (shape((PACK, BLK), BF), shape((4, 3 * SUB, BLK), BF)),
        [whole((BLK, BLK)), whole((1, BLK))] + [whole((BLK, 4 * SUB))] * 3,
        (whole((PACK, BLK)), whole((4, 3 * SUB, BLK))),
    )(tokens, norm_gain[None, :], w_gate, w_up, cotangent)

    own = []
    for grp in GROUPS:
        blocks = [pack if b == (0, 0) else from_z(pack, *b) for b in grp]
        own.append(jnp.stack(blocks))
    mine = [lax.all_gather(v, "x", axis=0, tiled=False) for v in own]
    theirs = [other_core(v) for v in mine]
    toks = {(grp, g): (mine, theirs)[g][grp] for grp in range(3) for g in range(2)}

    pieces = lax.all_to_all(pieces, "zh", 0, 0, tiled=True)
    weights = lax.all_to_all(jnp.broadcast_to(pieces[None, :, :ROWS], (4, 4, ROWS, BLK)), "y", 0, 0, tiled=True)

    pshape, sshape, gshape = shape((4, ROWS, BLK), F32), shape((4, 8, BLK), F32), shape((NB, 8, BLK), F32)
    wspec = by_x((4, ROWS, BLK))

    def tok_spec(grp):
        return by_x((len(GROUPS[grp]), PACK, BLK))

    def pre(parts, with_gain):
        outs = [pshape, sshape] + ([gshape] if with_gain else [])
        blocks = sum(len(GROUPS[p[0]]) for p in parts)
        return call(
            functools.partial(pre_kernel, parts, with_gain),
            outs,
            [SMEM, wspec] + [tok_spec(p[0]) for p in parts],
            [whole(s.shape) for s in outs],
            (4,),
            flops=blocks * 4 * 2 * ROWS * BLK * BLK,
            nbytes=blocks * 4 * 2 * PACK * BLK,
        )(ids, weights, *[toks[p] for p in parts])

    p0, s0, gabs = pre(((0, 0), (1, 0), (0, 1), (1, 1)), True)
    p1, s1 = pre(((2, 0),), False)
    p2, s2 = pre(((2, 1),), False)
    parts = ((0, 0), (1, 0), (2, 0), (0, 1), (1, 1), (2, 1))
    tok_specs = [tok_spec(p[0]) for p in parts]
    tok_refs = [toks[p] for p in parts]
    cost = {"flops": 64 * 2 * ROWS * BLK * BLK, "nbytes": 12 * 10**6}
    oshape = shape((4, 4, ROWS, BLK), BF)
    dscratch = [pltpu.VMEM((4, ROWS, BLK), BF)]
    first_specs = [whole(pshape.shape)] * 3 + [whole(sshape.shape)] * 3 + [whole(pieces.shape)]
    out1 = call(
        functools.partial(outer1_kernel, parts),
        oshape,
        [SMEM] + first_specs + tok_specs,
        by_x((4, ROWS, BLK)),
        (4,),
        dscratch,
        **cost,
    )(ids, p0, p1, p2, s0, s1, s2, pieces, *tok_refs)
    terms = lax.all_to_all(out1, "y", 0, 0, tiled=True)
    asc, part = call(
        ascent_kernel,
        (shape((4, ROWS, BLK), BF), shape((8, 128), F32)),
        [SMEM, whole(oshape.shape), whole(gshape.shape), whole((NB, 2, BLK))],
        (whole((4, ROWS, BLK)), whole((8, 128))),
    )(ids, terms, gabs, mask)
    ascs = lax.all_gather(asc, "y", axis=0, tiled=False)
    part = jnp.sum(spread(part, MP), axis=0)
    total = jnp.sum(spread(part, DP))
    factor = (radius[0] / (jnp.sqrt(total) + 1e-12))[None]
    pa = call(
        functools.partial(pre2_kernel, parts),
        pshape,
        [SMEM, wspec, whole((NB, 2, BLK)), whole(gshape.shape)] + tok_specs,
        whole(pshape.shape),
        (4,),
        **cost,
    )(ids, ascs, mask, gabs, *tok_refs)
    out2, dgp = call(
        functools.partial(outer2_kernel, parts),
        (oshape, shape((NB, BLK), F32)),
        [SMEM, SMEM] + first_specs + [whole(pshape.shape), wspec, wspec, whole((NB, 2, BLK))] + tok_specs,
        (by_x((4, ROWS, BLK)), whole((NB, BLK))),
        (4,),
        dscratch,
        **cost,
    )(factor, ids, p0, p1, p2, s0, s1, s2, pieces, pa, weights, ascs, mask, *tok_refs)
    sums = lax.psum_scatter(out2, "y", scatter_dimension=0, tiled=False)
    dg = jnp.sum(lax.all_to_all(dgp, MP, 0, 0, tiled=True), axis=0)
    grad_gain = jnp.sum(spread(dg, DP).reshape(16, BLK), axis=0)
    sums = lax.all_to_all(sums, "zh", 0, 0, tiled=True)
    out = shape((BLK, 4 * SUB), F32)
    grad_gate, grad_up = call(
        final_kernel,
        (out, out),
        [SMEM, whole(gshape.shape), whole((4, ROWS, BLK))],
        (whole((BLK, 4 * SUB)), whole((BLK, 4 * SUB))),
    )(ids, gabs, sums)
    return grad_gain, grad_gate, grad_up


def solution(mesh):
    fine = Mesh(mesh.devices.reshape(SIZES), NAMES)
    both = P(DP, MP)
    return jax.shard_map(
        body,
        mesh=fine,
        in_specs=(both, P(MP), both, both, both, P(), P()),
        out_specs=(P(MP), both, both),
        check_vma=False,
    )
```

```python
import functools
import jax
import jax.numpy as jnp
from jax import lax
from jax.experimental import pallas as pl
from jax.experimental.pallas import tpu as pltpu
from jax.sharding import Mesh, PartitionSpec as P

SIZES = (4, 4, 4, 2, 2)
NAMES = ("y", "zh", "x", "zl", "c")
DP, MP = ("y", "zh"), ("x", "zl", "c")
BLK = 256
SUB = 96
ROWS = 2 * SUB
NB = 16
PACK = BLK + 16
KC = 0.7978845608
KB = 0.044715
BF = jnp.bfloat16
F32 = jnp.float32
NT = (((1,), (1,)), ((), ()))
NN = (((1,), (0,)), ((), ()))

GROUPS = (
    ((0, 0),),
    ((0, 1),),
    ((1, 0), (3, 0), (2, 0)),
    ((1, 1), (3, 1), (2, 1)),
)
PLACE = {b: (g, i) for g, grp in enumerate(GROUPS) for i, b in enumerate(grp)}


def from_z(value, dzh, lz):
    pairs = []
    for zh in range(4):
        for zl in range(2):
            pairs.append((((zh + dzh) % 4) * 2 + (zl ^ lz), zh * 2 + zl))
    return lax.ppermute(value, ("zh", "zl"), pairs)


def other_core(value):
    return lax.ppermute(value, "c", [(0, 1), (1, 0)])


def shape(dims, dtype):
    return jax.ShapeDtypeStruct(dims, dtype)


def call(kernel, out_shape, in_specs, out_specs, grid=(), scratch=(), flops=10**6, nbytes=10**6):
    return pl.pallas_call(
        kernel,
        out_shape=out_shape,
        grid=grid,
        in_specs=in_specs,
        out_specs=out_specs,
        scratch_shapes=scratch,
        compiler_params=pltpu.CompilerParams(vmem_limit_bytes=32 * 1024 * 1024),
        cost_estimate=pl.CostEstimate(flops=flops, bytes_accessed=nbytes, transcendentals=0),
    )


def hbm(dims, dtype):
    return pltpu.HBM(dims, dtype)


def in_hbm(value):
    return pltpu.with_memory_space_constraint(value, pltpu.HBM)


SMEM = pl.BlockSpec(memory_space=pltpu.SMEM)


def whole(dims):
    return pl.BlockSpec(dims, lambda *_: (0,) * len(dims))


def by_x(dims):
    return pl.BlockSpec((1,) + dims, lambda i: (i,) + (0,) * len(dims))


def split3(value):
    hi = value.astype(BF)
    left = value - hi.astype(F32)
    mid = left.astype(BF)
    return [hi, mid, (left - mid.astype(F32)).astype(BF)]


def row(ref_rows, at):
    rows = ref_rows.astype(F32)
    return rows[at : at + 1] + rows[at + 1 : at + 2] + rows[at + 2 : at + 3]


def start_kernel(tokens, gain, w_gate, w_up, cot, pack, pieces):
    values = tokens[...].astype(F32)
    squares = jnp.sum((values * values).T, axis=0, keepdims=True)
    pack[0:BLK, :] = tokens[...]
    extra = split3(gain[...]) + split3(squares)
    tail = jnp.concatenate([e.astype(F32) for e in extra] + [jnp.zeros((10, BLK), F32)], axis=0)
    pack[BLK:PACK, :] = tail.astype(BF)
    for i, ref in enumerate((w_gate, w_up, cot)):
        turned = ref[...].astype(F32).T.astype(BF)
        for q in range(4):
            pieces[q, SUB * i : SUB * (i + 1), :] = turned[SUB * q : SUB * (q + 1), :]


def pre_kernel(parts, with_gain, ids, w, *refs):
    toks = refs[: len(parts)]
    out, sq = refs[len(parts)], refs[len(parts) + 1]
    gabs = refs[len(parts) + 2] if with_gain else None
    x, zh, zl, c = pl.program_id(0), ids[1], ids[3], ids[4]

    @pl.when(x == 0)
    def _():
        out[...] = jnp.zeros_like(out)
        sq[...] = jnp.zeros_like(sq)

    scaled, sums, squares = {}, {}, {}
    for (grp, g), ref in zip(parts, toks):
        for i, (k, l) in enumerate(GROUPS[grp]):
            tail = ref[0, i, BLK:PACK, :]
            if (l, g) not in scaled:
                gain = row(tail, 0)
                at = (zl ^ l) * 2 + (c ^ g)
                wv = w[0, at]
                scaled[l, g] = (wv.astype(F32) * gain).astype(BF)
                if gabs is not None:
                    gabs[x * 4 + at] = jnp.broadcast_to(gain, (8, BLK))
            term = lax.dot_general(scaled[l, g], ref[0, i, 0:BLK, :], NT, preferred_element_type=F32)
            sums[k] = sums[k] + term if k in sums else term
            s = row(tail, 3)
            squares[k] = squares[k] + s if k in squares else s
    for k, total in sums.items():
        out[k] += total
        sq[k] += jnp.broadcast_to(squares[k], (8, BLK))


def pre2_kernel(parts, ids, asc, mask, gabs, *refs):
    toks, out = refs[: len(parts)], refs[len(parts)]
    x, zl, c = pl.program_id(0), ids[3], ids[4]

    @pl.when(x == 0)
    def _():
        out[...] = jnp.zeros_like(out)

    scaled, sums = {}, {}
    for (grp, g), ref in zip(parts, toks):
        for i, (k, l) in enumerate(GROUPS[grp]):
            if (l, g) not in scaled:
                at = (zl ^ l) * 2 + (c ^ g)
                fb = x * 4 + at
                scaled[l, g] = (asc[0, at].astype(F32) * mask_rows(mask[fb]) * gabs[fb][0:1]).astype(BF)
            term = lax.dot_general(scaled[l, g], ref[0, i, 0:BLK, :], NT, preferred_element_type=F32)
            sums[k] = sums[k] + term if k in sums else term
    for k, total in sums.items():
        out[k] += total


def mask_rows(m):
    return jnp.concatenate(
        [jnp.broadcast_to(m[0:1, :], (SUB, BLK)), jnp.broadcast_to(m[1:2, :], (SUB, BLK))], axis=0
    )


def hidden_grads(pre, r, cot):
    gate = pre[0:SUB] * r
    up = pre[SUB:ROWS] * r
    u = cot.astype(F32)
    inner = KC * (gate + KB * gate * gate * gate)
    t = jnp.tanh(inner)
    act = 0.5 * gate * (1.0 + t)
    slope = 0.5 * (1.0 + t) + 0.5 * gate * (1.0 - t * t) * KC * (1.0 + 3.0 * KB * gate * gate)
    return jnp.concatenate([u * up * slope * r, u * act * r], axis=0).astype(BF)


def fill_grads(ids, d, pres, sqs, pieces):
    zh = ids[1]
    for k in range(4):
        pre, sq = pres(k), sqs[0][k][0:1]
        for s in sqs[1:]:
            sq = sq + s[k][0:1]
        r = lax.rsqrt(sq / (NB * BLK) + 1e-06)
        d[k] = hidden_grads(pre, r, pieces[lax.rem(zh + k, 4), ROWS : ROWS + SUB, :])


def outer_terms(parts, d, toks):
    where = {p: ref for p, ref in zip(parts, toks)}
    for l in range(2):
        for g in range(2):
            total = None
            for k in range(4):
                grp, i = PLACE[k, l]
                term = lax.dot_general(d[k], where[grp, g][0, i, 0:BLK, :], NN, preferred_element_type=F32)
                total = term if total is None else total + term
            yield l, g, total


def outer1_kernel(parts, ids, p0, p1, p2, s0, s1, s2, pieces, *refs):
    toks, out, d = refs[: len(parts)], refs[len(parts)], refs[len(parts) + 1]
    zl, c = ids[3], ids[4]

    @pl.when(pl.program_id(0) == 0)
    def _():
        fill_grads(ids, d, lambda k: p0[k] + p1[k] + p2[k], (s0, s1, s2), pieces)

    for l, g, total in outer_terms(parts, d, toks):
        out[0, (zl ^ l) * 2 + (c ^ g)] = total.astype(BF)


def outer2_kernel(parts, factor, ids, p0, p1, p2, s0, s1, s2, pieces, pa, w, asc, mask, *refs):
    toks, out, dgp, d = refs[: len(parts)], refs[len(parts)], refs[len(parts) + 1], refs[len(parts) + 2]
    x, zh, zl, c = pl.program_id(0), ids[1], ids[3], ids[4]
    f = factor[0]

    @pl.when(x == 0)
    def _():
        fill_grads(ids, d, lambda k: p0[k] + p1[k] + p2[k] + f * pa[k], (s0, s1, s2), pieces)

    for l, g, total in outer_terms(parts, d, toks):
        at = (zl ^ l) * 2 + (c ^ g)
        out[0, at] = total.astype(BF)
        fb = x * 4 + at
        wv = w[0, at].astype(F32)
        wv = wv + f * mask_rows(mask[fb]) * asc[0, at].astype(F32)
        dgp[pl.ds(fb, 1), :] = jnp.sum(wv * total, axis=0, keepdims=True)


def ascent_kernel(ids, terms, gabs, mask, asc, part):
    y = ids[0]
    acc = jnp.zeros((8, BLK), F32)
    for h in range(4):
        total = terms[0, h].astype(F32)
        for j in range(1, 4):
            total = total + terms[j, h].astype(F32)
        low = (total * gabs[y * 4 + h][0:1]).astype(BF)
        asc[h] = low
        wide = low.astype(F32)
        acc = acc + jnp.sum((mask_rows(mask[y * 4 + h]) * wide * wide).reshape(ROWS // 8, 8, BLK), axis=0)
    part[...] = acc[:, 0:128] + acc[:, 128:256]


def final_kernel(ids, gabs, sums, gate, up):
    g = gabs[ids[0] * 4 + ids[1]][0:1]
    tg = jnp.concatenate([sums[q, 0:SUB, :].astype(F32) for q in range(4)], axis=0) * g
    tu = jnp.concatenate([sums[q, SUB:ROWS, :].astype(F32) for q in range(4)], axis=0) * g
    gate[...] = tg.T
    up[...] = tu.T


def spread(value, axes):
    n = 16
    return lax.all_to_all(jnp.broadcast_to(value[None], (n,) + value.shape), axes, 0, 0, tiled=True)


def body(tokens, norm_gain, w_gate, w_up, cotangent, decay_mask, radius):
    ids = jnp.stack([lax.axis_index(n) for n in NAMES]).astype(jnp.int32)
    mask = decay_mask.astype(F32).reshape(2, NB, BLK).transpose(1, 0, 2)

    pack, pieces = call(
        start_kernel,
        (hbm((PACK, BLK), BF), hbm((4, 3 * SUB, BLK), BF)),
        [whole((BLK, BLK)), whole((1, BLK))] + [whole((BLK, 4 * SUB))] * 3,
        (whole((PACK, BLK)), whole((4, 3 * SUB, BLK))),
    )(in_hbm(tokens), norm_gain[None, :], in_hbm(w_gate), in_hbm(w_up), in_hbm(cotangent))

    def after(value, *others):
        return lax.optimization_barrier((value,) + others)[0]

    def over_x(value):
        return lax.all_to_all(jnp.broadcast_to(value[None], (4,) + value.shape), "x", 0, 0, tiled=True)

    mid = jnp.stack([from_z(pack, k, 0) for k, _ in GROUPS[2]])
    mid_x = lax.all_gather(mid, "x", axis=0, tiled=False)
    near = from_z(pack, 0, 1)
    own_x = over_x(pack[None])
    far_x = lax.all_gather(from_z(mid, 0, 1), "x", axis=0, tiled=False)
    near_x = over_x(near[None])
    pieces = lax.all_to_all(after(pieces, mid), "zh", 0, 0, tiled=True)
    weights = lax.all_to_all(jnp.broadcast_to(pieces[None, :, :ROWS], (4, 4, ROWS, BLK)), "y", 0, 0, tiled=True)
    weights = in_hbm(weights)
    mine = [own_x, near_x, mid_x, far_x]
    theirs = [other_core(v) for v in mine]
    toks = {(grp, g): in_hbm((mine, theirs)[g][grp]) for grp in range(len(GROUPS)) for g in range(2)}

    pshape, sshape, gshape = shape((4, ROWS, BLK), F32), shape((4, 8, BLK), F32), shape((NB, 8, BLK), F32)
    wspec = by_x((4, ROWS, BLK))

    def tok_spec(grp):
        return by_x((len(GROUPS[grp]), PACK, BLK))

    def pre(parts, with_gain):
        outs = [pshape, sshape] + ([gshape] if with_gain else [])
        blocks = sum(len(GROUPS[p[0]]) for p in parts)
        return call(
            functools.partial(pre_kernel, parts, with_gain),
            outs,
            [SMEM, wspec] + [tok_spec(p[0]) for p in parts],
            [whole(s.shape) for s in outs],
            (4,),
            flops=blocks * 4 * 2 * ROWS * BLK * BLK,
            nbytes=blocks * 4 * 2 * PACK * BLK,
        )(ids, weights, *[toks[p] for p in parts])

    p0, s0, gabs = pre(tuple((grp, g) for g in range(2) for grp in (0, 1, 2)), True)
    p1, s1 = pre(((3, 0),), False)
    p2, s2 = pre(((3, 1),), False)
    parts = tuple((grp, g) for g in range(2) for grp in range(len(GROUPS)))
    tok_specs = [tok_spec(p[0]) for p in parts]
    tok_refs = [toks[p] for p in parts]
    cost = {"flops": 64 * 2 * ROWS * BLK * BLK, "nbytes": 12 * 10**6}
    oshape = hbm((4, 4, ROWS, BLK), BF)
    dscratch = [pltpu.VMEM((4, ROWS, BLK), BF)]
    first_specs = [whole(pshape.shape)] * 3 + [whole(sshape.shape)] * 3 + [whole(pieces.shape)]
    out1 = call(
        functools.partial(outer1_kernel, parts),
        oshape,
        [SMEM] + first_specs + tok_specs,
        by_x((4, ROWS, BLK)),
        (4,),
        dscratch,
        **cost,
    )(ids, p0, p1, p2, s0, s1, s2, pieces, *tok_refs)
    terms = lax.all_to_all(out1, "y", 0, 0, tiled=True)
    asc, part = call(
        ascent_kernel,
        (hbm((4, ROWS, BLK), BF), shape((8, 128), F32)),
        [SMEM, whole(oshape.shape), whole(gshape.shape), whole((NB, 2, BLK))],
        (whole((4, ROWS, BLK)), whole((8, 128))),
    )(ids, terms, gabs, mask)
    ascs = in_hbm(lax.all_gather(asc, "y", axis=0, tiled=False))
    part = jnp.sum(spread(part, MP), axis=0)
    total = jnp.sum(spread(part, DP))
    factor = (radius[0] / (jnp.sqrt(total) + 1e-12))[None]
    pa = call(
        functools.partial(pre2_kernel, parts),
        pshape,
        [SMEM, wspec, whole((NB, 2, BLK)), whole(gshape.shape)] + tok_specs,
        whole(pshape.shape),
        (4,),
        **cost,
    )(ids, ascs, mask, gabs, *tok_refs)
    out2, dgp = call(
        functools.partial(outer2_kernel, parts),
        (oshape, shape((NB, BLK), F32)),
        [SMEM, SMEM] + first_specs + [whole(pshape.shape), wspec, wspec, whole((NB, 2, BLK))] + tok_specs,
        (by_x((4, ROWS, BLK)), whole((NB, BLK))),
        (4,),
        dscratch,
        **cost,
    )(factor, ids, p0, p1, p2, s0, s1, s2, pieces, pa, weights, ascs, mask, *tok_refs)
    sums = lax.psum_scatter(out2, "y", scatter_dimension=0, tiled=False)
    dg = jnp.sum(lax.all_to_all(dgp, MP, 0, 0, tiled=True), axis=0)
    grad_gain = jnp.sum(spread(dg, DP).reshape(16, BLK), axis=0)
    sums = lax.all_to_all(sums, "zh", 0, 0, tiled=True)
    out = hbm((BLK, 4 * SUB), F32)
    grad_gate, grad_up = call(
        final_kernel,
        (out, out),
        [SMEM, whole(gshape.shape), whole((4, ROWS, BLK))],
        (whole((BLK, 4 * SUB)), whole((BLK, 4 * SUB))),
    )(ids, gabs, sums)
    return grad_gain, grad_gate, grad_up


def solution(mesh):
    fine = Mesh(mesh.devices.reshape(SIZES), NAMES)
    both = P(DP, MP)
    return jax.shard_map(
        body,
        mesh=fine,
        in_specs=(both, P(MP), both, both, both, P(), P()),
        out_specs=(P(MP), both, both),
        check_vma=False,
    )
```

```python
import functools
import jax
import jax.numpy as jnp
from jax import lax
from jax.experimental import pallas as pl
from jax.experimental.pallas import tpu as pltpu
from jax.sharding import Mesh, PartitionSpec as P

SIZES = (4, 4, 4, 2, 2)
NAMES = ("y", "zh", "x", "zl", "c")
DP, MP = ("y", "zh"), ("x", "zl", "c")
BLK = 256
SUB = 96
ROWS = 2 * SUB
NB = 16
PACK = BLK + 16
KC = 0.7978845608
KB = 0.044715
BF = jnp.bfloat16
F32 = jnp.float32
NT = (((1,), (1,)), ((), ()))
NN = (((1,), (0,)), ((), ()))

GROUPS = (
    ((0, 0),),
    ((0, 1),),
    ((1, 0), (3, 0), (2, 0)),
    ((1, 1), (3, 1), (2, 1)),
)
PLACE = {b: (g, i) for g, grp in enumerate(GROUPS) for i, b in enumerate(grp)}


def from_z(value, dzh, lz):
    pairs = []
    for zh in range(4):
        for zl in range(2):
            pairs.append((((zh + dzh) % 4) * 2 + (zl ^ lz), zh * 2 + zl))
    return lax.ppermute(value, ("zh", "zl"), pairs)


def other_core(value):
    return lax.ppermute(value, "c", [(0, 1), (1, 0)])


def shape(dims, dtype):
    return jax.ShapeDtypeStruct(dims, dtype)


def call(kernel, out_shape, in_specs, out_specs, grid=(), scratch=(), flops=10**6, nbytes=10**6):
    return pl.pallas_call(
        kernel,
        out_shape=out_shape,
        grid=grid,
        in_specs=in_specs,
        out_specs=out_specs,
        scratch_shapes=scratch,
        compiler_params=pltpu.CompilerParams(vmem_limit_bytes=32 * 1024 * 1024),
        cost_estimate=pl.CostEstimate(flops=flops, bytes_accessed=nbytes, transcendentals=0),
    )


def hbm(dims, dtype):
    return pltpu.HBM(dims, dtype)


def in_hbm(value):
    return pltpu.with_memory_space_constraint(value, pltpu.HBM)


SMEM = pl.BlockSpec(memory_space=pltpu.SMEM)


def whole(dims):
    return pl.BlockSpec(dims, lambda *_: (0,) * len(dims))


def by_x(dims):
    return pl.BlockSpec((1,) + dims, lambda i: (i,) + (0,) * len(dims))


def split3(value):
    hi = value.astype(BF)
    left = value - hi.astype(F32)
    mid = left.astype(BF)
    return [hi, mid, (left - mid.astype(F32)).astype(BF)]


def row(ref_rows, at):
    rows = ref_rows.astype(F32)
    return rows[at : at + 1] + rows[at + 1 : at + 2] + rows[at + 2 : at + 3]


def start_kernel(ids, tokens, gain, w_gate, w_up, cot, pack, p0, p1, p2, p3, turned):
    values = tokens[...].astype(F32)
    squares = jnp.sum((values * values).T, axis=0, keepdims=True)
    pack[0:BLK, :] = tokens[...]
    extra = split3(gain[...]) + split3(squares)
    tail = jnp.concatenate([e.astype(F32) for e in extra] + [jnp.zeros((10, BLK), F32)], axis=0)
    pack[BLK:PACK, :] = tail.astype(BF)
    for i, ref in enumerate((w_gate, w_up, cot)):
        turned[i] = ref[...].astype(F32).T.astype(BF)
        for k, to in enumerate((p0, p1, p2, p3)):
            q = pl.multiple_of(lax.rem(ids[1] - k + 4, 4) * SUB, SUB)
            to[SUB * i : SUB * (i + 1), :] = turned[i, pl.ds(q, SUB), :]


def pre_kernel(parts, with_gain, ids, w, *refs):
    toks = refs[: len(parts)]
    out, sq = refs[len(parts)], refs[len(parts) + 1]
    gabs = refs[len(parts) + 2] if with_gain else None
    x, zh, zl, c = pl.program_id(0), ids[1], ids[3], ids[4]

    @pl.when(x == 0)
    def _():
        out[...] = jnp.zeros_like(out)
        sq[...] = jnp.zeros_like(sq)

    scaled, sums, squares = {}, {}, {}
    for (grp, g), ref in zip(parts, toks):
        for i, (k, l) in enumerate(GROUPS[grp]):
            tail = ref[0, i, BLK:PACK, :]
            if (l, g) not in scaled:
                gain = row(tail, 0)
                at = (zl ^ l) * 2 + (c ^ g)
                wv = w[0, lax.rem(at - zh + 4, 4)]
                scaled[l, g] = (wv.astype(F32) * gain).astype(BF)
                if gabs is not None:
                    gabs[x * 4 + at] = jnp.broadcast_to(gain, (8, BLK))
            term = lax.dot_general(scaled[l, g], ref[0, i, 0:BLK, :], NT, preferred_element_type=F32)
            sums[k] = sums[k] + term if k in sums else term
            s = row(tail, 3)
            squares[k] = squares[k] + s if k in squares else s
    for k, total in sums.items():
        out[k] += total
        sq[k] += jnp.broadcast_to(squares[k], (8, BLK))


def pre2_kernel(parts, ids, asc, mask, gabs, *refs):
    toks, out = refs[: len(parts)], refs[len(parts)]
    x, zl, c = pl.program_id(0), ids[3], ids[4]

    @pl.when(x == 0)
    def _():
        out[...] = jnp.zeros_like(out)

    scaled, sums = {}, {}
    for (grp, g), ref in zip(parts, toks):
        for i, (k, l) in enumerate(GROUPS[grp]):
            if (l, g) not in scaled:
                at = (zl ^ l) * 2 + (c ^ g)
                fb = x * 4 + at
                scaled[l, g] = (asc[0, at].astype(F32) * mask_rows(mask[fb]) * gabs[fb][0:1]).astype(BF)
            term = lax.dot_general(scaled[l, g], ref[0, i, 0:BLK, :], NT, preferred_element_type=F32)
            sums[k] = sums[k] + term if k in sums else term
    for k, total in sums.items():
        out[k] += total


def mask_rows(m):
    return jnp.concatenate(
        [jnp.broadcast_to(m[0:1, :], (SUB, BLK)), jnp.broadcast_to(m[1:2, :], (SUB, BLK))], axis=0
    )


def hidden_grads(pre, r, cot):
    gate = pre[0:SUB] * r
    up = pre[SUB:ROWS] * r
    u = cot.astype(F32)
    inner = KC * (gate + KB * gate * gate * gate)
    t = jnp.tanh(inner)
    act = 0.5 * gate * (1.0 + t)
    slope = 0.5 * (1.0 + t) + 0.5 * gate * (1.0 - t * t) * KC * (1.0 + 3.0 * KB * gate * gate)
    return jnp.concatenate([u * up * slope * r, u * act * r], axis=0).astype(BF)


def fill_grads(ids, d, pres, sqs, pieces):
    for k in range(4):
        pre, sq = pres(k), sqs[0][k][0:1]
        for s in sqs[1:]:
            sq = sq + s[k][0:1]
        r = lax.rsqrt(sq / (NB * BLK) + 1e-06)
        d[k] = hidden_grads(pre, r, pieces[k][ROWS : ROWS + SUB, :])


def outer_terms(parts, d, toks):
    where = {p: ref for p, ref in zip(parts, toks)}
    for l in range(2):
        for g in range(2):
            total = None
            for k in range(4):
                grp, i = PLACE[k, l]
                term = lax.dot_general(d[k], where[grp, g][0, i, 0:BLK, :], NN, preferred_element_type=F32)
                total = term if total is None else total + term
            yield l, g, total


def outer1_kernel(parts, ids, p0, p1, p2, s0, s1, s2, c0, c1, c2, c3, *refs):
    toks, out, d = refs[: len(parts)], refs[len(parts)], refs[len(parts) + 1]
    zl, c = ids[3], ids[4]

    @pl.when(pl.program_id(0) == 0)
    def _():
        fill_grads(ids, d, lambda k: p0[k] + p1[k] + p2[k], (s0, s1, s2), (c0, c1, c2, c3))

    for l, g, total in outer_terms(parts, d, toks):
        out[0, (zl ^ l) * 2 + (c ^ g)] = total.astype(BF)


def outer2_kernel(parts, factor, ids, p0, p1, p2, s0, s1, s2, c0, c1, c2, c3, pa, w, asc, mask, *refs):
    toks, out, dgp, d = refs[: len(parts)], refs[len(parts)], refs[len(parts) + 1], refs[len(parts) + 2]
    x, zh, zl, c = pl.program_id(0), ids[1], ids[3], ids[4]
    f = factor[0]

    @pl.when(x == 0)
    def _():
        fill_grads(ids, d, lambda k: p0[k] + p1[k] + p2[k] + f * pa[k], (s0, s1, s2), (c0, c1, c2, c3))

    for l, g, total in outer_terms(parts, d, toks):
        at = (zl ^ l) * 2 + (c ^ g)
        out[0, at] = total.astype(BF)
        fb = x * 4 + at
        wv = w[0, lax.rem(at - zh + 4, 4)].astype(F32)
        wv = wv + f * mask_rows(mask[fb]) * asc[0, at].astype(F32)
        dgp[pl.ds(fb, 1), :] = jnp.sum(wv * total, axis=0, keepdims=True)


def ascent_kernel(ids, terms, gabs, mask, asc, part):
    y = ids[0]
    acc = jnp.zeros((8, BLK), F32)
    for h in range(4):
        total = terms[0, h].astype(F32)
        for j in range(1, 4):
            total = total + terms[j, h].astype(F32)
        low = (total * gabs[y * 4 + h][0:1]).astype(BF)
        asc[h] = low
        wide = low.astype(F32)
        acc = acc + jnp.sum((mask_rows(mask[y * 4 + h]) * wide * wide).reshape(ROWS // 8, 8, BLK), axis=0)
    part[...] = acc[:, 0:128] + acc[:, 128:256]


def final_kernel(ids, gabs, sums, gate, up):
    g = gabs[ids[0] * 4 + ids[1]][0:1]
    tg = jnp.concatenate([sums[q, 0:SUB, :].astype(F32) for q in range(4)], axis=0) * g
    tu = jnp.concatenate([sums[q, SUB:ROWS, :].astype(F32) for q in range(4)], axis=0) * g
    gate[...] = tg.T
    up[...] = tu.T


def spread(value, axes):
    n = 16
    return lax.all_to_all(jnp.broadcast_to(value[None], (n,) + value.shape), axes, 0, 0, tiled=True)


def body(tokens, norm_gain, w_gate, w_up, cotangent, decay_mask, radius):
    ids = jnp.stack([lax.axis_index(n) for n in NAMES]).astype(jnp.int32)
    mask = decay_mask.astype(F32).reshape(2, NB, BLK).transpose(1, 0, 2)

    piece = hbm((3 * SUB, BLK), BF)
    pack, *pieces = call(
        start_kernel,
        (hbm((PACK, BLK), BF),) + (piece,) * 4,
        [SMEM, whole((BLK, BLK)), whole((1, BLK))] + [whole((BLK, 4 * SUB))] * 3,
        (whole((PACK, BLK)),) + (whole(piece.shape),) * 4,
        scratch=[pltpu.VMEM((3, 4 * SUB, BLK), BF)],
    )(ids, in_hbm(tokens), norm_gain[None, :], in_hbm(w_gate), in_hbm(w_up), in_hbm(cotangent))

    def after(value, *others):
        return lax.optimization_barrier((value,) + others)[0]

    def over_x(value):
        return lax.all_to_all(jnp.broadcast_to(value[None], (4,) + value.shape), "x", 0, 0, tiled=True)

    mids = [from_z(pack, k, 0) for k, _ in GROUPS[2]]
    near = from_z(pack, 0, 1)
    own_x = over_x(pack[None])
    pieces = [pieces[0]] + [from_z(pieces[k], k, 0) for k in range(1, 4)]
    part_w = jnp.stack([p[:ROWS] for p in pieces])
    weights = in_hbm(lax.all_gather(part_w, "y", axis=0, tiled=False))
    mid_x = over_x(after(jnp.stack(mids + [near]), own_x))
    far = from_z(jnp.stack(mids), 0, 1)
    far_x = over_x(after(far, part_w, mid_x))
    toks = {}
    for g in range(2):
        o, m, f = [in_hbm(other_core(v) if g else v) for v in (own_x, mid_x, far_x)]
        toks.update({(0, g): o, (1, g): m, (2, g): m, (3, g): f})

    pshape, sshape, gshape = shape((4, ROWS, BLK), F32), shape((4, 8, BLK), F32), shape((NB, 8, BLK), F32)
    wspec = by_x((4, ROWS, BLK))

    def tok_spec(grp):
        at = 3 if grp == 1 else 0
        return pl.BlockSpec((1, len(GROUPS[grp]), PACK, BLK), lambda i: (i, at, 0, 0))

    def pre(parts, with_gain):
        outs = [pshape, sshape] + ([gshape] if with_gain else [])
        blocks = sum(len(GROUPS[p[0]]) for p in parts)
        return call(
            functools.partial(pre_kernel, parts, with_gain),
            outs,
            [SMEM, wspec] + [tok_spec(p[0]) for p in parts],
            [whole(s.shape) for s in outs],
            (4,),
            flops=blocks * 4 * 2 * ROWS * BLK * BLK,
            nbytes=blocks * 4 * 2 * PACK * BLK,
        )(ids, weights, *[toks[p] for p in parts])

    p0, s0, gabs = pre(tuple((grp, g) for g in range(2) for grp in (0, 1, 2)), True)
    p1, s1 = pre(((3, 0),), False)
    p2, s2 = pre(((3, 1),), False)
    parts = tuple((grp, g) for g in range(2) for grp in range(len(GROUPS)))
    tok_specs = [tok_spec(p[0]) for p in parts]
    tok_refs = [toks[p] for p in parts]
    cost = {"flops": 64 * 2 * ROWS * BLK * BLK, "nbytes": 12 * 10**6}
    oshape = hbm((4, 4, ROWS, BLK), BF)
    dscratch = [pltpu.VMEM((4, ROWS, BLK), BF)]
    first_specs = [whole(pshape.shape)] * 3 + [whole(sshape.shape)] * 3 + [whole(piece.shape)] * 4
    out1 = call(
        functools.partial(outer1_kernel, parts),
        oshape,
        [SMEM] + first_specs + tok_specs,
        by_x((4, ROWS, BLK)),
        (4,),
        dscratch,
        **cost,
    )(ids, p0, p1, p2, s0, s1, s2, *pieces, *tok_refs)
    terms = lax.all_to_all(out1, "y", 0, 0, tiled=True)
    asc, part = call(
        ascent_kernel,
        (hbm((4, ROWS, BLK), BF), shape((8, 128), F32)),
        [SMEM, whole(oshape.shape), whole(gshape.shape), whole((NB, 2, BLK))],
        (whole((4, ROWS, BLK)), whole((8, 128))),
    )(ids, terms, gabs, mask)
    ascs = in_hbm(lax.all_gather(asc, "y", axis=0, tiled=False))
    part = jnp.sum(spread(part, MP), axis=0)
    total = jnp.sum(spread(part, DP))
    factor = (radius[0] / (jnp.sqrt(total) + 1e-12))[None]
    pa = call(
        functools.partial(pre2_kernel, parts),
        pshape,
        [SMEM, wspec, whole((NB, 2, BLK)), whole(gshape.shape)] + tok_specs,
        whole(pshape.shape),
        (4,),
        **cost,
    )(ids, ascs, mask, gabs, *tok_refs)
    out2, dgp = call(
        functools.partial(outer2_kernel, parts),
        (oshape, shape((NB, BLK), F32)),
        [SMEM, SMEM] + first_specs + [whole(pshape.shape), wspec, wspec, whole((NB, 2, BLK))] + tok_specs,
        (by_x((4, ROWS, BLK)), whole((NB, BLK))),
        (4,),
        dscratch,
        **cost,
    )(factor, ids, p0, p1, p2, s0, s1, s2, *pieces, pa, weights, ascs, mask, *tok_refs)
    sums = lax.psum_scatter(out2, "y", scatter_dimension=0, tiled=False)
    dg = jnp.sum(lax.all_to_all(dgp, MP, 0, 0, tiled=True), axis=0)
    grad_gain = jnp.sum(spread(dg, DP).reshape(16, BLK), axis=0)
    sums = lax.all_to_all(sums, "zh", 0, 0, tiled=True)
    out = hbm((BLK, 4 * SUB), F32)
    grad_gate, grad_up = call(
        final_kernel,
        (out, out),
        [SMEM, whole(gshape.shape), whole((4, ROWS, BLK))],
        (whole((BLK, 4 * SUB)), whole((BLK, 4 * SUB))),
    )(ids, gabs, sums)
    return grad_gain, grad_gate, grad_up


def solution(mesh):
    fine = Mesh(mesh.devices.reshape(SIZES), NAMES)
    both = P(DP, MP)
    return jax.shard_map(
        body,
        mesh=fine,
        in_specs=(both, P(MP), both, both, both, P(), P()),
        out_specs=(P(MP), both, both),
        check_vma=False,
    )
```

```python
import functools
import jax
import jax.numpy as jnp
from jax import lax
from jax.experimental import pallas as pl
from jax.experimental.pallas import tpu as pltpu
from jax.sharding import Mesh, PartitionSpec as P

SIZES = (4, 4, 4, 2, 2)
NAMES = ("y", "zh", "x", "zl", "c")
DP, MP = ("y", "zh"), ("x", "zl", "c")
BLK = 256
SUB = 96
ROWS = 2 * SUB
NB = 16
PACK = BLK + 16
KC = 0.7978845608
KB = 0.044715
BF = jnp.bfloat16
F32 = jnp.float32
NT = (((1,), (1,)), ((), ()))
NN = (((1,), (0,)), ((), ()))

GROUPS = (
    ((0, 0),),
    ((1, 0), (3, 0), (2, 0), (0, 1)),
    ((1, 1), (3, 1), (2, 1)),
)
PLACE = {b: (g, i) for g, grp in enumerate(GROUPS) for i, b in enumerate(grp)}


def from_z(value, dzh, lz):
    pairs = []
    for zh in range(4):
        for zl in range(2):
            pairs.append((((zh + dzh) % 4) * 2 + (zl ^ lz), zh * 2 + zl))
    return lax.ppermute(value, ("zh", "zl"), pairs)


def other_core(value):
    return lax.ppermute(value, "c", [(0, 1), (1, 0)])


def shape(dims, dtype):
    return jax.ShapeDtypeStruct(dims, dtype)


def call(kernel, out_shape, in_specs, out_specs, grid=(), scratch=(), flops=10**6, nbytes=10**6):
    return pl.pallas_call(
        kernel,
        out_shape=out_shape,
        grid=grid,
        in_specs=in_specs,
        out_specs=out_specs,
        scratch_shapes=scratch,
        compiler_params=pltpu.CompilerParams(vmem_limit_bytes=16 * 1024 * 1024),
        cost_estimate=pl.CostEstimate(flops=flops, bytes_accessed=nbytes, transcendentals=0),
    )


def hbm(dims, dtype):
    return pltpu.HBM(dims, dtype)


def in_hbm(value):
    return pltpu.with_memory_space_constraint(value, pltpu.HBM)


def in_vmem(value):
    return pltpu.with_memory_space_constraint(value, pltpu.VMEM)


SMEM = pl.BlockSpec(memory_space=pltpu.SMEM)


def whole(dims):
    return pl.BlockSpec(dims, lambda *_: (0,) * len(dims))


def by_x(dims):
    return pl.BlockSpec((1,) + dims, lambda i: (i,) + (0,) * len(dims))


def split3(value):
    hi = value.astype(BF)
    left = value - hi.astype(F32)
    mid = left.astype(BF)
    return [hi, mid, (left - mid.astype(F32)).astype(BF)]


def row(ref_rows, at):
    rows = ref_rows.astype(F32)
    return rows[at : at + 1] + rows[at + 1 : at + 2] + rows[at + 2 : at + 3]


def start_kernel(ids, tokens, gain, w_gate, w_up, cot, pack, p0, p1, p2, p3, turned):
    values = tokens[...].astype(F32)
    squares = jnp.sum((values * values).T, axis=0, keepdims=True)
    pack[0:BLK, :] = tokens[...]
    extra = split3(gain[...]) + split3(squares)
    tail = jnp.concatenate([e.astype(F32) for e in extra] + [jnp.zeros((10, BLK), F32)], axis=0)
    pack[BLK:PACK, :] = tail.astype(BF)
    for i, ref in enumerate((w_gate, w_up, cot)):
        turned[i] = ref[...].astype(F32).T.astype(BF)
        for k, to in enumerate((p0, p1, p2, p3)):
            q = pl.multiple_of(lax.rem(ids[1] - k + 4, 4) * SUB, SUB)
            to[SUB * i : SUB * (i + 1), :] = turned[i, pl.ds(q, SUB), :]


def pre_kernel(parts, with_gain, ids, w, *refs):
    toks = refs[: len(parts)]
    out, sq = refs[len(parts)], refs[len(parts) + 1]
    gabs = refs[len(parts) + 2] if with_gain else None
    x, zh, zl, c = pl.program_id(0), ids[1], ids[3], ids[4]

    @pl.when(x == 0)
    def _():
        out[...] = jnp.zeros_like(out)
        sq[...] = jnp.zeros_like(sq)

    scaled, sums, squares = {}, {}, {}
    for (grp, g), ref in zip(parts, toks):
        for i, (k, l) in enumerate(GROUPS[grp]):
            tail = ref[x, i, BLK:PACK, :]
            if (l, g) not in scaled:
                gain = row(tail, 0)
                at = (zl ^ l) * 2 + (c ^ g)
                wv = w[0, lax.rem(at - zh + 4, 4)]
                scaled[l, g] = (wv.astype(F32) * gain).astype(BF)
                if gabs is not None:
                    gabs[x * 4 + at] = jnp.broadcast_to(gain, (8, BLK))
            sums.setdefault(k, []).append((scaled[l, g], ref[x, i, 0:BLK, :]))
            s = row(tail, 3)
            squares[k] = squares[k] + s if k in squares else s
    for k, pairs in sums.items():
        out[k] += joined(pairs, 1, NT)
        sq[k] += jnp.broadcast_to(squares[k], (8, BLK))


def joined(pairs, axis, dims):
    left = jnp.concatenate([p[0] for p in pairs], axis=1)
    right = jnp.concatenate([p[1] for p in pairs], axis=axis)
    return lax.dot_general(left, right, dims, preferred_element_type=F32)


def pre2_kernel(parts, ids, asc, mask, gabs, *refs):
    toks, out = refs[: len(parts)], refs[len(parts)]
    x, zl, c = pl.program_id(0), ids[3], ids[4]

    @pl.when(x == 0)
    def _():
        out[...] = jnp.zeros_like(out)

    scaled, sums = {}, {}
    for (grp, g), ref in zip(parts, toks):
        for i, (k, l) in enumerate(GROUPS[grp]):
            if (l, g) not in scaled:
                at = (zl ^ l) * 2 + (c ^ g)
                fb = x * 4 + at
                scaled[l, g] = (asc[0, at].astype(F32) * mask_rows(mask[fb]) * gabs[fb][0:1]).astype(BF)
            sums.setdefault(k, []).append((scaled[l, g], ref[x, i, 0:BLK, :]))
    for k, pairs in sums.items():
        out[k] += joined(pairs, 1, NT)


def mask_rows(m):
    return jnp.concatenate(
        [jnp.broadcast_to(m[0:1, :], (SUB, BLK)), jnp.broadcast_to(m[1:2, :], (SUB, BLK))], axis=0
    )


def hidden_grads(pre, r, cot):
    gate = pre[0:SUB] * r
    up = pre[SUB:ROWS] * r
    u = cot.astype(F32)
    inner = KC * (gate + KB * gate * gate * gate)
    t = jnp.tanh(inner)
    act = 0.5 * gate * (1.0 + t)
    slope = 0.5 * (1.0 + t) + 0.5 * gate * (1.0 - t * t) * KC * (1.0 + 3.0 * KB * gate * gate)
    return jnp.concatenate([u * up * slope * r, u * act * r], axis=0).astype(BF)


def fill_grads(ids, d, pres, sqs, pieces):
    for k in range(4):
        pre, sq = pres(k), sqs[0][k][0:1]
        for s in sqs[1:]:
            sq = sq + s[k][0:1]
        r = lax.rsqrt(sq / (NB * BLK) + 1e-06)
        d[k] = hidden_grads(pre, r, pieces[k][ROWS : ROWS + SUB, :])


def outer_terms(parts, d, toks):
    where = {p: ref for p, ref in zip(parts, toks)}
    x = pl.program_id(0)
    for l in range(2):
        for g in range(2):
            places = [PLACE[k, l] for k in range(4)]
            pairs = [(d[k], where[grp, g][x, i, 0:BLK, :]) for k, (grp, i) in enumerate(places)]
            yield l, g, joined(pairs, 0, NN)


def outer1_kernel(parts, ids, p0, p1, p2, s0, s1, s2, c0, c1, c2, c3, *refs):
    toks, out, d = refs[: len(parts)], refs[len(parts)], refs[len(parts) + 1]
    zl, c = ids[3], ids[4]

    @pl.when(pl.program_id(0) == 0)
    def _():
        fill_grads(ids, d, lambda k: p0[k] + p1[k] + p2[k], (s0, s1, s2), (c0, c1, c2, c3))

    for l, g, total in outer_terms(parts, d, toks):
        out[0, (zl ^ l) * 2 + (c ^ g)] = total.astype(BF)


def outer2_kernel(parts, factor, ids, p0, p1, p2, s0, s1, s2, c0, c1, c2, c3, pa, w, asc, mask, *refs):
    toks, out, dgp, d = refs[: len(parts)], refs[len(parts)], refs[len(parts) + 1], refs[len(parts) + 2]
    x, zh, zl, c = pl.program_id(0), ids[1], ids[3], ids[4]
    f = factor[0]

    @pl.when(x == 0)
    def _():
        fill_grads(ids, d, lambda k: p0[k] + p1[k] + p2[k] + f * pa[k], (s0, s1, s2), (c0, c1, c2, c3))

    for l, g, total in outer_terms(parts, d, toks):
        at = (zl ^ l) * 2 + (c ^ g)
        out[0, at] = total.astype(BF)
        fb = x * 4 + at
        wv = w[0, lax.rem(at - zh + 4, 4)].astype(F32)
        wv = wv + f * mask_rows(mask[fb]) * asc[0, at].astype(F32)
        dgp[pl.ds(fb, 1), :] = jnp.sum(wv * total, axis=0, keepdims=True)


def ascent_kernel(ids, terms, gabs, mask, asc, part):
    y = ids[0]
    acc = jnp.zeros((8, BLK), F32)
    for h in range(4):
        total = terms[0, h].astype(F32)
        for j in range(1, 4):
            total = total + terms[j, h].astype(F32)
        low = (total * gabs[y * 4 + h][0:1]).astype(BF)
        asc[h] = low
        wide = low.astype(F32)
        acc = acc + jnp.sum((mask_rows(mask[y * 4 + h]) * wide * wide).reshape(ROWS // 8, 8, BLK), axis=0)
    part[...] = acc[:, 0:128] + acc[:, 128:256]


def final_kernel(ids, gabs, sums, gate, up):
    g = gabs[ids[0] * 4 + ids[1]][0:1]
    tg = jnp.concatenate([sums[q, 0:SUB, :].astype(F32) for q in range(4)], axis=0) * g
    tu = jnp.concatenate([sums[q, SUB:ROWS, :].astype(F32) for q in range(4)], axis=0) * g
    gate[...] = tg.T
    up[...] = tu.T


def spread(value, axes):
    n = 16
    return lax.all_to_all(jnp.broadcast_to(value[None], (n,) + value.shape), axes, 0, 0, tiled=True)


def body(tokens, norm_gain, w_gate, w_up, cotangent, decay_mask, radius):
    ids = jnp.stack([lax.axis_index(n) for n in NAMES]).astype(jnp.int32)
    mask = decay_mask.astype(F32).reshape(2, NB, BLK).transpose(1, 0, 2)

    piece = hbm((3 * SUB, BLK), BF)
    pack, *pieces = call(
        start_kernel,
        (hbm((PACK, BLK), BF),) + (piece,) * 4,
        [SMEM, whole((BLK, BLK)), whole((1, BLK))] + [whole((BLK, 4 * SUB))] * 3,
        (whole((PACK, BLK)),) + (whole(piece.shape),) * 4,
        scratch=[pltpu.VMEM((3, 4 * SUB, BLK), BF)],
    )(ids, in_hbm(tokens), norm_gain[None, :], in_hbm(w_gate), in_hbm(w_up), in_hbm(cotangent))

    def after(value, *others):
        return lax.optimization_barrier((value,) + others)[0]

    def over_x(value):
        return lax.all_to_all(jnp.broadcast_to(value[None], (4,) + value.shape), "x", 0, 0, tiled=True)

    mids = [from_z(pack, k, 0) for k in (1, 3, 2)]
    near = from_z(pack, 0, 1)
    own_x = over_x(pack[None])
    pieces = [pieces[0]] + [from_z(pieces[k], k, 0) for k in range(1, 4)]
    part_w = jnp.stack([p[:ROWS] for p in pieces])
    weights = in_hbm(lax.all_gather(part_w, "y", axis=0, tiled=False))
    mid_x = over_x(after(jnp.stack(mids + [near]), own_x))
    far = from_z(jnp.stack(mids), 0, 1)
    far_x = over_x(after(far, part_w, mid_x))
    mine = [in_vmem(v) for v in (own_x, mid_x)]
    toks = {(grp, g): in_vmem(other_core(v)) if g else v for grp, v in enumerate(mine) for g in range(2)}

    pshape, sshape, gshape = shape((4, ROWS, BLK), F32), shape((4, 8, BLK), F32), shape((NB, 8, BLK), F32)
    wspec = by_x((4, ROWS, BLK))

    def tok_spec(grp):
        return pl.BlockSpec(memory_space=pltpu.VMEM)

    def pre(parts, with_gain):
        outs = [pshape, sshape] + ([gshape] if with_gain else [])
        blocks = sum(len(GROUPS[p[0]]) for p in parts)
        return call(
            functools.partial(pre_kernel, parts, with_gain),
            outs,
            [SMEM, wspec] + [tok_spec(p[0]) for p in parts],
            [whole(s.shape) for s in outs],
            (4,),
            flops=blocks * 4 * 2 * ROWS * BLK * BLK,
            nbytes=blocks * 4 * 2 * PACK * BLK,
        )(ids, weights, *[toks[p] for p in parts])

    p0, s0, gabs = pre(tuple((grp, g) for g in range(2) for grp in (0, 1)), True)
    far_x = after(in_vmem(far_x), p0)
    toks[2, 0], toks[2, 1] = far_x, in_vmem(other_core(far_x))
    p1, s1 = pre(((2, 0),), False)
    p2, s2 = pre(((2, 1),), False)
    parts = tuple((grp, g) for g in range(2) for grp in range(len(GROUPS)))
    tok_specs = [tok_spec(p[0]) for p in parts]
    tok_refs = [toks[p] for p in parts]
    cost = {"flops": 64 * 2 * ROWS * BLK * BLK, "nbytes": 12 * 10**6}
    oshape = hbm((4, 4, ROWS, BLK), BF)
    dscratch = [pltpu.VMEM((4, ROWS, BLK), BF)]
    first_specs = [whole(pshape.shape)] * 3 + [whole(sshape.shape)] * 3 + [whole(piece.shape)] * 4
    out1 = call(
        functools.partial(outer1_kernel, parts),
        oshape,
        [SMEM] + first_specs + tok_specs,
        by_x((4, ROWS, BLK)),
        (4,),
        dscratch,
        **cost,
    )(ids, p0, p1, p2, s0, s1, s2, *pieces, *tok_refs)
    terms = lax.all_to_all(out1, "y", 0, 0, tiled=True)
    asc, part = call(
        ascent_kernel,
        (hbm((4, ROWS, BLK), BF), shape((8, 128), F32)),
        [SMEM, whole(oshape.shape), whole(gshape.shape), whole((NB, 2, BLK))],
        (whole((4, ROWS, BLK)), whole((8, 128))),
    )(ids, terms, gabs, mask)
    ascs = in_hbm(lax.all_gather(asc, "y", axis=0, tiled=False))
    part = jnp.sum(spread(part, MP), axis=0)
    total = jnp.sum(spread(part, DP))
    factor = (radius[0] / (jnp.sqrt(total) + 1e-12))[None]
    pa = call(
        functools.partial(pre2_kernel, parts),
        pshape,
        [SMEM, wspec, whole((NB, 2, BLK)), whole(gshape.shape)] + tok_specs,
        whole(pshape.shape),
        (4,),
        **cost,
    )(ids, ascs, mask, gabs, *tok_refs)
    out2, dgp = call(
        functools.partial(outer2_kernel, parts),
        (oshape, shape((NB, BLK), F32)),
        [SMEM, SMEM] + first_specs + [whole(pshape.shape), wspec, wspec, whole((NB, 2, BLK))] + tok_specs,
        (by_x((4, ROWS, BLK)), whole((NB, BLK))),
        (4,),
        dscratch,
        **cost,
    )(factor, ids, p0, p1, p2, s0, s1, s2, *pieces, pa, weights, ascs, mask, *tok_refs)
    sums = lax.psum_scatter(out2, "y", scatter_dimension=0, tiled=False)
    dg = jnp.sum(lax.all_to_all(dgp, MP, 0, 0, tiled=True), axis=0)
    grad_gain = jnp.sum(spread(dg, DP).reshape(16, BLK), axis=0)
    sums = lax.all_to_all(sums, "zh", 0, 0, tiled=True)
    out = hbm((BLK, 4 * SUB), F32)
    grad_gate, grad_up = call(
        final_kernel,
        (out, out),
        [SMEM, whole(gshape.shape), whole((4, ROWS, BLK))],
        (whole((BLK, 4 * SUB)), whole((BLK, 4 * SUB))),
    )(ids, gabs, sums)
    return grad_gain, grad_gate, grad_up


def solution(mesh):
    fine = Mesh(mesh.devices.reshape(SIZES), NAMES)
    both = P(DP, MP)
    return jax.shard_map(
        body,
        mesh=fine,
        in_specs=(both, P(MP), both, both, both, P(), P()),
        out_specs=(P(MP), both, both),
        check_vma=False,
    )
```

```python
import functools
import jax
import jax.numpy as jnp
from jax import lax
from jax.experimental import pallas as pl
from jax.experimental.pallas import tpu as pltpu
from jax.sharding import Mesh, PartitionSpec as P

SIZES = (4, 4, 4, 2, 2)
NAMES = ("y", "zh", "x", "zl", "c")
DP, MP = ("y", "zh"), ("x", "zl", "c")
BLK = 256
SUB = 96
ROWS = 2 * SUB
NB = 16
PACK = BLK + 16
KC = 0.7978845608
KB = 0.044715
BF = jnp.bfloat16
F32 = jnp.float32
NT = (((1,), (1,)), ((), ()))
NN = (((1,), (0,)), ((), ()))

GROUPS = (
    ((0, 0),),
    ((1, 0), (3, 0), (2, 0), (0, 1)),
    ((1, 1), (3, 1), (2, 1)),
)
PLACE = {b: (g, i) for g, grp in enumerate(GROUPS) for i, b in enumerate(grp)}


def from_z(value, dzh, lz):
    pairs = []
    for zh in range(4):
        for zl in range(2):
            pairs.append((((zh + dzh) % 4) * 2 + (zl ^ lz), zh * 2 + zl))
    return lax.ppermute(value, ("zh", "zl"), pairs)


def other_core(value):
    return lax.ppermute(value, "c", [(0, 1), (1, 0)])


def shape(dims, dtype):
    return jax.ShapeDtypeStruct(dims, dtype)


def call(kernel, out_shape, in_specs, out_specs, grid=(), scratch=(), flops=10**6, nbytes=10**6):
    return pl.pallas_call(
        kernel,
        out_shape=out_shape,
        grid=grid,
        in_specs=in_specs,
        out_specs=out_specs,
        scratch_shapes=scratch,
        compiler_params=pltpu.CompilerParams(vmem_limit_bytes=16 * 1024 * 1024),
        cost_estimate=pl.CostEstimate(flops=flops, bytes_accessed=nbytes, transcendentals=0),
    )


def hbm(dims, dtype):
    return pltpu.HBM(dims, dtype)


def in_hbm(value):
    return pltpu.with_memory_space_constraint(value, pltpu.HBM)


SMEM = pl.BlockSpec(memory_space=pltpu.SMEM)


def whole(dims):
    return pl.BlockSpec(dims, lambda *_: (0,) * len(dims))


def by_x(dims):
    return pl.BlockSpec((1,) + dims, lambda i: (i,) + (0,) * len(dims))


def split3(value):
    hi = value.astype(BF)
    left = value - hi.astype(F32)
    mid = left.astype(BF)
    return [hi, mid, (left - mid.astype(F32)).astype(BF)]


def row(ref_rows, at):
    rows = ref_rows.astype(F32)
    return rows[at : at + 1] + rows[at + 1 : at + 2] + rows[at + 2 : at + 3]


def start_kernel(ids, tokens, gain, w_gate, w_up, cot, pack, p0, p1, p2, p3, turned):
    values = tokens[...].astype(F32)
    squares = jnp.sum((values * values).T, axis=0, keepdims=True)
    pack[0:BLK, :] = tokens[...]
    extra = split3(gain[...]) + split3(squares)
    tail = jnp.concatenate([e.astype(F32) for e in extra] + [jnp.zeros((10, BLK), F32)], axis=0)
    pack[BLK:PACK, :] = tail.astype(BF)
    for i, ref in enumerate((w_gate, w_up, cot)):
        turned[i] = ref[...].astype(F32).T.astype(BF)
        for k, to in enumerate((p0, p1, p2, p3)):
            q = pl.multiple_of(lax.rem(ids[1] - k + 4, 4) * SUB, SUB)
            to[SUB * i : SUB * (i + 1), :] = turned[i, pl.ds(q, SUB), :]


def pre_kernel(parts, with_gain, ids, w, *refs):
    toks = refs[: len(parts)]
    out, sq = refs[len(parts)], refs[len(parts) + 1]
    gabs = refs[len(parts) + 2] if with_gain else None
    x, zh, zl, c = pl.program_id(0), ids[1], ids[3], ids[4]

    @pl.when(x == 0)
    def _():
        out[...] = jnp.zeros_like(out)
        sq[...] = jnp.zeros_like(sq)

    scaled, sums, squares = {}, {}, {}
    for (grp, g), ref in zip(parts, toks):
        for i, (k, l) in enumerate(GROUPS[grp]):
            tail = ref[0, i, BLK:PACK, :]
            if (l, g) not in scaled:
                gain = row(tail, 0)
                at = (zl ^ l) * 2 + (c ^ g)
                wv = w[0, lax.rem(at - zh + 4, 4)]
                scaled[l, g] = (wv.astype(F32) * gain).astype(BF)
                if gabs is not None:
                    gabs[x * 4 + at] = jnp.broadcast_to(gain, (8, BLK))
            sums.setdefault(k, []).append((scaled[l, g], ref[0, i, 0:BLK, :]))
            s = row(tail, 3)
            squares[k] = squares[k] + s if k in squares else s
    for k, pairs in sums.items():
        out[k] += joined(pairs, 1, NT)
        sq[k] += jnp.broadcast_to(squares[k], (8, BLK))


def joined(pairs, axis, dims):
    left = jnp.concatenate([p[0] for p in pairs], axis=1)
    right = jnp.concatenate([p[1] for p in pairs], axis=axis)
    return lax.dot_general(left, right, dims, preferred_element_type=F32)


def pre2_kernel(parts, ids, asc, mask, gabs, *refs):
    toks, out = refs[: len(parts)], refs[len(parts)]
    x, zl, c = pl.program_id(0), ids[3], ids[4]

    @pl.when(x == 0)
    def _():
        out[...] = jnp.zeros_like(out)

    scaled, sums = {}, {}
    for (grp, g), ref in zip(parts, toks):
        for i, (k, l) in enumerate(GROUPS[grp]):
            if (l, g) not in scaled:
                at = (zl ^ l) * 2 + (c ^ g)
                fb = x * 4 + at
                scaled[l, g] = (asc[0, at].astype(F32) * mask_rows(mask[fb]) * gabs[fb][0:1]).astype(BF)
            sums.setdefault(k, []).append((scaled[l, g], ref[0, i, 0:BLK, :]))
    for k, pairs in sums.items():
        out[k] += joined(pairs, 1, NT)


def mask_rows(m):
    return jnp.concatenate(
        [jnp.broadcast_to(m[0:1, :], (SUB, BLK)), jnp.broadcast_to(m[1:2, :], (SUB, BLK))], axis=0
    )


def hidden_grads(pre, r, cot):
    gate = pre[0:SUB] * r
    up = pre[SUB:ROWS] * r
    u = cot.astype(F32)
    inner = KC * (gate + KB * gate * gate * gate)
    t = jnp.tanh(inner)
    act = 0.5 * gate * (1.0 + t)
    slope = 0.5 * (1.0 + t) + 0.5 * gate * (1.0 - t * t) * KC * (1.0 + 3.0 * KB * gate * gate)
    return jnp.concatenate([u * up * slope * r, u * act * r], axis=0).astype(BF)


def outer_terms(parts, d, toks):
    where = {p: ref for p, ref in zip(parts, toks)}
    for l in range(2):
        for g in range(2):
            places = [PLACE[k, l] for k in range(4)]
            pairs = [(d[k], where[grp, g][0, i, 0:BLK, :]) for k, (grp, i) in enumerate(places)]
            yield l, g, joined(pairs, 0, NN)


def outer1_kernel(parts, ids, p0, p1, p2, s0, s1, s2, c0, c1, c2, c3, *refs):
    toks, (out, praw, rs, d) = refs[: len(parts)], refs[len(parts) :]
    zl, c = ids[3], ids[4]

    @pl.when(pl.program_id(0) == 0)
    def _():
        for k, cot in enumerate((c0, c1, c2, c3)):
            r = lax.rsqrt((s0[k] + s1[k] + s2[k]) / (NB * BLK) + 1e-06)
            pre = p0[k] + p1[k] + p2[k]
            rs[k] = r
            praw[k] = pre
            d[k] = hidden_grads(pre, r[0:1], cot[ROWS : ROWS + SUB, :])

    for l, g, total in outer_terms(parts, d, toks):
        out[0, (zl ^ l) * 2 + (c ^ g)] = total.astype(BF)


def outer2_kernel(parts, factor, ids, praw, rs, pa, c0, c1, c2, c3, w, asc, mask, *refs):
    toks, (out, dgp, d) = refs[: len(parts)], refs[len(parts) :]
    x, zh, zl, c = pl.program_id(0), ids[1], ids[3], ids[4]
    f = factor[0]

    @pl.when(x == 0)
    def _():
        for k, cot in enumerate((c0, c1, c2, c3)):
            d[k] = hidden_grads(praw[k] + f * pa[k], rs[k][0:1], cot[ROWS : ROWS + SUB, :])

    for l, g, total in outer_terms(parts, d, toks):
        at = (zl ^ l) * 2 + (c ^ g)
        out[0, at] = total.astype(BF)
        fb = x * 4 + at
        wv = w[0, lax.rem(at - zh + 4, 4)].astype(F32)
        wv = wv + f * mask_rows(mask[fb]) * asc[0, at].astype(F32)
        dgp[fb] = jnp.sum(wv * total, axis=0, keepdims=True)


def ascent_kernel(ids, terms, gabs, mask, asc, part):
    y = ids[0]
    acc = jnp.zeros((8, BLK), F32)
    for h in range(4):
        total = terms[0, h].astype(F32)
        for j in range(1, 4):
            total = total + terms[j, h].astype(F32)
        low = (total * gabs[y * 4 + h][0:1]).astype(BF)
        asc[h] = low
        wide = low.astype(F32)
        acc = acc + jnp.sum((mask_rows(mask[y * 4 + h]) * wide * wide).reshape(ROWS // 8, 8, BLK), axis=0)
    part[...] = acc[:, 0:128] + acc[:, 128:256]


def final_kernel(ids, gabs, sums, gate, up):
    g = gabs[ids[0] * 4 + ids[1]][0:1]
    tg = jnp.concatenate([sums[q, 0:SUB, :].astype(F32) for q in range(4)], axis=0) * g
    tu = jnp.concatenate([sums[q, SUB:ROWS, :].astype(F32) for q in range(4)], axis=0) * g
    gate[...] = tg.T
    up[...] = tu.T


def spread(value, axes):
    n = 16
    return lax.all_to_all(jnp.broadcast_to(value[None], (n,) + value.shape), axes, 0, 0, tiled=True)


def body(tokens, norm_gain, w_gate, w_up, cotangent, decay_mask, radius):
    ids = jnp.stack([lax.axis_index(n) for n in NAMES]).astype(jnp.int32)
    mask = decay_mask.astype(F32).reshape(2, NB, BLK).transpose(1, 0, 2)

    piece = hbm((3 * SUB, BLK), BF)
    pack, *pieces = call(
        start_kernel,
        (hbm((PACK, BLK), BF),) + (piece,) * 4,
        [SMEM, whole((BLK, BLK)), whole((1, BLK))] + [whole((BLK, 4 * SUB))] * 3,
        (whole((PACK, BLK)),) + (whole(piece.shape),) * 4,
        scratch=[pltpu.VMEM((3, 4 * SUB, BLK), BF)],
    )(ids, in_hbm(tokens), norm_gain[None, :], in_hbm(w_gate), in_hbm(w_up), in_hbm(cotangent))

    def after(value, *others):
        return lax.optimization_barrier((value,) + others)[0]

    def over_x(value):
        return lax.all_to_all(jnp.broadcast_to(value[None], (4,) + value.shape), "x", 0, 0, tiled=True)

    mids = [from_z(pack, k, 0) for k in (1, 3, 2)]
    near = from_z(pack, 0, 1)
    own_x = over_x(pack[None])
    pieces = [pieces[0]] + [from_z(pieces[k], k, 0) for k in range(1, 4)]
    part_w = jnp.stack([p[:ROWS] for p in pieces])
    mid_x = over_x(after(jnp.stack(mids + [near]), own_x))
    far = from_z(jnp.stack(mids), 0, 1)
    weights = in_hbm(lax.all_gather(after(part_w, far), "y", axis=0, tiled=False))
    far_x = over_x(after(far, part_w, mid_x))
    mine = [in_hbm(v) for v in (own_x, mid_x)]
    toks = {(grp, g): in_hbm(other_core(v)) if g else v for grp, v in enumerate(mine) for g in range(2)}

    pshape, sshape, gshape = shape((4, ROWS, BLK), F32), shape((4, 8, BLK), F32), shape((NB, 8, BLK), F32)
    wspec = by_x((4, ROWS, BLK))

    def tok_spec(grp):
        return by_x((len(GROUPS[grp]), PACK, BLK))

    def pre(parts, with_gain):
        outs = [hbm(pshape.shape, F32) if with_gain else pshape, sshape] + ([gshape] if with_gain else [])
        blocks = sum(len(GROUPS[p[0]]) for p in parts)
        return call(
            functools.partial(pre_kernel, parts, with_gain),
            outs,
            [SMEM, wspec] + [tok_spec(p[0]) for p in parts],
            [whole(s.shape) for s in outs],
            (4,),
            flops=blocks * 4 * 2 * ROWS * BLK * BLK,
            nbytes=blocks * 4 * 2 * PACK * BLK,
        )(ids, weights, *[toks[p] for p in parts])

    p0, s0, gabs = pre(tuple((grp, g) for g in range(2) for grp in (0, 1)), True)
    far_x = after(far_x, p0)
    toks[2, 0], toks[2, 1] = far_x, other_core(far_x)
    p1, s1 = pre(((2, 0),), False)
    p2, s2 = pre(((2, 1),), False)
    parts = tuple((grp, g) for g in range(2) for grp in range(len(GROUPS)))
    tok_specs = [tok_spec(p[0]) for p in parts]
    tok_refs = [toks[p] for p in parts]
    cost = {"flops": 64 * 2 * ROWS * BLK * BLK, "nbytes": 12 * 10**6}
    oshape = hbm((4, 4, ROWS, BLK), BF)
    pspec, sspec = whole(pshape.shape), whole(sshape.shape)
    pieces = [in_hbm(p) for p in pieces]
    dscratch = [pltpu.VMEM((4, ROWS, BLK), BF)]
    out1, praw, rs = call(
        functools.partial(outer1_kernel, parts),
        (oshape, hbm(pshape.shape, F32), hbm(sshape.shape, F32)),
        [SMEM] + [pspec] * 3 + [sspec] * 3 + [whole(piece.shape)] * 4 + tok_specs,
        (by_x((4, ROWS, BLK)), pspec, sspec),
        (4,),
        dscratch,
        **cost,
    )(ids, p0, p1, p2, s0, s1, s2, *pieces, *tok_refs)
    terms = lax.all_to_all(out1, "y", 0, 0, tiled=True)
    asc, part = call(
        ascent_kernel,
        (hbm((4, ROWS, BLK), BF), shape((8, 128), F32)),
        [SMEM, whole(oshape.shape), whole(gshape.shape), whole((NB, 2, BLK))],
        (whole((4, ROWS, BLK)), whole((8, 128))),
    )(ids, terms, gabs, mask)
    ascs = in_hbm(lax.all_gather(asc, "y", axis=0, tiled=False))
    part = spread(jnp.sum(spread(part, MP), axis=0), DP)
    pa = call(
        functools.partial(pre2_kernel, parts),
        hbm(pshape.shape, F32),
        [SMEM, wspec, whole((NB, 2, BLK)), whole(gshape.shape)] + tok_specs,
        whole(pshape.shape),
        (4,),
        **cost,
    )(ids, ascs, mask, gabs, *tok_refs)
    total = jnp.sum(after(part, pa))
    factor = (radius[0] / (jnp.sqrt(total) + 1e-12))[None]
    out2, dgp = call(
        functools.partial(outer2_kernel, parts),
        (oshape, hbm((NB, 1, BLK), F32)),
        [SMEM, SMEM, pspec, sspec, pspec] + [whole(piece.shape)] * 4 + [wspec, wspec, whole((NB, 2, BLK))] + tok_specs,
        (by_x((4, ROWS, BLK)), whole((NB, 1, BLK))),
        (4,),
        dscratch,
        **cost,
    )(factor, ids, in_hbm(praw), in_hbm(rs), in_hbm(pa), *pieces, weights, ascs, mask, *tok_refs)
    sums = lax.psum_scatter(out2, "y", scatter_dimension=0, tiled=False)
    dg = jnp.sum(lax.all_to_all(dgp, MP, 0, 0, tiled=True), axis=0)
    grad_gain = jnp.sum(spread(dg, DP).reshape(16, BLK), axis=0)
    sums = lax.all_to_all(sums, "zh", 0, 0, tiled=True)
    out = hbm((BLK, 4 * SUB), F32)
    grad_gate, grad_up = call(
        final_kernel,
        (out, out),
        [SMEM, whole(gshape.shape), whole((4, ROWS, BLK))],
        (whole((BLK, 4 * SUB)), whole((BLK, 4 * SUB))),
    )(ids, gabs, sums)
    return grad_gain, grad_gate, grad_up


def solution(mesh):
    fine = Mesh(mesh.devices.reshape(SIZES), NAMES)
    both = P(DP, MP)
    return jax.shard_map(
        body,
        mesh=fine,
        in_specs=(both, P(MP), both, both, both, P(), P()),
        out_specs=(P(MP), both, both),
        check_vma=False,
    )
```

```python
import functools
import jax
import jax.numpy as jnp
from jax import lax
from jax.experimental import pallas as pl
from jax.experimental.pallas import tpu as pltpu
from jax.sharding import Mesh, PartitionSpec as P

SIZES = (4, 4, 4, 2, 2)
NAMES = ("y", "zh", "x", "zl", "c")
DP, MP = ("y", "zh"), ("x", "zl", "c")
BLK = 256
SUB = 96
ROWS = 2 * SUB
NB = 16
PACK = BLK + 16
KC = 0.7978845608
KB = 0.044715
BF = jnp.bfloat16
F32 = jnp.float32
NT = (((1,), (1,)), ((), ()))
NN = (((1,), (0,)), ((), ()))

GROUPS = (
    ((0, 0),),
    ((1, 0), (3, 0), (2, 0), (0, 1)),
    ((1, 1), (3, 1), (2, 1)),
)
PLACE = {b: (g, i) for g, grp in enumerate(GROUPS) for i, b in enumerate(grp)}


def from_z(value, dzh, lz):
    pairs = []
    for zh in range(4):
        for zl in range(2):
            pairs.append((((zh + dzh) % 4) * 2 + (zl ^ lz), zh * 2 + zl))
    return lax.ppermute(value, ("zh", "zl"), pairs)


def other_core(value):
    return lax.ppermute(value, "c", [(0, 1), (1, 0)])


def shape(dims, dtype):
    return jax.ShapeDtypeStruct(dims, dtype)


def call(kernel, out_shape, in_specs, out_specs, grid=(), scratch=(), flops=10**6, nbytes=10**6):
    return pl.pallas_call(
        kernel,
        out_shape=out_shape,
        grid=grid,
        in_specs=in_specs,
        out_specs=out_specs,
        scratch_shapes=scratch,
        compiler_params=pltpu.CompilerParams(vmem_limit_bytes=16 * 1024 * 1024),
        cost_estimate=pl.CostEstimate(flops=flops, bytes_accessed=nbytes, transcendentals=0),
    )


def hbm(dims, dtype):
    return pltpu.HBM(dims, dtype)


def in_hbm(value):
    return pltpu.with_memory_space_constraint(value, pltpu.HBM)


SMEM = pl.BlockSpec(memory_space=pltpu.SMEM)


def whole(dims):
    return pl.BlockSpec(dims, lambda *_: (0,) * len(dims))


def by_x(dims):
    return pl.BlockSpec((1,) + dims, lambda i: (i,) + (0,) * len(dims))


def split3(value):
    hi = value.astype(BF)
    left = value - hi.astype(F32)
    mid = left.astype(BF)
    return [hi, mid, (left - mid.astype(F32)).astype(BF)]


def row(ref_rows, at):
    rows = ref_rows.astype(F32)
    return rows[at : at + 1] + rows[at + 1 : at + 2] + rows[at + 2 : at + 3]


def start_kernel(ids, tokens, gain, w_gate, w_up, cot, pack, packs, p0, p1, p2, p3, turned):
    values = tokens[...].astype(F32)
    squares = jnp.sum((values * values).T, axis=0, keepdims=True)
    pack[0:BLK, :] = tokens[...]
    extra = split3(gain[...]) + split3(squares)
    tail = jnp.concatenate([e.astype(F32) for e in extra] + [jnp.zeros((10, BLK), F32)], axis=0)
    pack[BLK:PACK, :] = tail.astype(BF)
    for i in range(4):
        packs[i, 0] = pack[...]
    for i, ref in enumerate((w_gate, w_up, cot)):
        turned[i] = ref[...].astype(F32).T.astype(BF)
        for k, to in enumerate((p0, p1, p2, p3)):
            q = pl.multiple_of(lax.rem(ids[1] - k + 4, 4) * SUB, SUB)
            to[SUB * i : SUB * (i + 1), :] = turned[i, pl.ds(q, SUB), :]


def pre_kernel(parts, with_gain, ids, w, *refs):
    toks = refs[: len(parts)]
    out, sq = refs[len(parts)], refs[len(parts) + 1]
    gabs = refs[len(parts) + 2] if with_gain else None
    x, zh, zl, c = pl.program_id(0), ids[1], ids[3], ids[4]

    @pl.when(x == 0)
    def _():
        out[...] = jnp.zeros_like(out)
        sq[...] = jnp.zeros_like(sq)

    scaled, sums, squares = {}, {}, {}
    for (grp, g), ref in zip(parts, toks):
        for i, (k, l) in enumerate(GROUPS[grp]):
            tail = ref[0, i, BLK:PACK, :]
            if (l, g) not in scaled:
                gain = row(tail, 0)
                at = (zl ^ l) * 2 + (c ^ g)
                wv = w[0, lax.rem(at - zh + 4, 4)]
                scaled[l, g] = (wv.astype(F32) * gain).astype(BF)
                if gabs is not None:
                    gabs[x * 4 + at] = jnp.broadcast_to(gain, (8, BLK))
            sums.setdefault(k, []).append((scaled[l, g], ref[0, i, 0:BLK, :]))
            s = row(tail, 3)
            squares[k] = squares[k] + s if k in squares else s
    for k, pairs in sums.items():
        out[k] += joined(pairs, 1, NT)
        sq[k] += jnp.broadcast_to(squares[k], (8, BLK))


def joined(pairs, axis, dims):
    left = jnp.concatenate([p[0] for p in pairs], axis=1)
    right = jnp.concatenate([p[1] for p in pairs], axis=axis)
    return lax.dot_general(left, right, dims, preferred_element_type=F32)


def pre2_kernel(parts, ids, asc, mask, gabs, *refs):
    toks, out = refs[: len(parts)], refs[len(parts)]
    x, zl, c = pl.program_id(0), ids[3], ids[4]

    @pl.when(x == 0)
    def _():
        out[...] = jnp.zeros_like(out)

    scaled, sums = {}, {}
    for (grp, g), ref in zip(parts, toks):
        for i, (k, l) in enumerate(GROUPS[grp]):
            if (l, g) not in scaled:
                at = (zl ^ l) * 2 + (c ^ g)
                fb = x * 4 + at
                scaled[l, g] = (asc[0, at].astype(F32) * mask_rows(mask[fb]) * gabs[fb][0:1]).astype(BF)
            sums.setdefault(k, []).append((scaled[l, g], ref[0, i, 0:BLK, :]))
    for k, pairs in sums.items():
        out[k] += joined(pairs, 1, NT)


def mask_rows(m):
    return jnp.concatenate(
        [jnp.broadcast_to(m[0:1, :], (SUB, BLK)), jnp.broadcast_to(m[1:2, :], (SUB, BLK))], axis=0
    )


def hidden_grads(pre, r, cot):
    gate = pre[0:SUB] * r
    up = pre[SUB:ROWS] * r
    u = cot.astype(F32)
    inner = KC * (gate + KB * gate * gate * gate)
    t = jnp.tanh(inner)
    act = 0.5 * gate * (1.0 + t)
    slope = 0.5 * (1.0 + t) + 0.5 * gate * (1.0 - t * t) * KC * (1.0 + 3.0 * KB * gate * gate)
    return jnp.concatenate([u * up * slope * r, u * act * r], axis=0).astype(BF)


def outer_terms(parts, d, toks):
    where = {p: ref for p, ref in zip(parts, toks)}
    for l in range(2):
        for g in range(2):
            places = [PLACE[k, l] for k in range(4)]
            pairs = [(d[k], where[grp, g][0, i, 0:BLK, :]) for k, (grp, i) in enumerate(places)]
            yield l, g, joined(pairs, 0, NN)


def outer1_kernel(parts, ids, p0, p1, p2, s0, s1, s2, c0, c1, c2, c3, *refs):
    toks, (out, praw, rs, d) = refs[: len(parts)], refs[len(parts) :]
    zl, c = ids[3], ids[4]

    @pl.when(pl.program_id(0) == 0)
    def _():
        for k, cot in enumerate((c0, c1, c2, c3)):
            r = lax.rsqrt((s0[k] + s1[k] + s2[k]) / (NB * BLK) + 1e-06)
            pre = p0[k] + p1[k] + p2[k]
            rs[k] = r
            praw[k] = pre
            d[k] = hidden_grads(pre, r[0:1], cot[ROWS : ROWS + SUB, :])

    for l, g, total in outer_terms(parts, d, toks):
        out[0, (zl ^ l) * 2 + (c ^ g)] = total.astype(BF)


def outer2_kernel(parts, factor, ids, praw, rs, pa, c0, c1, c2, c3, w, asc, mask, *refs):
    toks, (out, dgp, d) = refs[: len(parts)], refs[len(parts) :]
    x, zh, zl, c = pl.program_id(0), ids[1], ids[3], ids[4]
    f = factor[0]

    @pl.when(x == 0)
    def _():
        for k, cot in enumerate((c0, c1, c2, c3)):
            d[k] = hidden_grads(praw[k] + f * pa[k], rs[k][0:1], cot[ROWS : ROWS + SUB, :])

    for l, g, total in outer_terms(parts, d, toks):
        at = (zl ^ l) * 2 + (c ^ g)
        out[0, at] = total.astype(BF)
        fb = x * 4 + at
        wv = w[0, lax.rem(at - zh + 4, 4)].astype(F32)
        wv = wv + f * mask_rows(mask[fb]) * asc[0, at].astype(F32)
        dgp[fb] = jnp.sum(wv * total, axis=0, keepdims=True)


def ascent_kernel(ids, terms, gabs, mask, asc, part):
    y = ids[0]
    acc = jnp.zeros((8, BLK), F32)
    for h in range(4):
        total = terms[0, h].astype(F32)
        for j in range(1, 4):
            total = total + terms[j, h].astype(F32)
        low = (total * gabs[y * 4 + h][0:1]).astype(BF)
        asc[h] = low
        wide = low.astype(F32)
        acc = acc + jnp.sum((mask_rows(mask[y * 4 + h]) * wide * wide).reshape(ROWS // 8, 8, BLK), axis=0)
    part[...] = acc[:, 0:128] + acc[:, 128:256]


def final_kernel(ids, gabs, sums, gate, up):
    g = gabs[ids[0] * 4 + ids[1]][0:1]
    tg = jnp.concatenate([sums[q, 0:SUB, :].astype(F32) for q in range(4)], axis=0) * g
    tu = jnp.concatenate([sums[q, SUB:ROWS, :].astype(F32) for q in range(4)], axis=0) * g
    gate[...] = tg.T
    up[...] = tu.T


def spread(value, axes):
    n = 16
    return lax.all_to_all(jnp.broadcast_to(value[None], (n,) + value.shape), axes, 0, 0, tiled=True)


def body(tokens, norm_gain, w_gate, w_up, cotangent, decay_mask, radius):
    ids = jnp.stack([lax.axis_index(n) for n in NAMES]).astype(jnp.int32)
    mask = decay_mask.astype(F32).reshape(2, NB, BLK).transpose(1, 0, 2)

    piece = hbm((3 * SUB, BLK), BF)
    pack, packs, *pieces = call(
        start_kernel,
        (hbm((PACK, BLK), BF), hbm((4, 1, PACK, BLK), BF)) + (piece,) * 4,
        [SMEM, whole((BLK, BLK)), whole((1, BLK))] + [whole((BLK, 4 * SUB))] * 3,
        (whole((PACK, BLK)), whole((4, 1, PACK, BLK))) + (whole(piece.shape),) * 4,
        scratch=[pltpu.VMEM((3, 4 * SUB, BLK), BF)],
    )(ids, in_hbm(tokens), norm_gain[None, :], in_hbm(w_gate), in_hbm(w_up), in_hbm(cotangent))

    def after(value, *others):
        return lax.optimization_barrier((value,) + others)[0]

    def over_x(value):
        return lax.all_to_all(jnp.broadcast_to(value[None], (4,) + value.shape), "x", 0, 0, tiled=True)

    mids = [from_z(pack, k, 0) for k in (1, 3, 2)]
    near = from_z(pack, 0, 1)
    own_x = lax.all_to_all(packs, "x", 0, 0, tiled=True)
    pieces = [pieces[0]] + [from_z(pieces[k], k, 0) for k in range(1, 4)]
    part_w = jnp.stack([p[:ROWS] for p in pieces])
    mid_x = over_x(after(jnp.stack(mids + [near]), own_x))
    far = from_z(jnp.stack(mids), 0, 1)
    weights = in_hbm(lax.all_gather(part_w, "y", axis=0, tiled=False))
    far_x = over_x(after(far, part_w, mid_x))
    mine = [in_hbm(v) for v in (own_x, after(mid_x, far))]
    toks = {(grp, g): in_hbm(other_core(v)) if g else v for grp, v in enumerate(mine) for g in range(2)}

    pshape, sshape, gshape = shape((4, ROWS, BLK), F32), shape((4, 8, BLK), F32), shape((NB, 8, BLK), F32)
    wspec = by_x((4, ROWS, BLK))

    def tok_spec(grp):
        return by_x((len(GROUPS[grp]), PACK, BLK))

    def pre(parts, with_gain):
        outs = [hbm(pshape.shape, F32) if with_gain else pshape, sshape] + ([gshape] if with_gain else [])
        blocks = sum(len(GROUPS[p[0]]) for p in parts)
        return call(
            functools.partial(pre_kernel, parts, with_gain),
            outs,
            [SMEM, wspec] + [tok_spec(p[0]) for p in parts],
            [whole(s.shape) for s in outs],
            (4,),
            flops=blocks * 4 * 2 * ROWS * BLK * BLK,
            nbytes=blocks * 4 * 2 * PACK * BLK,
        )(ids, weights, *[toks[p] for p in parts])

    p0, s0, gabs = pre(tuple((grp, g) for g in range(2) for grp in (0, 1)), True)
    far_x = after(far_x, p0)
    toks[2, 0], toks[2, 1] = far_x, other_core(far_x)
    p1, s1 = pre(((2, 0),), False)
    p2, s2 = pre(((2, 1),), False)
    parts = tuple((grp, g) for g in range(2) for grp in range(len(GROUPS)))
    tok_specs = [tok_spec(p[0]) for p in parts]
    tok_refs = [toks[p] for p in parts]
    cost = {"flops": 64 * 2 * ROWS * BLK * BLK, "nbytes": 12 * 10**6}
    oshape = hbm((4, 4, ROWS, BLK), BF)
    pspec, sspec = whole(pshape.shape), whole(sshape.shape)
    pieces = [in_hbm(p) for p in pieces]
    dscratch = [pltpu.VMEM((4, ROWS, BLK), BF)]
    out1, praw, rs = call(
        functools.partial(outer1_kernel, parts),
        (oshape, hbm(pshape.shape, F32), hbm(sshape.shape, F32)),
        [SMEM] + [pspec] * 3 + [sspec] * 3 + [whole(piece.shape)] * 4 + tok_specs,
        (by_x((4, ROWS, BLK)), pspec, sspec),
        (4,),
        dscratch,
        **cost,
    )(ids, p0, p1, p2, s0, s1, s2, *pieces, *tok_refs)
    terms = lax.all_to_all(out1, "y", 0, 0, tiled=True)
    asc, part = call(
        ascent_kernel,
        (hbm((4, ROWS, BLK), BF), shape((8, 128), F32)),
        [SMEM, whole(oshape.shape), whole(gshape.shape), whole((NB, 2, BLK))],
        (whole((4, ROWS, BLK)), whole((8, 128))),
    )(ids, terms, gabs, mask)
    ascs = in_hbm(lax.all_gather(asc, "y", axis=0, tiled=False))
    part = spread(jnp.sum(spread(part, MP), axis=0), DP)
    pa = call(
        functools.partial(pre2_kernel, parts),
        hbm(pshape.shape, F32),
        [SMEM, wspec, whole((NB, 2, BLK)), whole(gshape.shape)] + tok_specs,
        whole(pshape.shape),
        (4,),
        **cost,
    )(ids, ascs, mask, gabs, *tok_refs)
    total = jnp.sum(after(part, pa))
    factor = (radius[0] / (jnp.sqrt(total) + 1e-12))[None]
    out2, dgp = call(
        functools.partial(outer2_kernel, parts),
        (oshape, hbm((NB, 1, BLK), F32)),
        [SMEM, SMEM, pspec, sspec, pspec] + [whole(piece.shape)] * 4 + [wspec, wspec, whole((NB, 2, BLK))] + tok_specs,
        (by_x((4, ROWS, BLK)), whole((NB, 1, BLK))),
        (4,),
        dscratch,
        **cost,
    )(factor, ids, in_hbm(praw), in_hbm(rs), in_hbm(pa), *pieces, weights, ascs, mask, *tok_refs)
    sums = lax.psum_scatter(out2, "y", scatter_dimension=0, tiled=False)
    dg = jnp.sum(lax.all_to_all(dgp, MP, 0, 0, tiled=True), axis=0)
    grad_gain = jnp.sum(spread(dg, DP).reshape(16, BLK), axis=0)
    sums = lax.all_to_all(sums, "zh", 0, 0, tiled=True)
    out = hbm((BLK, 4 * SUB), F32)
    grad_gate, grad_up = call(
        final_kernel,
        (out, out),
        [SMEM, whole(gshape.shape), whole((4, ROWS, BLK))],
        (whole((BLK, 4 * SUB)), whole((BLK, 4 * SUB))),
    )(ids, gabs, sums)
    return grad_gain, grad_gate, grad_up


def solution(mesh):
    fine = Mesh(mesh.devices.reshape(SIZES), NAMES)
    both = P(DP, MP)
    return jax.shard_map(
        body,
        mesh=fine,
        in_specs=(both, P(MP), both, both, both, P(), P()),
        out_specs=(P(MP), both, both),
        check_vma=False,
    )
```

```python
import functools
import jax
import jax.numpy as jnp
from jax import lax
from jax.experimental import pallas as pl
from jax.experimental.pallas import tpu as pltpu
from jax.sharding import Mesh, PartitionSpec as P

SIZES = (4, 4, 4, 2, 2)
NAMES = ("y", "zh", "x", "zl", "c")
DP, MP = ("y", "zh"), ("x", "zl", "c")
BLK = 256
SUB = 96
ROWS = 2 * SUB
NB = 16
PACK = BLK + 16
KC = 0.7978845608
KB = 0.044715
BF = jnp.bfloat16
F32 = jnp.float32
NT = (((1,), (1,)), ((), ()))
NN = (((1,), (0,)), ((), ()))

GROUPS = (
    ((0, 0),),
    ((1, 0), (3, 0), (2, 0), (0, 1)),
    ((1, 1), (3, 1), (2, 1)),
)
PLACE = {b: (g, i) for g, grp in enumerate(GROUPS) for i, b in enumerate(grp)}


def from_z(value, dzh, lz):
    pairs = []
    for zh in range(4):
        for zl in range(2):
            pairs.append((((zh + dzh) % 4) * 2 + (zl ^ lz), zh * 2 + zl))
    return lax.ppermute(value, ("zh", "zl"), pairs)


def other_core(value):
    return lax.ppermute(value, "c", [(0, 1), (1, 0)])


def shape(dims, dtype):
    return jax.ShapeDtypeStruct(dims, dtype)


def call(kernel, out_shape, in_specs, out_specs, grid=(), scratch=(), flops=10**6, nbytes=10**6):
    return pl.pallas_call(
        kernel,
        out_shape=out_shape,
        grid=grid,
        in_specs=in_specs,
        out_specs=out_specs,
        scratch_shapes=scratch,
        compiler_params=pltpu.CompilerParams(vmem_limit_bytes=16 * 1024 * 1024),
        cost_estimate=pl.CostEstimate(flops=flops, bytes_accessed=nbytes, transcendentals=0),
    )


def hbm(dims, dtype):
    return pltpu.HBM(dims, dtype)


def in_hbm(value):
    return pltpu.with_memory_space_constraint(value, pltpu.HBM)


SMEM = pl.BlockSpec(memory_space=pltpu.SMEM)


def whole(dims):
    return pl.BlockSpec(dims, lambda *_: (0,) * len(dims))


def by_x(dims):
    return pl.BlockSpec((1,) + dims, lambda i: (i,) + (0,) * len(dims))


def split3(value):
    hi = value.astype(BF)
    left = value - hi.astype(F32)
    mid = left.astype(BF)
    return [hi, mid, (left - mid.astype(F32)).astype(BF)]


def row(ref_rows, at):
    rows = ref_rows.astype(F32)
    return rows[at : at + 1] + rows[at + 1 : at + 2] + rows[at + 2 : at + 3]


def start_kernel(ids, tokens, gain, w_gate, w_up, cot, pack, packs, p0, p1, p2, p3, turned):
    values = tokens[...].astype(F32)
    squares = jnp.sum((values * values).T, axis=0, keepdims=True)
    pack[0:BLK, :] = tokens[...]
    extra = split3(gain[...]) + split3(squares)
    tail = jnp.concatenate([e.astype(F32) for e in extra] + [jnp.zeros((10, BLK), F32)], axis=0)
    pack[BLK:PACK, :] = tail.astype(BF)
    for i in range(4):
        packs[i, 0] = pack[...]
    for i, ref in enumerate((w_gate, w_up, cot)):
        turned[i] = ref[...].astype(F32).T.astype(BF)
        for k, to in enumerate((p0, p1, p2, p3)):
            q = pl.multiple_of(lax.rem(ids[1] - k + 4, 4) * SUB, SUB)
            to[SUB * i : SUB * (i + 1), :] = turned[i, pl.ds(q, SUB), :]


def pre_kernel(parts, with_gain, ids, w, *refs):
    toks = refs[: len(parts)]
    out, sq = refs[len(parts)], refs[len(parts) + 1]
    gabs = refs[len(parts) + 2] if with_gain else None
    x, zh, zl, c = pl.program_id(0), ids[1], ids[3], ids[4]

    @pl.when(x == 0)
    def _():
        out[...] = jnp.zeros_like(out)
        sq[...] = jnp.zeros_like(sq)

    scaled, sums, squares = {}, {}, {}
    for (grp, g), ref in zip(parts, toks):
        for i, (k, l) in enumerate(GROUPS[grp]):
            tail = ref[0, i, BLK:PACK, :]
            if (l, g) not in scaled:
                gain = row(tail, 0)
                at = (zl ^ l) * 2 + (c ^ g)
                wv = w[0, lax.rem(at - zh + 4, 4)]
                scaled[l, g] = (wv.astype(F32) * gain).astype(BF)
                if gabs is not None:
                    gabs[x * 4 + at] = jnp.broadcast_to(gain, (8, BLK))
            sums.setdefault(k, []).append((scaled[l, g], ref[0, i, 0:BLK, :]))
            s = row(tail, 3)
            squares[k] = squares[k] + s if k in squares else s
    for k, pairs in sums.items():
        out[k] += joined(pairs, 1, NT)
        sq[k] += jnp.broadcast_to(squares[k], (8, BLK))


def joined(pairs, axis, dims):
    left = jnp.concatenate([p[0] for p in pairs], axis=1)
    right = jnp.concatenate([p[1] for p in pairs], axis=axis)
    return lax.dot_general(left, right, dims, preferred_element_type=F32)


def pre2_kernel(parts, ids, asc, mask, gabs, *refs):
    toks, out = refs[: len(parts)], refs[len(parts)]
    x, zl, c = pl.program_id(0), ids[3], ids[4]

    @pl.when(x == 0)
    def _():
        out[...] = jnp.zeros_like(out)

    scaled, sums = {}, {}
    for (grp, g), ref in zip(parts, toks):
        for i, (k, l) in enumerate(GROUPS[grp]):
            if (l, g) not in scaled:
                at = (zl ^ l) * 2 + (c ^ g)
                fb = x * 4 + at
                scaled[l, g] = (asc[0, at].astype(F32) * mask_rows(mask[fb]) * gabs[fb][0:1]).astype(BF)
            sums.setdefault(k, []).append((scaled[l, g], ref[0, i, 0:BLK, :]))
    for k, pairs in sums.items():
        out[k] += joined(pairs, 1, NT)


def mask_rows(m):
    return jnp.concatenate(
        [jnp.broadcast_to(m[0:1, :], (SUB, BLK)), jnp.broadcast_to(m[1:2, :], (SUB, BLK))], axis=0
    )


def hidden_grads(pre, r, cot):
    gate = pre[0:SUB] * r
    up = pre[SUB:ROWS] * r
    u = cot.astype(F32)
    inner = KC * (gate + KB * gate * gate * gate)
    t = jnp.tanh(inner)
    act = 0.5 * gate * (1.0 + t)
    slope = 0.5 * (1.0 + t) + 0.5 * gate * (1.0 - t * t) * KC * (1.0 + 3.0 * KB * gate * gate)
    return jnp.concatenate([u * up * slope * r, u * act * r], axis=0).astype(BF)


def outer_terms(parts, d, toks):
    where = {p: ref for p, ref in zip(parts, toks)}
    for l in range(2):
        for g in range(2):
            places = [PLACE[k, l] for k in range(4)]
            pairs = [(d[k], where[grp, g][0, i, 0:BLK, :]) for k, (grp, i) in enumerate(places)]
            yield l, g, joined(pairs, 0, NN)


def outer1_kernel(parts, ids, p0, p1, p2, s0, s1, s2, c0, c1, c2, c3, *refs):
    toks, (out, praw, rs, d) = refs[: len(parts)], refs[len(parts) :]
    zl, c = ids[3], ids[4]

    @pl.when(pl.program_id(0) == 0)
    def _():
        for k, cot in enumerate((c0, c1, c2, c3)):
            r = lax.rsqrt((s0[k] + s1[k] + s2[k]) / (NB * BLK) + 1e-06)
            pre = p0[k] + p1[k] + p2[k]
            rs[k] = r
            praw[k] = pre
            d[k] = hidden_grads(pre, r[0:1], cot[ROWS : ROWS + SUB, :])

    for l, g, total in outer_terms(parts, d, toks):
        out[0, (zl ^ l) * 2 + (c ^ g)] = total.astype(BF)


def outer2_kernel(parts, radius, ids, totals, praw, rs, pa, c0, c1, c2, c3, w, asc, mask, *refs):
    toks, (out, dgp, d) = refs[: len(parts)], refs[len(parts) :]
    x, zh, zl, c = pl.program_id(0), ids[1], ids[3], ids[4]
    total = jnp.sum(jnp.sum(jnp.sum(totals[...], axis=0), axis=0, keepdims=True), axis=1, keepdims=True)
    f = radius[0] / (jnp.sqrt(total) + 1e-12)

    @pl.when(x == 0)
    def _():
        for k, cot in enumerate((c0, c1, c2, c3)):
            d[k] = hidden_grads(praw[k] + f * pa[k], rs[k][0:1], cot[ROWS : ROWS + SUB, :])

    for l, g, total in outer_terms(parts, d, toks):
        at = (zl ^ l) * 2 + (c ^ g)
        out[0, at] = total.astype(BF)
        fb = x * 4 + at
        wv = w[0, lax.rem(at - zh + 4, 4)].astype(F32)
        wv = wv + f * mask_rows(mask[fb]) * asc[0, at].astype(F32)
        dgp[fb] = jnp.sum(wv * total, axis=0, keepdims=True)


def ascent_kernel(ids, terms, gabs, mask, asc, part, acc):
    h = pl.program_id(0)
    fb = ids[0] * 4 + h
    total = terms[0, 0].astype(F32)
    for j in range(1, 4):
        total = total + terms[j, 0].astype(F32)
    low = (total * gabs[fb][0:1]).astype(BF)
    asc[0] = low
    wide = low.astype(F32)
    here = jnp.sum((mask_rows(mask[fb]) * wide * wide).reshape(ROWS // 8, 8, BLK), axis=0)
    here = here[:, 0:128] + here[:, 128:256]

    @pl.when(h == 0)
    def _():
        acc[...] = here

    @pl.when(h > 0)
    def _():
        acc[...] += here

    @pl.when(h == 3)
    def _():
        for i in range(16):
            part[i] = acc[...]


def final_kernel(ids, gabs, sums, gate, up):
    g = gabs[ids[0] * 4 + ids[1]][0:1]
    tg = jnp.concatenate([sums[q, 0:SUB, :].astype(F32) for q in range(4)], axis=0) * g
    tu = jnp.concatenate([sums[q, SUB:ROWS, :].astype(F32) for q in range(4)], axis=0) * g
    gate[...] = tg.T
    up[...] = tu.T


def spread(value, axes):
    n = 16
    return lax.all_to_all(jnp.broadcast_to(value[None], (n,) + value.shape), axes, 0, 0, tiled=True)


def body(tokens, norm_gain, w_gate, w_up, cotangent, decay_mask, radius):
    ids = jnp.stack([lax.axis_index(n) for n in NAMES]).astype(jnp.int32)
    mask = decay_mask.astype(F32).reshape(2, NB, BLK).transpose(1, 0, 2)

    piece = hbm((3 * SUB, BLK), BF)
    pack, packs, *pieces = call(
        start_kernel,
        (hbm((PACK, BLK), BF), hbm((4, 1, PACK, BLK), BF)) + (piece,) * 4,
        [SMEM, whole((BLK, BLK)), whole((1, BLK))] + [whole((BLK, 4 * SUB))] * 3,
        (whole((PACK, BLK)), whole((4, 1, PACK, BLK))) + (whole(piece.shape),) * 4,
        scratch=[pltpu.VMEM((3, 4 * SUB, BLK), BF)],
    )(ids, in_hbm(tokens), in_hbm(norm_gain[None, :]), in_hbm(w_gate), in_hbm(w_up), in_hbm(cotangent))

    def after(value, *others):
        return lax.optimization_barrier((value,) + others)[0]

    def over_x(value):
        return lax.all_to_all(jnp.broadcast_to(value[None], (4,) + value.shape), "x", 0, 0, tiled=True)

    mids = [from_z(pack, k, 0) for k in (1, 3, 2)]
    near = from_z(pack, 0, 1)
    own_x = lax.all_to_all(packs, "x", 0, 0, tiled=True)
    pieces = [pieces[0]] + [from_z(pieces[k], k, 0) for k in range(1, 4)]
    part_w = jnp.stack([p[:ROWS] for p in pieces])
    mid_x = over_x(after(jnp.stack(mids + [near]), own_x))
    far = from_z(jnp.stack(mids), 0, 1)
    weights = in_hbm(lax.all_gather(part_w, "y", axis=0, tiled=False))
    far_x = over_x(after(far, part_w, mid_x))
    mine = [in_hbm(v) for v in (own_x, after(mid_x, far))]
    toks = {(grp, g): in_hbm(other_core(v)) if g else v for grp, v in enumerate(mine) for g in range(2)}

    pshape, sshape, gshape = shape((4, ROWS, BLK), F32), shape((4, 8, BLK), F32), shape((NB, 8, BLK), F32)
    wspec = by_x((4, ROWS, BLK))

    def tok_spec(grp):
        return by_x((len(GROUPS[grp]), PACK, BLK))

    def pre(parts, with_gain):
        outs = [hbm(pshape.shape, F32) if with_gain else pshape, sshape] + ([gshape] if with_gain else [])
        blocks = sum(len(GROUPS[p[0]]) for p in parts)
        return call(
            functools.partial(pre_kernel, parts, with_gain),
            outs,
            [SMEM, wspec] + [tok_spec(p[0]) for p in parts],
            [whole(s.shape) for s in outs],
            (4,),
            flops=blocks * 4 * 2 * ROWS * BLK * BLK,
            nbytes=blocks * 4 * 2 * PACK * BLK,
        )(ids, weights, *[toks[p] for p in parts])

    p0, s0, gabs = pre(tuple((grp, g) for g in range(2) for grp in (0, 1)), True)
    far_x = after(far_x, p0)
    toks[2, 0], toks[2, 1] = far_x, other_core(far_x)
    p1, s1 = pre(((2, 0),), False)
    p2, s2 = pre(((2, 1),), False)
    parts = tuple((grp, g) for g in range(2) for grp in range(len(GROUPS)))
    tok_specs = [tok_spec(p[0]) for p in parts]
    tok_refs = [toks[p] for p in parts]
    cost = {"flops": 64 * 2 * ROWS * BLK * BLK, "nbytes": 12 * 10**6}
    oshape = hbm((4, 4, ROWS, BLK), BF)
    pspec, sspec = whole(pshape.shape), whole(sshape.shape)
    pieces = [in_hbm(p) for p in pieces]
    dscratch = [pltpu.VMEM((4, ROWS, BLK), BF)]
    out1, praw, rs = call(
        functools.partial(outer1_kernel, parts),
        (oshape, hbm(pshape.shape, F32), hbm(sshape.shape, F32)),
        [SMEM] + [pspec] * 3 + [sspec] * 3 + [whole(piece.shape)] * 4 + tok_specs,
        (by_x((4, ROWS, BLK)), pspec, sspec),
        (4,),
        dscratch,
        **cost,
    )(ids, p0, p1, p2, s0, s1, s2, *pieces, *tok_refs)
    terms = lax.all_to_all(out1, "y", 0, 0, tiled=True)
    asc, part = call(
        ascent_kernel,
        (hbm((4, ROWS, BLK), BF), hbm((16, 8, 128), F32)),
        [
            SMEM,
            pl.BlockSpec((4, 1, ROWS, BLK), lambda h: (0, h, 0, 0)),
            whole(gshape.shape),
            whole((NB, 2, BLK)),
        ],
        (by_x((ROWS, BLK)), whole((16, 8, 128))),
        (4,),
        [pltpu.VMEM((8, 128), F32)],
    )(ids, terms, gabs, mask)
    ascs = in_hbm(lax.all_gather(asc, "y", axis=0, tiled=False))
    part = lax.all_to_all(part, MP, 0, 0, tiled=True)
    part = spread(jnp.sum(part, axis=0), DP)
    pa = call(
        functools.partial(pre2_kernel, parts),
        hbm(pshape.shape, F32),
        [SMEM, wspec, whole((NB, 2, BLK)), whole(gshape.shape)] + tok_specs,
        whole(pshape.shape),
        (4,),
        **cost,
    )(ids, ascs, mask, gabs, *tok_refs)
    out2, dgp = call(
        functools.partial(outer2_kernel, parts),
        (oshape, hbm((NB, 1, BLK), F32)),
        [SMEM, SMEM, whole((16, 8, 128)), pspec, sspec, pspec] + [whole(piece.shape)] * 4 + [wspec, wspec, whole((NB, 2, BLK))] + tok_specs,
        (by_x((4, ROWS, BLK)), whole((NB, 1, BLK))),
        (4,),
        dscratch,
        **cost,
    )(radius, ids, after(part, pa), in_hbm(praw), in_hbm(rs), in_hbm(pa), *pieces, weights, ascs, mask, *tok_refs)
    sums = lax.psum_scatter(out2, "y", scatter_dimension=0, tiled=False)
    dg = jnp.sum(lax.all_to_all(dgp, MP, 0, 0, tiled=True), axis=0)
    grad_gain = jnp.sum(spread(dg, DP).reshape(16, BLK), axis=0)
    sums = lax.all_to_all(sums, "zh", 0, 0, tiled=True)
    out = hbm((BLK, 4 * SUB), F32)
    grad_gate, grad_up = call(
        final_kernel,
        (out, out),
        [SMEM, whole(gshape.shape), whole((4, ROWS, BLK))],
        (whole((BLK, 4 * SUB)), whole((BLK, 4 * SUB))),
    )(ids, gabs, sums)
    return grad_gain, grad_gate, grad_up


def solution(mesh):
    fine = Mesh(mesh.devices.reshape(SIZES), NAMES)
    both = P(DP, MP)
    return jax.shard_map(
        body,
        mesh=fine,
        in_specs=(both, P(MP), both, both, both, P(), P()),
        out_specs=(P(MP), both, both),
        check_vma=False,
    )
```

```python
import functools
import jax
import jax.numpy as jnp
from jax import lax
from jax.experimental import pallas as pl
from jax.experimental.pallas import tpu as pltpu
from jax.sharding import Mesh, PartitionSpec as P

SIZES = (4, 4, 4, 2, 2)
NAMES = ("y", "zh", "x", "zl", "c")
DP, MP = ("y", "zh"), ("x", "zl", "c")
BLK = 256
SUB = 96
ROWS = 2 * SUB
NB = 16
PACK = BLK + 16
KC = 0.7978845608
KB = 0.044715
BF = jnp.bfloat16
F32 = jnp.float32
NT = (((1,), (1,)), ((), ()))
NN = (((1,), (0,)), ((), ()))

GROUPS = (
    ((0, 0),),
    ((1, 0), (3, 0), (2, 0), (0, 1)),
    ((1, 1), (3, 1), (2, 1)),
)
PLACE = {b: (g, i) for g, grp in enumerate(GROUPS) for i, b in enumerate(grp)}


def from_z(value, dzh, lz):
    pairs = []
    for zh in range(4):
        for zl in range(2):
            pairs.append((((zh + dzh) % 4) * 2 + (zl ^ lz), zh * 2 + zl))
    return lax.ppermute(value, ("zh", "zl"), pairs)


def other_core(value):
    return lax.ppermute(value, "c", [(0, 1), (1, 0)])


def shape(dims, dtype):
    return jax.ShapeDtypeStruct(dims, dtype)


def call(kernel, out_shape, in_specs, out_specs, grid=(), scratch=(), flops=10**6, nbytes=10**6):
    return pl.pallas_call(
        kernel,
        out_shape=out_shape,
        grid=grid,
        in_specs=in_specs,
        out_specs=out_specs,
        scratch_shapes=scratch,
        compiler_params=pltpu.CompilerParams(vmem_limit_bytes=16 * 1024 * 1024),
        cost_estimate=pl.CostEstimate(flops=flops, bytes_accessed=nbytes, transcendentals=0),
    )


def hbm(dims, dtype):
    return pltpu.HBM(dims, dtype)


def in_hbm(value):
    return pltpu.with_memory_space_constraint(value, pltpu.HBM)


SMEM = pl.BlockSpec(memory_space=pltpu.SMEM)


def whole(dims):
    return pl.BlockSpec(dims, lambda *_: (0,) * len(dims))


def by_x(dims):
    return pl.BlockSpec((1,) + dims, lambda i: (i,) + (0,) * len(dims))


def split3(value):
    hi = value.astype(BF)
    left = value - hi.astype(F32)
    mid = left.astype(BF)
    return [hi, mid, (left - mid.astype(F32)).astype(BF)]


def row(ref_rows, at):
    rows = ref_rows.astype(F32)
    return rows[at : at + 1] + rows[at + 1 : at + 2] + rows[at + 2 : at + 3]


def start_kernel(ids, tokens, gain, w_gate, w_up, cot, pack, packs, p0, p1, p2, p3, turned):
    values = tokens[...].astype(F32)
    squares = jnp.sum((values * values).T, axis=0, keepdims=True)
    pack[0:BLK, :] = tokens[...]
    extra = split3(gain[...]) + split3(squares)
    tail = jnp.concatenate([e.astype(F32) for e in extra] + [jnp.zeros((10, BLK), F32)], axis=0)
    pack[BLK:PACK, :] = tail.astype(BF)
    for i in range(4):
        packs[i, 0] = pack[...]
    for i, ref in enumerate((w_gate, w_up, cot)):
        turned[i] = ref[...].astype(F32).T.astype(BF)
        for k, to in enumerate((p0, p1, p2, p3)):
            q = pl.multiple_of(lax.rem(ids[1] - k + 4, 4) * SUB, SUB)
            to[SUB * i : SUB * (i + 1), :] = turned[i, pl.ds(q, SUB), :]


def pre_kernel(parts, with_gain, ids, w, *refs):
    toks = refs[: len(parts)]
    out, sq = refs[len(parts)], refs[len(parts) + 1]
    gabs = refs[len(parts) + 2] if with_gain else None
    x, zh, zl, c = pl.program_id(0), ids[1], ids[3], ids[4]

    @pl.when(x == 0)
    def _():
        out[...] = jnp.zeros_like(out)
        sq[...] = jnp.zeros_like(sq)

    scaled, sums, squares = {}, {}, {}
    for (grp, g), ref in zip(parts, toks):
        for i, (k, l) in enumerate(GROUPS[grp]):
            tail = ref[0, i, BLK:PACK, :]
            if (l, g) not in scaled:
                gain = row(tail, 0)
                at = (zl ^ l) * 2 + (c ^ g)
                wv = w[0, lax.rem(at - zh + 4, 4)]
                scaled[l, g] = (wv.astype(F32) * gain).astype(BF)
                if gabs is not None:
                    gabs[x * 4 + at] = jnp.broadcast_to(gain, (8, BLK))
            sums.setdefault(k, []).append((scaled[l, g], ref[0, i, 0:BLK, :]))
            s = row(tail, 3)
            squares[k] = squares[k] + s if k in squares else s
    for k, pairs in sums.items():
        out[k] += joined(pairs, 1, NT)
        sq[k] += jnp.broadcast_to(squares[k], (8, BLK))


def joined(pairs, axis, dims):
    left = jnp.concatenate([p[0] for p in pairs], axis=1)
    right = jnp.concatenate([p[1] for p in pairs], axis=axis)
    return lax.dot_general(left, right, dims, preferred_element_type=F32)


def pre2_kernel(parts, ids, asc, mask, gabs, *refs):
    toks, out = refs[: len(parts)], refs[len(parts)]
    x, zl, c = pl.program_id(0), ids[3], ids[4]

    @pl.when(x == 0)
    def _():
        out[...] = jnp.zeros_like(out)

    scaled, sums = {}, {}
    for (grp, g), ref in zip(parts, toks):
        for i, (k, l) in enumerate(GROUPS[grp]):
            if (l, g) not in scaled:
                at = (zl ^ l) * 2 + (c ^ g)
                fb = x * 4 + at
                scaled[l, g] = (asc[0, at].astype(F32) * mask_rows(mask[fb]) * gabs[fb][0:1]).astype(BF)
            sums.setdefault(k, []).append((scaled[l, g], ref[0, i, 0:BLK, :]))
    for k, pairs in sums.items():
        out[k] += joined(pairs, 1, NT)


def mask_rows(m):
    return jnp.concatenate(
        [jnp.broadcast_to(m[0:1, :], (SUB, BLK)), jnp.broadcast_to(m[1:2, :], (SUB, BLK))], axis=0
    )


def hidden_grads(pre, r, cot):
    gate = pre[0:SUB] * r
    up = pre[SUB:ROWS] * r
    u = cot.astype(F32)
    inner = KC * (gate + KB * gate * gate * gate)
    t = jnp.tanh(inner)
    act = 0.5 * gate * (1.0 + t)
    slope = 0.5 * (1.0 + t) + 0.5 * gate * (1.0 - t * t) * KC * (1.0 + 3.0 * KB * gate * gate)
    return jnp.concatenate([u * up * slope * r, u * act * r], axis=0).astype(BF)


def outer_terms(parts, d, toks):
    where = {p: ref for p, ref in zip(parts, toks)}
    for l in range(2):
        for g in range(2):
            places = [PLACE[k, l] for k in range(4)]
            pairs = [(d[k], where[grp, g][0, i, 0:BLK, :]) for k, (grp, i) in enumerate(places)]
            yield l, g, joined(pairs, 0, NN)


def outer1_kernel(parts, ids, p0, p1, s0, s1, c0, c1, c2, c3, w, *refs):
    toks, (out, praw, rs, d) = refs[: len(parts)], refs[len(parts) :]
    i, zh, zl, c = pl.program_id(0), ids[1], ids[3], ids[4]
    grp, g = parts[-1]

    @pl.when(i == 0)
    def _():
        praw[...] = p0[...] + p1[...]
        rs[...] = s0[...] + s1[...]

    @pl.when(i < 4)
    def _():
        wv = w[0, lax.rem((zl ^ 1) * 2 + (c ^ g) - zh + 4, 4)].astype(F32)
        scaled = (wv * row(toks[-1][0, 0, BLK:PACK, :], 0)).astype(BF)
        for j, (k, _) in enumerate(GROUPS[grp]):
            praw[k] += lax.dot_general(scaled, toks[-1][0, j, 0:BLK, :], NT, preferred_element_type=F32)
            rs[k] += jnp.broadcast_to(row(toks[-1][0, j, BLK:PACK, :], 3), (8, BLK))

    @pl.when(i == 4)
    def _():
        for k, cot in enumerate((c0, c1, c2, c3)):
            r = lax.rsqrt(rs[k] / (NB * BLK) + 1e-06)
            rs[k] = r
            d[k] = hidden_grads(praw[k], r[0:1], cot[ROWS : ROWS + SUB, :])

    @pl.when(i >= 4)
    def _():
        for l, h, total in outer_terms(parts, d, toks):
            out[0, (zl ^ l) * 2 + (c ^ h)] = total.astype(BF)


def outer2_kernel(parts, radius, ids, totals, praw, rs, pa, c0, c1, c2, c3, w, asc, mask, *refs):
    toks, (out, dgp, d) = refs[: len(parts)], refs[len(parts) :]
    x, zh, zl, c = pl.program_id(0), ids[1], ids[3], ids[4]
    total = jnp.sum(jnp.sum(jnp.sum(totals[...], axis=0), axis=0, keepdims=True), axis=1, keepdims=True)
    f = radius[0] / (jnp.sqrt(total) + 1e-12)

    @pl.when(x == 0)
    def _():
        for k, cot in enumerate((c0, c1, c2, c3)):
            d[k] = hidden_grads(praw[k] + f * pa[k], rs[k][0:1], cot[ROWS : ROWS + SUB, :])

    for l, g, total in outer_terms(parts, d, toks):
        at = (zl ^ l) * 2 + (c ^ g)
        out[0, at] = total.astype(BF)
        fb = x * 4 + at
        wv = w[0, lax.rem(at - zh + 4, 4)].astype(F32)
        wv = wv + f * mask_rows(mask[fb]) * asc[0, at].astype(F32)
        dgp[fb] = jnp.sum(wv * total, axis=0, keepdims=True)


def ascent_kernel(ids, terms, gabs, mask, asc, part, acc):
    h = pl.program_id(0)
    fb = ids[0] * 4 + h
    total = terms[0, 0].astype(F32)
    for j in range(1, 4):
        total = total + terms[j, 0].astype(F32)
    low = (total * gabs[fb][0:1]).astype(BF)
    asc[0] = low
    wide = low.astype(F32)
    here = jnp.sum((mask_rows(mask[fb]) * wide * wide).reshape(ROWS // 8, 8, BLK), axis=0)
    here = here[:, 0:128] + here[:, 128:256]

    @pl.when(h == 0)
    def _():
        acc[...] = here

    @pl.when(h > 0)
    def _():
        acc[...] += here

    @pl.when(h == 3)
    def _():
        for i in range(16):
            part[i] = acc[...]


def final_kernel(ids, gabs, sums, gate, up):
    g = gabs[ids[0] * 4 + ids[1]][0:1]
    tg = jnp.concatenate([sums[q, 0:SUB, :].astype(F32) for q in range(4)], axis=0) * g
    tu = jnp.concatenate([sums[q, SUB:ROWS, :].astype(F32) for q in range(4)], axis=0) * g
    gate[...] = tg.T
    up[...] = tu.T


def spread(value, axes):
    n = 16
    return lax.all_to_all(jnp.broadcast_to(value[None], (n,) + value.shape), axes, 0, 0, tiled=True)


def body(tokens, norm_gain, w_gate, w_up, cotangent, decay_mask, radius):
    ids = jnp.stack([lax.axis_index(n) for n in NAMES]).astype(jnp.int32)
    mask = decay_mask.astype(F32).reshape(2, NB, BLK).transpose(1, 0, 2)

    piece = hbm((3 * SUB, BLK), BF)
    pack, packs, *pieces = call(
        start_kernel,
        (hbm((PACK, BLK), BF), hbm((4, 1, PACK, BLK), BF)) + (piece,) * 4,
        [SMEM, whole((BLK, BLK)), whole((1, BLK))] + [whole((BLK, 4 * SUB))] * 3,
        (whole((PACK, BLK)), whole((4, 1, PACK, BLK))) + (whole(piece.shape),) * 4,
        scratch=[pltpu.VMEM((3, 4 * SUB, BLK), BF)],
    )(ids, in_hbm(tokens), in_hbm(norm_gain[None, :]), in_hbm(w_gate), in_hbm(w_up), in_hbm(cotangent))

    def after(value, *others):
        return lax.optimization_barrier((value,) + others)[0]

    def over_x(value):
        return lax.all_to_all(jnp.broadcast_to(value[None], (4,) + value.shape), "x", 0, 0, tiled=True)

    mids = [from_z(pack, k, 0) for k in (1, 3, 2)]
    near = from_z(pack, 0, 1)
    own_x = lax.all_to_all(packs, "x", 0, 0, tiled=True)
    pieces = [pieces[0]] + [from_z(pieces[k], k, 0) for k in range(1, 4)]
    part_w = jnp.stack([p[:ROWS] for p in pieces])
    mid_x = over_x(after(jnp.stack(mids + [near]), own_x))
    far = from_z(jnp.stack(mids), 0, 1)
    weights = in_hbm(lax.all_gather(part_w, "y", axis=0, tiled=False))
    far_x = over_x(after(far, part_w, mid_x))
    mine = [in_hbm(v) for v in (own_x, after(mid_x, far))]
    toks = {(grp, g): in_hbm(other_core(v)) if g else v for grp, v in enumerate(mine) for g in range(2)}

    pshape, sshape, gshape = shape((4, ROWS, BLK), F32), shape((4, 8, BLK), F32), shape((NB, 8, BLK), F32)
    wspec = by_x((4, ROWS, BLK))

    def tok_spec(grp):
        return by_x((len(GROUPS[grp]), PACK, BLK))

    def pre(parts, with_gain):
        outs = [hbm(pshape.shape, F32) if with_gain else pshape, sshape] + ([gshape] if with_gain else [])
        blocks = sum(len(GROUPS[p[0]]) for p in parts)
        return call(
            functools.partial(pre_kernel, parts, with_gain),
            outs,
            [SMEM, wspec] + [tok_spec(p[0]) for p in parts],
            [whole(s.shape) for s in outs],
            (4,),
            flops=blocks * 4 * 2 * ROWS * BLK * BLK,
            nbytes=blocks * 4 * 2 * PACK * BLK,
        )(ids, weights, *[toks[p] for p in parts])

    p0, s0, gabs = pre(tuple((grp, g) for g in range(2) for grp in (0, 1)), True)
    far_x = after(far_x, p0)
    toks[2, 0], toks[2, 1] = far_x, other_core(far_x)
    p1, s1 = pre(((2, 0),), False)
    parts = tuple((grp, g) for g in range(2) for grp in range(len(GROUPS)))
    tok_specs = [tok_spec(p[0]) for p in parts]
    tok_refs = [toks[p] for p in parts]
    cost = {"flops": 64 * 2 * ROWS * BLK * BLK, "nbytes": 12 * 10**6}
    oshape = hbm((4, 4, ROWS, BLK), BF)
    pspec, sspec = whole(pshape.shape), whole(sshape.shape)
    pieces = [in_hbm(p) for p in pieces]
    dscratch = [pltpu.VMEM((4, ROWS, BLK), BF)]
    def late(dims):
        return pl.BlockSpec((1,) + dims, lambda i: (jnp.maximum(i - 4, 0),) + (0,) * len(dims))

    late_specs = [late((len(GROUPS[p[0]]), PACK, BLK)) for p in parts[:-1]]
    both_spec = pl.BlockSpec((1, len(GROUPS[2]), PACK, BLK), lambda i: (lax.rem(i, 4), 0, 0, 0))
    early_w = pl.BlockSpec((1, 4, ROWS, BLK), lambda i: (jnp.minimum(i, 3), 0, 0, 0))
    out1, praw, rs = call(
        functools.partial(outer1_kernel, parts),
        (oshape, hbm(pshape.shape, F32), hbm(sshape.shape, F32)),
        [SMEM] + [pspec] * 2 + [sspec] * 2 + [whole(piece.shape)] * 4 + [early_w] + late_specs + [both_spec],
        (late((4, ROWS, BLK)), pspec, sspec),
        (8,),
        dscratch,
        **cost,
    )(ids, p0, p1, s0, s1, *pieces, weights, *tok_refs)
    terms = lax.all_to_all(out1, "y", 0, 0, tiled=True)
    asc, part = call(
        ascent_kernel,
        (hbm((4, ROWS, BLK), BF), hbm((16, 8, 128), F32)),
        [
            SMEM,
            pl.BlockSpec((4, 1, ROWS, BLK), lambda h: (0, h, 0, 0)),
            whole(gshape.shape),
            whole((NB, 2, BLK)),
        ],
        (by_x((ROWS, BLK)), whole((16, 8, 128))),
        (4,),
        [pltpu.VMEM((8, 128), F32)],
    )(ids, terms, gabs, mask)
    ascs = in_hbm(lax.all_gather(asc, "y", axis=0, tiled=False))
    part = lax.all_to_all(part, MP, 0, 0, tiled=True)
    part = spread(jnp.sum(part, axis=0), DP)
    pa = call(
        functools.partial(pre2_kernel, parts),
        hbm(pshape.shape, F32),
        [SMEM, wspec, whole((NB, 2, BLK)), whole(gshape.shape)] + tok_specs,
        whole(pshape.shape),
        (4,),
        **cost,
    )(ids, ascs, mask, gabs, *tok_refs)
    out2, dgp = call(
        functools.partial(outer2_kernel, parts),
        (oshape, hbm((NB, 1, BLK), F32)),
        [SMEM, SMEM, whole((16, 8, 128)), pspec, sspec, pspec] + [whole(piece.shape)] * 4 + [wspec, wspec, whole((NB, 2, BLK))] + tok_specs,
        (by_x((4, ROWS, BLK)), whole((NB, 1, BLK))),
        (4,),
        dscratch,
        **cost,
    )(radius, ids, after(part, pa), in_hbm(praw), in_hbm(rs), in_hbm(pa), *pieces, weights, ascs, mask, *tok_refs)
    sums = lax.psum_scatter(out2, "y", scatter_dimension=0, tiled=False)
    dg = jnp.sum(lax.all_to_all(dgp, MP, 0, 0, tiled=True), axis=0)
    grad_gain = jnp.sum(spread(dg, DP).reshape(16, BLK), axis=0)
    sums = lax.all_to_all(sums, "zh", 0, 0, tiled=True)
    out = hbm((BLK, 4 * SUB), F32)
    grad_gate, grad_up = call(
        final_kernel,
        (out, out),
        [SMEM, whole(gshape.shape), whole((4, ROWS, BLK))],
        (whole((BLK, 4 * SUB)), whole((BLK, 4 * SUB))),
    )(ids, gabs, sums)
    return grad_gain, grad_gate, grad_up


def solution(mesh):
    fine = Mesh(mesh.devices.reshape(SIZES), NAMES)
    both = P(DP, MP)
    return jax.shard_map(
        body,
        mesh=fine,
        in_specs=(both, P(MP), both, both, both, P(), P()),
        out_specs=(P(MP), both, both),
        check_vma=False,
    )
```

```python
import functools
import jax
import jax.numpy as jnp
from jax import lax
from jax.experimental import pallas as pl
from jax.experimental.pallas import tpu as pltpu
from jax.sharding import Mesh, PartitionSpec as P

SIZES = (4, 4, 4, 2, 2)
NAMES = ("y", "zh", "x", "zl", "c")
DP, MP = ("y", "zh"), ("x", "zl", "c")
BLK = 256
SUB = 96
ROWS = 2 * SUB
NB = 16
PACK = BLK + 16
KC = 0.7978845608
KB = 0.044715
BF = jnp.bfloat16
F32 = jnp.float32
NT = (((1,), (1,)), ((), ()))
NN = (((1,), (0,)), ((), ()))

GROUPS = (
    ((0, 0),),
    ((1, 0), (3, 0), (2, 0), (0, 1)),
    ((1, 1), (3, 1), (2, 1)),
)
PLACE = {b: (g, i) for g, grp in enumerate(GROUPS) for i, b in enumerate(grp)}


def from_z(value, dzh, lz):
    pairs = []
    for zh in range(4):
        for zl in range(2):
            pairs.append((((zh + dzh) % 4) * 2 + (zl ^ lz), zh * 2 + zl))
    return lax.ppermute(value, ("zh", "zl"), pairs)


def other_core(value):
    return lax.ppermute(value, "c", [(0, 1), (1, 0)])


def shape(dims, dtype):
    return jax.ShapeDtypeStruct(dims, dtype)


def call(kernel, out_shape, in_specs, out_specs, grid=(), scratch=(), flops=10**6, nbytes=10**6):
    return pl.pallas_call(
        kernel,
        out_shape=out_shape,
        grid=grid,
        in_specs=in_specs,
        out_specs=out_specs,
        scratch_shapes=scratch,
        compiler_params=pltpu.CompilerParams(vmem_limit_bytes=16 * 1024 * 1024),
        cost_estimate=pl.CostEstimate(flops=flops, bytes_accessed=nbytes, transcendentals=0),
    )


def hbm(dims, dtype):
    return pltpu.HBM(dims, dtype)


def in_hbm(value):
    return pltpu.with_memory_space_constraint(value, pltpu.HBM)


SMEM = pl.BlockSpec(memory_space=pltpu.SMEM)


def whole(dims):
    return pl.BlockSpec(dims, lambda *_: (0,) * len(dims))


def by_x(dims):
    return pl.BlockSpec((1,) + dims, lambda i: (i,) + (0,) * len(dims))


def split3(value):
    hi = value.astype(BF)
    left = value - hi.astype(F32)
    mid = left.astype(BF)
    return [hi, mid, (left - mid.astype(F32)).astype(BF)]


def row(ref_rows, at):
    rows = ref_rows.astype(F32)
    return rows[at : at + 1] + rows[at + 1 : at + 2] + rows[at + 2 : at + 3]


def start_kernel(ids, tokens, gain, w_gate, w_up, cot, pack, packs, p0, p1, p2, p3, turned):
    values = tokens[...].astype(F32)
    squares = jnp.sum((values * values).T, axis=0, keepdims=True)
    pack[0:BLK, :] = tokens[...]
    extra = split3(gain[...]) + split3(squares)
    tail = jnp.concatenate([e.astype(F32) for e in extra] + [jnp.zeros((10, BLK), F32)], axis=0)
    pack[BLK:PACK, :] = tail.astype(BF)
    for i in range(4):
        packs[i, 0] = pack[...]
    for i, ref in enumerate((w_gate, w_up, cot)):
        turned[i] = ref[...].astype(F32).T.astype(BF)
        for k, to in enumerate((p0, p1, p2, p3)):
            q = pl.multiple_of(lax.rem(ids[1] - k + 4, 4) * SUB, SUB)
            to[SUB * i : SUB * (i + 1), :] = turned[i, pl.ds(q, SUB), :]


def pre_kernel(parts, with_gain, ids, w, *refs):
    toks = refs[: len(parts)]
    out, sq = refs[len(parts)], refs[len(parts) + 1]
    gabs = refs[len(parts) + 2] if with_gain else None
    x, zh, zl, c = pl.program_id(0), ids[1], ids[3], ids[4]

    @pl.when(x == 0)
    def _():
        out[...] = jnp.zeros_like(out)
        sq[...] = jnp.zeros_like(sq)

    scaled, sums, squares = {}, {}, {}
    for (grp, g), ref in zip(parts, toks):
        for i, (k, l) in enumerate(GROUPS[grp]):
            tail = ref[0, i, BLK:PACK, :]
            if (l, g) not in scaled:
                gain = row(tail, 0)
                at = (zl ^ l) * 2 + (c ^ g)
                wv = w[0, lax.rem(at - zh + 4, 4)]
                scaled[l, g] = (wv.astype(F32) * gain).astype(BF)
                if gabs is not None:
                    gabs[x * 4 + at] = jnp.broadcast_to(gain, (8, BLK))
            sums.setdefault(k, []).append((scaled[l, g], ref[0, i, 0:BLK, :]))
            s = row(tail, 3)
            squares[k] = squares[k] + s if k in squares else s
    for k, pairs in sums.items():
        out[k] += joined(pairs, 1, NT)
        sq[k] += jnp.broadcast_to(squares[k], (8, BLK))


def joined(pairs, axis, dims):
    left = jnp.concatenate([p[0] for p in pairs], axis=1)
    right = jnp.concatenate([p[1] for p in pairs], axis=axis)
    return lax.dot_general(left, right, dims, preferred_element_type=F32)


def pre2_kernel(parts, ids, asc, mask, gabs, *refs):
    toks, out = refs[: len(parts)], refs[len(parts)]
    x, zl, c = pl.program_id(0), ids[3], ids[4]

    @pl.when(x == 0)
    def _():
        out[...] = jnp.zeros_like(out)

    scaled, sums = {}, {}
    for (grp, g), ref in zip(parts, toks):
        for i, (k, l) in enumerate(GROUPS[grp]):
            if (l, g) not in scaled:
                at = (zl ^ l) * 2 + (c ^ g)
                fb = x * 4 + at
                scaled[l, g] = (asc[0, at].astype(F32) * mask_rows(mask[fb]) * gabs[fb][0:1]).astype(BF)
            sums.setdefault(k, []).append((scaled[l, g], ref[0, i, 0:BLK, :]))
    for k, pairs in sums.items():
        out[k] += joined(pairs, 1, NT)


def mask_rows(m):
    return jnp.concatenate(
        [jnp.broadcast_to(m[0:1, :], (SUB, BLK)), jnp.broadcast_to(m[1:2, :], (SUB, BLK))], axis=0
    )


def hidden_grads(pre, r, cot):
    gate = pre[0:SUB] * r
    up = pre[SUB:ROWS] * r
    u = cot.astype(F32)
    inner = KC * (gate + KB * gate * gate * gate)
    t = jnp.tanh(inner)
    act = 0.5 * gate * (1.0 + t)
    slope = 0.5 * (1.0 + t) + 0.5 * gate * (1.0 - t * t) * KC * (1.0 + 3.0 * KB * gate * gate)
    return jnp.concatenate([u * up * slope * r, u * act * r], axis=0).astype(BF)


def outer_terms(parts, d, toks):
    where = {p: ref for p, ref in zip(parts, toks)}
    for l in range(2):
        for g in range(2):
            places = [PLACE[k, l] for k in range(4)]
            pairs = [(d[k], where[grp, g][0, i, 0:BLK, :]) for k, (grp, i) in enumerate(places)]
            yield l, g, joined(pairs, 0, NN)


def outer1_kernel(parts, ids, p0, p1, s0, s1, c0, c1, c2, c3, w, *refs):
    toks, (out, praw, rs, d) = refs[: len(parts)], refs[len(parts) :]
    i, zh, zl, c = pl.program_id(0), ids[1], ids[3], ids[4]
    grp, g = parts[-1]

    @pl.when(i == 0)
    def _():
        praw[...] = p0[...] + p1[...]
        rs[...] = s0[...] + s1[...]

    @pl.when(i < 4)
    def _():
        wv = w[0, lax.rem((zl ^ 1) * 2 + (c ^ g) - zh + 4, 4)].astype(F32)
        scaled = (wv * row(toks[-1][0, 0, BLK:PACK, :], 0)).astype(BF)
        for j, (k, _) in enumerate(GROUPS[grp]):
            praw[k] += lax.dot_general(scaled, toks[-1][0, j, 0:BLK, :], NT, preferred_element_type=F32)
            rs[k] += jnp.broadcast_to(row(toks[-1][0, j, BLK:PACK, :], 3), (8, BLK))

    @pl.when(i == 4)
    def _():
        for k, cot in enumerate((c0, c1, c2, c3)):
            r = lax.rsqrt(rs[k] / (NB * BLK) + 1e-06)
            rs[k] = r
            d[k] = hidden_grads(praw[k], r[0:1], cot[ROWS : ROWS + SUB, :])

    @pl.when(i >= 4)
    def _():
        for l, h, total in outer_terms(parts, d, toks):
            out[0, (zl ^ l) * 2 + (c ^ h)] = total.astype(BF)


def outer2_kernel(parts, radius, ids, totals, praw, rs, pa, c0, c1, c2, c3, w, asc, mask, *refs):
    toks, (out, dgp, d) = refs[: len(parts)], refs[len(parts) :]
    x, zh, zl, c = pl.program_id(0), ids[1], ids[3], ids[4]
    total = jnp.sum(jnp.sum(jnp.sum(totals[...], axis=0), axis=0, keepdims=True), axis=1, keepdims=True)
    f = radius[0] / (jnp.sqrt(total) + 1e-12)

    @pl.when(x == 0)
    def _():
        for k, cot in enumerate((c0, c1, c2, c3)):
            d[k] = hidden_grads(praw[k] + f * pa[k], rs[k][0:1], cot[ROWS : ROWS + SUB, :])

    for l, g, total in outer_terms(parts, d, toks):
        at = (zl ^ l) * 2 + (c ^ g)
        out[0, lax.rem(at - zh + 4, 4)] = total.astype(BF)
        fb = x * 4 + at
        wv = w[0, lax.rem(at - zh + 4, 4)].astype(F32)
        wv = wv + f * mask_rows(mask[fb]) * asc[0, at].astype(F32)
        dgp[fb] = jnp.sum(wv * total, axis=0, keepdims=True)


def ascent_kernel(ids, terms, gabs, mask, asc, part):
    acc = jnp.zeros((8, BLK), F32)
    for h in range(4):
        fb = ids[0] * 4 + h
        total = terms[0, h].astype(F32)
        for j in range(1, 4):
            total = total + terms[j, h].astype(F32)
        low = (total * gabs[fb][0:1]).astype(BF)
        asc[h] = low
        wide = low.astype(F32)
        acc = acc + jnp.sum((mask_rows(mask[fb]) * wide * wide).reshape(ROWS // 8, 8, BLK), axis=0)
    acc = acc[:, 0:128] + acc[:, 128:256]
    for i in range(16):
        part[i] = acc


def final_kernel(ids, gabs, b0, b1, b2, b3, gate, up, tg, tu):
    g = gabs[ids[0] * 4 + ids[1]][0:1]
    for k, ref in enumerate((b0, b1, b2, b3)):
        q = pl.multiple_of(lax.rem(ids[1] - k + 4, 4) * SUB, SUB)
        tg[pl.ds(q, SUB), :] = ref[0:SUB, :].astype(F32) * g
        tu[pl.ds(q, SUB), :] = ref[SUB:ROWS, :].astype(F32) * g
    gate[...] = tg[...].T
    up[...] = tu[...].T


def spread(value, axes):
    n = 16
    return lax.all_to_all(jnp.broadcast_to(value[None], (n,) + value.shape), axes, 0, 0, tiled=True)


def body(tokens, norm_gain, w_gate, w_up, cotangent, decay_mask, radius):
    ids = jnp.stack([lax.axis_index(n) for n in NAMES]).astype(jnp.int32)
    mask = decay_mask.astype(F32).reshape(2, NB, BLK).transpose(1, 0, 2)

    piece = hbm((3 * SUB, BLK), BF)
    pack, packs, *pieces = call(
        start_kernel,
        (hbm((PACK, BLK), BF), hbm((4, 1, PACK, BLK), BF)) + (piece,) * 4,
        [SMEM, whole((BLK, BLK)), whole((1, BLK))] + [whole((BLK, 4 * SUB))] * 3,
        (whole((PACK, BLK)), whole((4, 1, PACK, BLK))) + (whole(piece.shape),) * 4,
        scratch=[pltpu.VMEM((3, 4 * SUB, BLK), BF)],
    )(ids, in_hbm(tokens), in_hbm(norm_gain[None, :]), in_hbm(w_gate), in_hbm(w_up), in_hbm(cotangent))

    def after(value, *others):
        return lax.optimization_barrier((value,) + others)[0]

    def over_x(value):
        return lax.all_to_all(jnp.broadcast_to(value[None], (4,) + value.shape), "x", 0, 0, tiled=True)

    mids = [from_z(pack, k, 0) for k in (1, 3, 2)]
    near = from_z(pack, 0, 1)
    own_x = lax.all_to_all(packs, "x", 0, 0, tiled=True)
    pieces = [pieces[0]] + [from_z(pieces[k], k, 0) for k in range(1, 4)]
    part_w = jnp.stack([p[:ROWS] for p in pieces])
    mid_x = over_x(after(jnp.stack(mids + [near]), own_x))
    far = from_z(jnp.stack(mids), 0, 1)
    weights = in_hbm(lax.all_gather(part_w, "y", axis=0, tiled=False))
    far_x = over_x(after(far, part_w, mid_x))
    mine = [in_hbm(v) for v in (own_x, after(mid_x, far))]
    toks = {(grp, g): in_hbm(other_core(v)) if g else v for grp, v in enumerate(mine) for g in range(2)}

    pshape, sshape, gshape = shape((4, ROWS, BLK), F32), shape((4, 8, BLK), F32), shape((NB, 8, BLK), F32)
    wspec = by_x((4, ROWS, BLK))

    def tok_spec(grp):
        return by_x((len(GROUPS[grp]), PACK, BLK))

    def pre(parts, with_gain):
        outs = [hbm(pshape.shape, F32) if with_gain else pshape, sshape] + ([gshape] if with_gain else [])
        blocks = sum(len(GROUPS[p[0]]) for p in parts)
        return call(
            functools.partial(pre_kernel, parts, with_gain),
            outs,
            [SMEM, wspec] + [tok_spec(p[0]) for p in parts],
            [whole(s.shape) for s in outs],
            (4,),
            flops=blocks * 4 * 2 * ROWS * BLK * BLK,
            nbytes=blocks * 4 * 2 * PACK * BLK,
        )(ids, weights, *[toks[p] for p in parts])

    p0, s0, gabs = pre(tuple((grp, g) for g in range(2) for grp in (0, 1)), True)
    far_x = after(far_x, p0)
    toks[2, 0], toks[2, 1] = far_x, other_core(far_x)
    p1, s1 = pre(((2, 0),), False)
    parts = tuple((grp, g) for g in range(2) for grp in range(len(GROUPS)))
    tok_specs = [tok_spec(p[0]) for p in parts]
    tok_refs = [toks[p] for p in parts]
    cost = {"flops": 64 * 2 * ROWS * BLK * BLK, "nbytes": 12 * 10**6}
    oshape = hbm((4, 4, ROWS, BLK), BF)
    pspec, sspec = whole(pshape.shape), whole(sshape.shape)
    pieces = [in_hbm(p) for p in pieces]
    dscratch = [pltpu.VMEM((4, ROWS, BLK), BF)]
    def late(dims):
        return pl.BlockSpec((1,) + dims, lambda i: (jnp.maximum(i - 4, 0),) + (0,) * len(dims))

    late_specs = [late((len(GROUPS[p[0]]), PACK, BLK)) for p in parts[:-1]]
    both_spec = pl.BlockSpec((1, len(GROUPS[2]), PACK, BLK), lambda i: (lax.rem(i, 4), 0, 0, 0))
    early_w = pl.BlockSpec((1, 4, ROWS, BLK), lambda i: (jnp.minimum(i, 3), 0, 0, 0))
    out1, praw, rs = call(
        functools.partial(outer1_kernel, parts),
        (oshape, hbm(pshape.shape, F32), hbm(sshape.shape, F32)),
        [SMEM] + [pspec] * 2 + [sspec] * 2 + [whole(piece.shape)] * 4 + [early_w] + late_specs + [both_spec],
        (late((4, ROWS, BLK)), pspec, sspec),
        (8,),
        dscratch,
        **cost,
    )(ids, p0, p1, s0, s1, *pieces, weights, *tok_refs)
    terms = lax.all_to_all(out1, "y", 0, 0, tiled=True)
    asc, part = call(
        ascent_kernel,
        (hbm((4, ROWS, BLK), BF), hbm((16, 8, 128), F32)),
        [SMEM, whole(oshape.shape), whole(gshape.shape), whole((NB, 2, BLK))],
        (whole((4, ROWS, BLK)), whole((16, 8, 128))),
    )(ids, terms, gabs, mask)
    ascs = in_hbm(lax.all_gather(asc, "y", axis=0, tiled=False))
    part = lax.all_to_all(part, MP, 0, 0, tiled=True)
    part = spread(jnp.sum(part, axis=0), DP)
    pa = call(
        functools.partial(pre2_kernel, parts),
        hbm(pshape.shape, F32),
        [SMEM, wspec, whole((NB, 2, BLK)), whole(gshape.shape)] + tok_specs,
        whole(pshape.shape),
        (4,),
        **cost,
    )(ids, ascs, mask, gabs, *tok_refs)
    out2, dgp = call(
        functools.partial(outer2_kernel, parts),
        (oshape, hbm((NB, 1, BLK), F32)),
        [SMEM, SMEM, whole((16, 8, 128)), pspec, sspec, pspec] + [whole(piece.shape)] * 4 + [wspec, wspec, whole((NB, 2, BLK))] + tok_specs,
        (by_x((4, ROWS, BLK)), whole((NB, 1, BLK))),
        (4,),
        dscratch,
        **cost,
    )(radius, ids, after(part, pa), in_hbm(praw), in_hbm(rs), in_hbm(pa), *pieces, weights, ascs, mask, *tok_refs)
    sums = lax.psum_scatter(out2, "y", scatter_dimension=0, tiled=False)
    dg = jnp.sum(lax.all_to_all(dgp, MP, 0, 0, tiled=True), axis=0)
    grad_gain = jnp.sum(spread(dg, DP).reshape(16, BLK), axis=0)
    sums = [sums[0]] + [from_z(sums[k], 4 - k, 0) for k in range(1, 4)]
    out = hbm((BLK, 4 * SUB), F32)
    grad_gate, grad_up = call(
        final_kernel,
        (out, out),
        [SMEM, whole(gshape.shape)] + [whole((ROWS, BLK))] * 4,
        (whole((BLK, 4 * SUB)), whole((BLK, 4 * SUB))),
        scratch=[pltpu.VMEM((4 * SUB, BLK), F32)] * 2,
    )(ids, gabs, *sums)
    return grad_gain, grad_gate, grad_up


def solution(mesh):
    fine = Mesh(mesh.devices.reshape(SIZES), NAMES)
    both = P(DP, MP)
    return jax.shard_map(
        body,
        mesh=fine,
        in_specs=(both, P(MP), both, both, both, P(), P()),
        out_specs=(P(MP), both, both),
        check_vma=False,
    )
```

```python
import functools
import jax
import jax.numpy as jnp
from jax import lax
from jax.experimental import pallas as pl
from jax.experimental.pallas import tpu as pltpu
from jax.sharding import Mesh, PartitionSpec as P

SIZES = (4, 4, 4, 2, 2)
NAMES = ("y", "zh", "x", "zl", "c")
DP, MP = ("y", "zh"), ("x", "zl", "c")
BLK = 256
SUB = 96
ROWS = 2 * SUB
NB = 16
PACK = BLK + 16
KC = 0.7978845608
KB = 0.044715
BF = jnp.bfloat16
F32 = jnp.float32
NT = (((1,), (1,)), ((), ()))
NN = (((1,), (0,)), ((), ()))

GROUPS = (
    ((0, 0),),
    ((1, 0), (3, 0), (2, 0), (0, 1)),
    ((1, 1), (3, 1), (2, 1)),
)
PLACE = {b: (g, i) for g, grp in enumerate(GROUPS) for i, b in enumerate(grp)}


def from_z(value, dzh, lz):
    pairs = []
    for zh in range(4):
        for zl in range(2):
            pairs.append((((zh + dzh) % 4) * 2 + (zl ^ lz), zh * 2 + zl))
    return lax.ppermute(value, ("zh", "zl"), pairs)


def other_core(value):
    return lax.ppermute(value, "c", [(0, 1), (1, 0)])


def shape(dims, dtype):
    return jax.ShapeDtypeStruct(dims, dtype)


def call(kernel, out_shape, in_specs, out_specs, grid=(), scratch=(), flops=10**6, nbytes=10**6):
    return pl.pallas_call(
        kernel,
        out_shape=out_shape,
        grid=grid,
        in_specs=in_specs,
        out_specs=out_specs,
        scratch_shapes=scratch,
        compiler_params=pltpu.CompilerParams(vmem_limit_bytes=16 * 1024 * 1024),
        cost_estimate=pl.CostEstimate(flops=flops, bytes_accessed=nbytes, transcendentals=0),
    )


def hbm(dims, dtype):
    return pltpu.HBM(dims, dtype)


def in_hbm(value):
    return pltpu.with_memory_space_constraint(value, pltpu.HBM)


SMEM = pl.BlockSpec(memory_space=pltpu.SMEM)


def whole(dims):
    return pl.BlockSpec(dims, lambda *_: (0,) * len(dims))


def by_x(dims):
    return pl.BlockSpec((1,) + dims, lambda i: (i,) + (0,) * len(dims))


def split3(value):
    hi = value.astype(BF)
    left = value - hi.astype(F32)
    mid = left.astype(BF)
    return [hi, mid, (left - mid.astype(F32)).astype(BF)]


def row(ref_rows, at):
    rows = ref_rows.astype(F32)
    return rows[at : at + 1] + rows[at + 1 : at + 2] + rows[at + 2 : at + 3]


def start_kernel(ids, tokens, gain, w_gate, w_up, cot, pack, packs, p0, p1, p2, p3, turned):
    values = tokens[...].astype(F32)
    squares = jnp.sum((values * values).T, axis=0, keepdims=True)
    pack[0:BLK, :] = tokens[...]
    extra = split3(gain[...]) + split3(squares)
    tail = jnp.concatenate([e.astype(F32) for e in extra] + [jnp.zeros((10, BLK), F32)], axis=0)
    pack[BLK:PACK, :] = tail.astype(BF)
    for i in range(4):
        packs[i, 0] = pack[...]
    for i, ref in enumerate((w_gate, w_up, cot)):
        turned[i] = ref[...].astype(F32).T.astype(BF)
        for k, to in enumerate((p0, p1, p2, p3)):
            q = pl.multiple_of(lax.rem(ids[1] - k + 4, 4) * SUB, SUB)
            to[SUB * i : SUB * (i + 1), :] = turned[i, pl.ds(q, SUB), :]


def pre_kernel(parts, with_gain, ids, w, *refs):
    toks = refs[: len(parts)]
    out, sq = refs[len(parts)], refs[len(parts) + 1]
    gabs = refs[len(parts) + 2] if with_gain else None
    x, zh, zl, c = pl.program_id(0), ids[1], ids[3], ids[4]

    @pl.when(x == 0)
    def _():
        out[...] = jnp.zeros_like(out)
        sq[...] = jnp.zeros_like(sq)

    scaled, sums, squares = {}, {}, {}
    for (grp, g), ref in zip(parts, toks):
        for i, (k, l) in enumerate(GROUPS[grp]):
            tail = ref[0, i, BLK:PACK, :]
            if (l, g) not in scaled:
                gain = row(tail, 0)
                at = (zl ^ l) * 2 + (c ^ g)
                wv = w[0, lax.rem(at - zh + 4, 4)]
                scaled[l, g] = (wv.astype(F32) * gain).astype(BF)
                if gabs is not None:
                    gabs[x * 4 + at] = jnp.broadcast_to(gain, (8, BLK))
            sums.setdefault(k, []).append((scaled[l, g], ref[0, i, 0:BLK, :]))
            s = row(tail, 3)
            squares[k] = squares[k] + s if k in squares else s
    for k, pairs in sums.items():
        out[k] += joined(pairs, 1, NT)
        sq[k] += jnp.broadcast_to(squares[k], (8, BLK))


def joined(pairs, axis, dims):
    left = jnp.concatenate([p[0] for p in pairs], axis=1)
    right = jnp.concatenate([p[1] for p in pairs], axis=axis)
    return lax.dot_general(left, right, dims, preferred_element_type=F32)


def pre2_kernel(parts, ids, asc, mask, gabs, *refs):
    toks, out = refs[: len(parts)], refs[len(parts)]
    x, zl, c = pl.program_id(0), ids[3], ids[4]

    @pl.when(x == 0)
    def _():
        out[...] = jnp.zeros_like(out)

    scaled, sums = {}, {}
    for (grp, g), ref in zip(parts, toks):
        for i, (k, l) in enumerate(GROUPS[grp]):
            if (l, g) not in scaled:
                at = (zl ^ l) * 2 + (c ^ g)
                fb = x * 4 + at
                scaled[l, g] = (asc[0, at].astype(F32) * mask_rows(mask[fb]) * gabs[fb][0:1]).astype(BF)
            sums.setdefault(k, []).append((scaled[l, g], ref[0, i, 0:BLK, :]))
    for k, pairs in sums.items():
        out[k] += joined(pairs, 1, NT)


def mask_rows(m):
    return jnp.concatenate(
        [jnp.broadcast_to(m[0:1, :], (SUB, BLK)), jnp.broadcast_to(m[1:2, :], (SUB, BLK))], axis=0
    )


def hidden_grads(pre, r, cot):
    gate = pre[0:SUB] * r
    up = pre[SUB:ROWS] * r
    u = cot.astype(F32)
    inner = KC * (gate + KB * gate * gate * gate)
    t = jnp.tanh(inner)
    act = 0.5 * gate * (1.0 + t)
    slope = 0.5 * (1.0 + t) + 0.5 * gate * (1.0 - t * t) * KC * (1.0 + 3.0 * KB * gate * gate)
    return jnp.concatenate([u * up * slope * r, u * act * r], axis=0).astype(BF)


def outer_terms(parts, d, toks):
    where = {p: ref for p, ref in zip(parts, toks)}
    for l in range(2):
        for g in range(2):
            places = [PLACE[k, l] for k in range(4)]
            pairs = [(d[k], where[grp, g][0, i, 0:BLK, :]) for k, (grp, i) in enumerate(places)]
            yield l, g, joined(pairs, 0, NN)


def outer1_kernel(parts, ids, p0, p1, s0, s1, c0, c1, c2, c3, w, *refs):
    toks, (out, praw, rs, d) = refs[: len(parts)], refs[len(parts) :]
    i, zh, zl, c = pl.program_id(0), ids[1], ids[3], ids[4]
    grp, g = parts[-1]

    @pl.when(i == 0)
    def _():
        praw[...] = p0[...] + p1[...]
        rs[...] = s0[...] + s1[...]

    @pl.when(i < 4)
    def _():
        wv = w[0, lax.rem((zl ^ 1) * 2 + (c ^ g) - zh + 4, 4)].astype(F32)
        scaled = (wv * row(toks[-1][0, 0, BLK:PACK, :], 0)).astype(BF)
        for j, (k, _) in enumerate(GROUPS[grp]):
            praw[k] += lax.dot_general(scaled, toks[-1][0, j, 0:BLK, :], NT, preferred_element_type=F32)
            rs[k] += jnp.broadcast_to(row(toks[-1][0, j, BLK:PACK, :], 3), (8, BLK))

    @pl.when(i == 4)
    def _():
        for k, cot in enumerate((c0, c1, c2, c3)):
            r = lax.rsqrt(rs[k] / (NB * BLK) + 1e-06)
            rs[k] = r
            d[k] = hidden_grads(praw[k], r[0:1], cot[ROWS : ROWS + SUB, :])

    @pl.when(i >= 4)
    def _():
        for l, h, total in outer_terms(parts, d, toks):
            out[0, (zl ^ l) * 2 + (c ^ h)] = total.astype(BF)


def outer2_kernel(parts, radius, ids, totals, praw, rs, pa, c0, c1, c2, c3, w, asc, mask, *refs):
    toks, (out, dgp, d) = refs[: len(parts)], refs[len(parts) :]
    x, zh, zl, c = pl.program_id(0), ids[1], ids[3], ids[4]
    total = jnp.sum(jnp.sum(jnp.sum(totals[...], axis=0), axis=0, keepdims=True), axis=1, keepdims=True)
    f = radius[0] / (jnp.sqrt(total) + 1e-12)

    @pl.when(x == 0)
    def _():
        for k, cot in enumerate((c0, c1, c2, c3)):
            d[k] = hidden_grads(praw[k] + f * pa[k], rs[k][0:1], cot[ROWS : ROWS + SUB, :])

    for l, g, total in outer_terms(parts, d, toks):
        at = (zl ^ l) * 2 + (c ^ g)
        out[0, lax.rem(at - zh + 4, 4)] = total.astype(BF)
        fb = x * 4 + at
        wv = w[0, lax.rem(at - zh + 4, 4)].astype(F32)
        wv = wv + f * mask_rows(mask[fb]) * asc[0, at].astype(F32)
        dgp[fb] = jnp.sum(wv * total, axis=0, keepdims=True)


def ascent_kernel(ids, terms, gabs, mask, asc, part):
    acc = jnp.zeros((8, BLK), F32)
    for h in range(4):
        fb = ids[0] * 4 + h
        total = terms[0, h].astype(F32)
        for j in range(1, 4):
            total = total + terms[j, h].astype(F32)
        low = (total * gabs[fb][0:1]).astype(BF)
        asc[h] = low
        wide = low.astype(F32)
        acc = acc + jnp.sum((mask_rows(mask[fb]) * wide * wide).reshape(ROWS // 8, 8, BLK), axis=0)
    acc = acc[:, 0:128] + acc[:, 128:256]
    for i in range(16):
        part[i] = acc


def final_kernel(ids, gabs, b0, b1, b2, b3, gate, up, tg, tu):
    g = gabs[ids[0] * 4 + ids[1]][0:1]
    for k, ref in enumerate((b0, b1, b2, b3)):
        q = pl.multiple_of(lax.rem(ids[1] - k + 4, 4) * SUB, SUB)
        tg[pl.ds(q, SUB), :] = ref[0:SUB, :].astype(F32) * g
        tu[pl.ds(q, SUB), :] = ref[SUB:ROWS, :].astype(F32) * g
    gate[...] = tg[...].T
    up[...] = tu[...].T


def spread(value, axes):
    n = 16
    return lax.all_to_all(jnp.broadcast_to(value[None], (n,) + value.shape), axes, 0, 0, tiled=True)


def body(tokens, norm_gain, w_gate, w_up, cotangent, decay_mask, radius):
    ids = jnp.stack([lax.axis_index(n) for n in NAMES]).astype(jnp.int32)
    mask = decay_mask.astype(F32).reshape(2, NB, BLK).transpose(1, 0, 2)

    piece = hbm((3 * SUB, BLK), BF)
    pack, packs, *pieces = call(
        start_kernel,
        (hbm((PACK, BLK), BF), hbm((4, 1, PACK, BLK), BF)) + (piece,) * 4,
        [SMEM, whole((BLK, BLK)), whole((1, BLK))] + [whole((BLK, 4 * SUB))] * 3,
        (whole((PACK, BLK)), whole((4, 1, PACK, BLK))) + (whole(piece.shape),) * 4,
        scratch=[pltpu.VMEM((3, 4 * SUB, BLK), BF)],
    )(ids, in_hbm(tokens), in_hbm(norm_gain[None, :]), in_hbm(w_gate), in_hbm(w_up), in_hbm(cotangent))

    def after(value, *others):
        return lax.optimization_barrier((value,) + others)[0]

    def over_x(value):
        return lax.all_to_all(jnp.broadcast_to(value[None], (4,) + value.shape), "x", 0, 0, tiled=True)

    mids = [from_z(pack, k, 0) for k in (1, 3, 2)]
    near = from_z(pack, 0, 1)
    own_x = lax.all_to_all(packs, "x", 0, 0, tiled=True)
    pieces = [pieces[0]] + [from_z(pieces[k], k, 0) for k in range(1, 4)]
    part_w = jnp.stack([p[:ROWS] for p in pieces])
    mid_x = over_x(after(jnp.stack(mids + [near]), own_x))
    far = from_z(jnp.stack(mids), 0, 1)
    weights = in_hbm(lax.all_gather(part_w, "y", axis=0, tiled=False))
    far_x = over_x(after(far, part_w, mid_x))
    mine = [in_hbm(v) for v in (own_x, after(mid_x, far))]
    toks = {(grp, g): in_hbm(other_core(v)) if g else v for grp, v in enumerate(mine) for g in range(2)}

    pshape, sshape, gshape = shape((4, ROWS, BLK), F32), shape((4, 8, BLK), F32), shape((NB, 8, BLK), F32)
    wspec = by_x((4, ROWS, BLK))

    def tok_spec(grp):
        return by_x((len(GROUPS[grp]), PACK, BLK))

    def pre(parts, with_gain):
        outs = [hbm(pshape.shape, F32) if with_gain else pshape, sshape] + ([gshape] if with_gain else [])
        blocks = sum(len(GROUPS[p[0]]) for p in parts)
        return call(
            functools.partial(pre_kernel, parts, with_gain),
            outs,
            [SMEM, wspec] + [tok_spec(p[0]) for p in parts],
            [whole(s.shape) for s in outs],
            (4,),
            flops=blocks * 4 * 2 * ROWS * BLK * BLK,
            nbytes=blocks * 4 * 2 * PACK * BLK,
        )(ids, weights, *[toks[p] for p in parts])

    p0, s0, gabs = pre(tuple((grp, g) for g in range(2) for grp in (0, 1)), True)
    far_x = after(far_x, p0)
    toks[2, 0], toks[2, 1] = far_x, other_core(far_x)
    p1, s1 = pre(((2, 0),), False)
    parts = tuple((grp, g) for g in range(2) for grp in range(len(GROUPS)))
    tok_specs = [tok_spec(p[0]) for p in parts]
    tok_refs = [toks[p] for p in parts]
    cost = {"flops": 64 * 2 * ROWS * BLK * BLK, "nbytes": 12 * 10**6}
    oshape = hbm((4, 4, ROWS, BLK), BF)
    pspec, sspec = whole(pshape.shape), whole(sshape.shape)
    pieces = [in_hbm(p) for p in pieces]
    dscratch = [pltpu.VMEM((4, ROWS, BLK), BF)]
    def late(dims):
        return pl.BlockSpec((1,) + dims, lambda i: (jnp.maximum(i - 4, 0),) + (0,) * len(dims))

    late_specs = [late((len(GROUPS[p[0]]), PACK, BLK)) for p in parts[:-1]]
    both_spec = pl.BlockSpec((1, len(GROUPS[2]), PACK, BLK), lambda i: (lax.rem(i, 4), 0, 0, 0))
    early_w = pl.BlockSpec((1, 4, ROWS, BLK), lambda i: (jnp.minimum(i, 3), 0, 0, 0))
    out1, praw, rs = call(
        functools.partial(outer1_kernel, parts),
        (oshape, hbm(pshape.shape, F32), hbm(sshape.shape, F32)),
        [SMEM] + [pspec] * 2 + [sspec] * 2 + [whole(piece.shape)] * 4 + [early_w] + late_specs + [both_spec],
        (late((4, ROWS, BLK)), pspec, sspec),
        (8,),
        dscratch,
        **cost,
    )(ids, p0, p1, s0, s1, *pieces, weights, *tok_refs)
    terms = lax.all_to_all(out1, "y", 0, 0, tiled=True)
    asc, part = call(
        ascent_kernel,
        (hbm((4, ROWS, BLK), BF), hbm((16, 8, 128), F32)),
        [SMEM, whole(oshape.shape), whole(gshape.shape), whole((NB, 2, BLK))],
        (whole((4, ROWS, BLK)), whole((16, 8, 128))),
    )(ids, terms, gabs, mask)
    ascs = in_hbm(lax.all_gather(asc, "y", axis=0, tiled=False))
    part = lax.all_to_all(part, MP, 0, 0, tiled=True)
    part = spread(jnp.sum(part, axis=0), DP)
    pa = call(
        functools.partial(pre2_kernel, parts),
        hbm(pshape.shape, F32),
        [SMEM, wspec, whole((NB, 2, BLK)), whole(gshape.shape)] + tok_specs,
        whole(pshape.shape),
        (4,),
        **cost,
    )(ids, ascs, mask, gabs, *tok_refs)
    out2, dgp = call(
        functools.partial(outer2_kernel, parts),
        (oshape, hbm((NB, 1, BLK), F32)),
        [SMEM, SMEM, whole((16, 8, 128)), pspec, sspec, pspec] + [whole(piece.shape)] * 4 + [wspec, wspec, whole((NB, 2, BLK))] + tok_specs,
        (by_x((4, ROWS, BLK)), whole((NB, 1, BLK))),
        (4,),
        dscratch,
        **cost,
    )(radius, ids, after(part, pa), in_hbm(praw), in_hbm(rs), in_hbm(pa), *pieces, weights, ascs, mask, *tok_refs)
    sums = lax.psum_scatter(out2, "y", scatter_dimension=0, tiled=False)
    dg = jnp.sum(lax.all_to_all(dgp, MP, 0, 0, tiled=True), axis=0)
    dg = spread(dg, DP)
    sums = after(sums, dg)
    grad_gain = jnp.sum(dg.reshape(16, BLK), axis=0)
    sums = [sums[0]] + [from_z(sums[k], 4 - k, 0) for k in range(1, 4)]
    out = hbm((BLK, 4 * SUB), F32)
    grad_gate, grad_up = call(
        final_kernel,
        (out, out),
        [SMEM, whole(gshape.shape)] + [whole((ROWS, BLK))] * 4,
        (whole((BLK, 4 * SUB)), whole((BLK, 4 * SUB))),
        scratch=[pltpu.VMEM((4 * SUB, BLK), F32)] * 2,
    )(ids, gabs, *sums)
    return grad_gain, grad_gate, grad_up


def solution(mesh):
    fine = Mesh(mesh.devices.reshape(SIZES), NAMES)
    both = P(DP, MP)
    return jax.shard_map(
        body,
        mesh=fine,
        in_specs=(both, P(MP), both, both, both, P(), P()),
        out_specs=(P(MP), both, both),
        check_vma=False,
    )
```

```python
import functools
import jax
import jax.numpy as jnp
from jax import lax
from jax.experimental import pallas as pl
from jax.experimental.pallas import tpu as pltpu
from jax.sharding import Mesh, PartitionSpec as P

SIZES = (4, 4, 4, 2, 2)
NAMES = ("y", "zh", "x", "zl", "c")
DP, MP = ("y", "zh"), ("x", "zl", "c")
BLK = 256
SUB = 96
ROWS = 2 * SUB
NB = 16
PACK = BLK + 16
KC = 0.7978845608
KB = 0.044715
BF = jnp.bfloat16
F32 = jnp.float32
NT = (((1,), (1,)), ((), ()))
NN = (((1,), (0,)), ((), ()))

GROUPS = (
    ((0, 0),),
    ((1, 0), (3, 0), (2, 0), (0, 1)),
    ((1, 1), (3, 1), (2, 1)),
)
PLACE = {b: (g, i) for g, grp in enumerate(GROUPS) for i, b in enumerate(grp)}


def from_z(value, dzh, lz):
    pairs = []
    for zh in range(4):
        for zl in range(2):
            pairs.append((((zh + dzh) % 4) * 2 + (zl ^ lz), zh * 2 + zl))
    return lax.ppermute(value, ("zh", "zl"), pairs)


def other_core(value):
    return lax.ppermute(value, "c", [(0, 1), (1, 0)])


def shape(dims, dtype):
    return jax.ShapeDtypeStruct(dims, dtype)


def call(kernel, out_shape, in_specs, out_specs, grid=(), scratch=(), flops=10**6, nbytes=10**6):
    return pl.pallas_call(
        kernel,
        out_shape=out_shape,
        grid=grid,
        in_specs=in_specs,
        out_specs=out_specs,
        scratch_shapes=scratch,
        compiler_params=pltpu.CompilerParams(vmem_limit_bytes=16 * 1024 * 1024),
        cost_estimate=pl.CostEstimate(flops=flops, bytes_accessed=nbytes, transcendentals=0),
    )


def hbm(dims, dtype):
    return pltpu.HBM(dims, dtype)


def in_hbm(value):
    return pltpu.with_memory_space_constraint(value, pltpu.HBM)


SMEM = pl.BlockSpec(memory_space=pltpu.SMEM)


def whole(dims):
    return pl.BlockSpec(dims, lambda *_: (0,) * len(dims))


def by_x(dims):
    return pl.BlockSpec((1,) + dims, lambda i: (i,) + (0,) * len(dims))


def split3(value):
    hi = value.astype(BF)
    left = value - hi.astype(F32)
    mid = left.astype(BF)
    return [hi, mid, (left - mid.astype(F32)).astype(BF)]


def row(ref_rows, at):
    rows = ref_rows.astype(F32)
    return rows[at : at + 1] + rows[at + 1 : at + 2] + rows[at + 2 : at + 3]


def pack_kernel(tokens, gain, pack, packs):
    values = tokens[...].astype(F32)
    squares = jnp.sum((values * values).T, axis=0, keepdims=True)
    pack[0:BLK, :] = tokens[...]
    extra = split3(gain[...]) + split3(squares)
    tail = jnp.concatenate([e.astype(F32) for e in extra] + [jnp.zeros((10, BLK), F32)], axis=0)
    pack[BLK:PACK, :] = tail.astype(BF)
    for i in range(4):
        packs[i, 0] = pack[...]


def quarter_kernel(ids, w_gate, w_up, cot, p0, p1, p2, p3, turned):
    for i, ref in enumerate((w_gate, w_up, cot)):
        turned[i] = ref[...].astype(F32).T.astype(BF)
        for k, to in enumerate((p0, p1, p2, p3)):
            q = pl.multiple_of(lax.rem(ids[1] - k + 4, 4) * SUB, SUB)
            to[SUB * i : SUB * (i + 1), :] = turned[i, pl.ds(q, SUB), :]


def pre_kernel(parts, with_gain, ids, w, *refs):
    toks = refs[: len(parts)]
    out, sq = refs[len(parts)], refs[len(parts) + 1]
    gabs = refs[len(parts) + 2] if with_gain else None
    x, zh, zl, c = pl.program_id(0), ids[1], ids[3], ids[4]

    @pl.when(x == 0)
    def _():
        out[...] = jnp.zeros_like(out)
        sq[...] = jnp.zeros_like(sq)

    scaled, sums, squares = {}, {}, {}
    for (grp, g), ref in zip(parts, toks):
        for i, (k, l) in enumerate(GROUPS[grp]):
            tail = ref[0, i, BLK:PACK, :]
            if (l, g) not in scaled:
                gain = row(tail, 0)
                at = (zl ^ l) * 2 + (c ^ g)
                wv = w[0, lax.rem(at - zh + 4, 4)]
                scaled[l, g] = (wv.astype(F32) * gain).astype(BF)
                if gabs is not None:
                    gabs[x * 4 + at] = jnp.broadcast_to(gain, (8, BLK))
            sums.setdefault(k, []).append((scaled[l, g], ref[0, i, 0:BLK, :]))
            s = row(tail, 3)
            squares[k] = squares[k] + s if k in squares else s
    for k, pairs in sums.items():
        out[k] += joined(pairs, 1, NT)
        sq[k] += jnp.broadcast_to(squares[k], (8, BLK))


def joined(pairs, axis, dims):
    left = jnp.concatenate([p[0] for p in pairs], axis=1)
    right = jnp.concatenate([p[1] for p in pairs], axis=axis)
    return lax.dot_general(left, right, dims, preferred_element_type=F32)


def pre2_kernel(parts, ids, asc, mask, gabs, *refs):
    toks, out = refs[: len(parts)], refs[len(parts)]
    x, zl, c = pl.program_id(0), ids[3], ids[4]

    @pl.when(x == 0)
    def _():
        out[...] = jnp.zeros_like(out)

    scaled, sums = {}, {}
    for (grp, g), ref in zip(parts, toks):
        for i, (k, l) in enumerate(GROUPS[grp]):
            if (l, g) not in scaled:
                at = (zl ^ l) * 2 + (c ^ g)
                fb = x * 4 + at
                scaled[l, g] = (asc[0, at].astype(F32) * mask_rows(mask[fb]) * gabs[fb][0:1]).astype(BF)
            sums.setdefault(k, []).append((scaled[l, g], ref[0, i, 0:BLK, :]))
    for k, pairs in sums.items():
        out[k] += joined(pairs, 1, NT)


def mask_rows(m):
    return jnp.concatenate(
        [jnp.broadcast_to(m[0:1, :], (SUB, BLK)), jnp.broadcast_to(m[1:2, :], (SUB, BLK))], axis=0
    )


def hidden_grads(pre, r, cot):
    gate = pre[0:SUB] * r
    up = pre[SUB:ROWS] * r
    u = cot.astype(F32)
    inner = KC * (gate + KB * gate * gate * gate)
    t = jnp.tanh(inner)
    act = 0.5 * gate * (1.0 + t)
    slope = 0.5 * (1.0 + t) + 0.5 * gate * (1.0 - t * t) * KC * (1.0 + 3.0 * KB * gate * gate)
    return jnp.concatenate([u * up * slope * r, u * act * r], axis=0).astype(BF)


def outer_terms(parts, d, toks):
    where = {p: ref for p, ref in zip(parts, toks)}
    for l in range(2):
        for g in range(2):
            places = [PLACE[k, l] for k in range(4)]
            pairs = [(d[k], where[grp, g][0, i, 0:BLK, :]) for k, (grp, i) in enumerate(places)]
            yield l, g, joined(pairs, 0, NN)


def outer1_kernel(parts, ids, p0, p1, s0, s1, c0, c1, c2, c3, w, *refs):
    toks, (out, praw, rs, d) = refs[: len(parts)], refs[len(parts) :]
    i, zh, zl, c = pl.program_id(0), ids[1], ids[3], ids[4]
    grp, g = parts[-1]

    @pl.when(i == 0)
    def _():
        praw[...] = p0[...] + p1[...]
        rs[...] = s0[...] + s1[...]

    @pl.when(i < 4)
    def _():
        wv = w[0, lax.rem((zl ^ 1) * 2 + (c ^ g) - zh + 4, 4)].astype(F32)
        scaled = (wv * row(toks[-1][0, 0, BLK:PACK, :], 0)).astype(BF)
        for j, (k, _) in enumerate(GROUPS[grp]):
            praw[k] += lax.dot_general(scaled, toks[-1][0, j, 0:BLK, :], NT, preferred_element_type=F32)
            rs[k] += jnp.broadcast_to(row(toks[-1][0, j, BLK:PACK, :], 3), (8, BLK))

    @pl.when(i == 4)
    def _():
        for k, cot in enumerate((c0, c1, c2, c3)):
            r = lax.rsqrt(rs[k] / (NB * BLK) + 1e-06)
            rs[k] = r
            d[k] = hidden_grads(praw[k], r[0:1], cot[ROWS : ROWS + SUB, :])

    @pl.when(i >= 4)
    def _():
        for l, h, total in outer_terms(parts, d, toks):
            out[0, (zl ^ l) * 2 + (c ^ h)] = total.astype(BF)


def outer2_kernel(parts, radius, ids, totals, praw, rs, pa, c0, c1, c2, c3, w, asc, mask, *refs):
    toks, (out, dgp, d) = refs[: len(parts)], refs[len(parts) :]
    x, zh, zl, c = pl.program_id(0), ids[1], ids[3], ids[4]
    total = jnp.sum(jnp.sum(jnp.sum(totals[...], axis=0), axis=0, keepdims=True), axis=1, keepdims=True)
    f = radius[0] / (jnp.sqrt(total) + 1e-12)

    @pl.when(x == 0)
    def _():
        for k, cot in enumerate((c0, c1, c2, c3)):
            d[k] = hidden_grads(praw[k] + f * pa[k], rs[k][0:1], cot[ROWS : ROWS + SUB, :])

    for l, g, total in outer_terms(parts, d, toks):
        at = (zl ^ l) * 2 + (c ^ g)
        out[0, lax.rem(at - zh + 4, 4)] = total.astype(BF)
        fb = x * 4 + at
        wv = w[0, lax.rem(at - zh + 4, 4)].astype(F32)
        wv = wv + f * mask_rows(mask[fb]) * asc[0, at].astype(F32)
        dgp[fb] = jnp.sum(wv * total, axis=0, keepdims=True)


def ascent_kernel(ids, terms, gabs, mask, asc, part):
    acc = jnp.zeros((8, BLK), F32)
    for h in range(4):
        fb = ids[0] * 4 + h
        total = terms[0, h].astype(F32)
        for j in range(1, 4):
            total = total + terms[j, h].astype(F32)
        low = (total * gabs[fb][0:1]).astype(BF)
        asc[h] = low
        wide = low.astype(F32)
        acc = acc + jnp.sum((mask_rows(mask[fb]) * wide * wide).reshape(ROWS // 8, 8, BLK), axis=0)
    acc = acc[:, 0:128] + acc[:, 128:256]
    for i in range(16):
        part[i] = acc


def final_kernel(ids, gabs, b0, b1, b2, b3, gate, up, tg, tu):
    g = gabs[ids[0] * 4 + ids[1]][0:1]
    for k, ref in enumerate((b0, b1, b2, b3)):
        q = pl.multiple_of(lax.rem(ids[1] - k + 4, 4) * SUB, SUB)
        tg[pl.ds(q, SUB), :] = ref[0:SUB, :].astype(F32) * g
        tu[pl.ds(q, SUB), :] = ref[SUB:ROWS, :].astype(F32) * g
    gate[...] = tg[...].T
    up[...] = tu[...].T


def spread(value, axes):
    n = 16
    return lax.all_to_all(jnp.broadcast_to(value[None], (n,) + value.shape), axes, 0, 0, tiled=True)


def body(tokens, norm_gain, w_gate, w_up, cotangent, decay_mask, radius):
    ids = jnp.stack([lax.axis_index(n) for n in NAMES]).astype(jnp.int32)
    mask = decay_mask.astype(F32).reshape(2, NB, BLK).transpose(1, 0, 2)

    piece = hbm((3 * SUB, BLK), BF)
    pack, packs = call(
        pack_kernel,
        (hbm((PACK, BLK), BF), hbm((4, 1, PACK, BLK), BF)),
        [whole((BLK, BLK)), whole((1, BLK))],
        (whole((PACK, BLK)), whole((4, 1, PACK, BLK))),
    )(in_hbm(tokens), in_hbm(norm_gain[None, :]))
    pieces = call(
        quarter_kernel,
        (piece,) * 4,
        [SMEM] + [whole((BLK, 4 * SUB))] * 3,
        (whole(piece.shape),) * 4,
        scratch=[pltpu.VMEM((3, 4 * SUB, BLK), BF)],
    )(ids, in_hbm(w_gate), in_hbm(w_up), in_hbm(cotangent))

    def after(value, *others):
        return lax.optimization_barrier((value,) + others)[0]

    def over_x(value):
        return lax.all_to_all(jnp.broadcast_to(value[None], (4,) + value.shape), "x", 0, 0, tiled=True)

    mids = [from_z(pack, k, 0) for k in (1, 3, 2)]
    near = from_z(pack, 0, 1)
    own_x = lax.all_to_all(packs, "x", 0, 0, tiled=True)
    pieces = [pieces[0]] + [from_z(pieces[k], k, 0) for k in range(1, 4)]
    part_w = jnp.stack([p[:ROWS] for p in pieces])
    mid_x = over_x(after(jnp.stack(mids + [near]), own_x, pieces[0]))
    far = from_z(jnp.stack(mids), 0, 1)
    weights = in_hbm(lax.all_gather(part_w, "y", axis=0, tiled=False))
    far_x = over_x(after(far, part_w, mid_x))
    mine = [in_hbm(v) for v in (own_x, after(mid_x, far))]
    toks = {(grp, g): in_hbm(other_core(v)) if g else v for grp, v in enumerate(mine) for g in range(2)}

    pshape, sshape, gshape = shape((4, ROWS, BLK), F32), shape((4, 8, BLK), F32), shape((NB, 8, BLK), F32)
    wspec = by_x((4, ROWS, BLK))

    def tok_spec(grp):
        return by_x((len(GROUPS[grp]), PACK, BLK))

    def pre(parts, with_gain):
        outs = [hbm(pshape.shape, F32) if with_gain else pshape, sshape] + ([gshape] if with_gain else [])
        blocks = sum(len(GROUPS[p[0]]) for p in parts)
        return call(
            functools.partial(pre_kernel, parts, with_gain),
            outs,
            [SMEM, wspec] + [tok_spec(p[0]) for p in parts],
            [whole(s.shape) for s in outs],
            (4,),
            flops=blocks * 4 * 2 * ROWS * BLK * BLK,
            nbytes=blocks * 4 * 2 * PACK * BLK,
        )(ids, weights, *[toks[p] for p in parts])

    p0, s0, gabs = pre(tuple((grp, g) for g in range(2) for grp in (0, 1)), True)
    far_x = after(far_x, p0)
    toks[2, 0], toks[2, 1] = far_x, other_core(far_x)
    p1, s1 = pre(((2, 0),), False)
    parts = tuple((grp, g) for g in range(2) for grp in range(len(GROUPS)))
    tok_specs = [tok_spec(p[0]) for p in parts]
    tok_refs = [toks[p] for p in parts]
    cost = {"flops": 64 * 2 * ROWS * BLK * BLK, "nbytes": 12 * 10**6}
    oshape = hbm((4, 4, ROWS, BLK), BF)
    pspec, sspec = whole(pshape.shape), whole(sshape.shape)
    pieces = [in_hbm(p) for p in pieces]
    dscratch = [pltpu.VMEM((4, ROWS, BLK), BF)]
    def late(dims):
        return pl.BlockSpec((1,) + dims, lambda i: (jnp.maximum(i - 4, 0),) + (0,) * len(dims))

    late_specs = [late((len(GROUPS[p[0]]), PACK, BLK)) for p in parts[:-1]]
    both_spec = pl.BlockSpec((1, len(GROUPS[2]), PACK, BLK), lambda i: (lax.rem(i, 4), 0, 0, 0))
    early_w = pl.BlockSpec((1, 4, ROWS, BLK), lambda i: (jnp.minimum(i, 3), 0, 0, 0))
    out1, praw, rs = call(
        functools.partial(outer1_kernel, parts),
        (oshape, hbm(pshape.shape, F32), hbm(sshape.shape, F32)),
        [SMEM] + [pspec] * 2 + [sspec] * 2 + [whole(piece.shape)] * 4 + [early_w] + late_specs + [both_spec],
        (late((4, ROWS, BLK)), pspec, sspec),
        (8,),
        dscratch,
        **cost,
    )(ids, p0, p1, s0, s1, *pieces, weights, *tok_refs)
    terms = lax.all_to_all(out1, "y", 0, 0, tiled=True)
    asc, part = call(
        ascent_kernel,
        (hbm((4, ROWS, BLK), BF), hbm((16, 8, 128), F32)),
        [SMEM, whole(oshape.shape), whole(gshape.shape), whole((NB, 2, BLK))],
        (whole((4, ROWS, BLK)), whole((16, 8, 128))),
    )(ids, terms, gabs, mask)
    ascs = in_hbm(lax.all_gather(asc, "y", axis=0, tiled=False))
    part = lax.all_to_all(part, MP, 0, 0, tiled=True)
    part = spread(jnp.sum(part, axis=0), DP)
    pa = call(
        functools.partial(pre2_kernel, parts),
        hbm(pshape.shape, F32),
        [SMEM, wspec, whole((NB, 2, BLK)), whole(gshape.shape)] + tok_specs,
        whole(pshape.shape),
        (4,),
        **cost,
    )(ids, ascs, mask, gabs, *tok_refs)
    out2, dgp = call(
        functools.partial(outer2_kernel, parts),
        (oshape, hbm((NB, 1, BLK), F32)),
        [SMEM, SMEM, whole((16, 8, 128)), pspec, sspec, pspec] + [whole(piece.shape)] * 4 + [wspec, wspec, whole((NB, 2, BLK))] + tok_specs,
        (by_x((4, ROWS, BLK)), whole((NB, 1, BLK))),
        (4,),
        dscratch,
        **cost,
    )(radius, ids, after(part, pa), in_hbm(praw), in_hbm(rs), in_hbm(pa), *pieces, weights, ascs, mask, *tok_refs)
    sums = lax.psum_scatter(out2, "y", scatter_dimension=0, tiled=False)
    dg = jnp.sum(lax.all_to_all(dgp, MP, 0, 0, tiled=True), axis=0)
    dg = spread(dg, DP)
    sums = after(sums, dg)
    grad_gain = jnp.sum(dg.reshape(16, BLK), axis=0)
    sums = [sums[0]] + [from_z(sums[k], 4 - k, 0) for k in range(1, 4)]
    out = hbm((BLK, 4 * SUB), F32)
    grad_gate, grad_up = call(
        final_kernel,
        (out, out),
        [SMEM, whole(gshape.shape)] + [whole((ROWS, BLK))] * 4,
        (whole((BLK, 4 * SUB)), whole((BLK, 4 * SUB))),
        scratch=[pltpu.VMEM((4 * SUB, BLK), F32)] * 2,
    )(ids, gabs, *sums)
    return grad_gain, grad_gate, grad_up


def solution(mesh):
    fine = Mesh(mesh.devices.reshape(SIZES), NAMES)
    both = P(DP, MP)
    return jax.shard_map(
        body,
        mesh=fine,
        in_specs=(both, P(MP), both, both, both, P(), P()),
        out_specs=(P(MP), both, both),
        check_vma=False,
    )
```

```python
import functools
import jax
import jax.numpy as jnp
from jax import lax
from jax.experimental import pallas as pl
from jax.experimental.pallas import tpu as pltpu
from jax.sharding import Mesh, PartitionSpec as P

SIZES = (4, 4, 4, 2, 2)
NAMES = ("y", "zh", "x", "zl", "c")
DP, MP = ("y", "zh"), ("x", "zl", "c")
BLK = 256
SUB = 96
ROWS = 2 * SUB
NB = 16
PACK = BLK + 16
KC = 0.7978845608
KB = 0.044715
BF = jnp.bfloat16
F32 = jnp.float32
NT = (((1,), (1,)), ((), ()))
NN = (((1,), (0,)), ((), ()))

GROUPS = (
    ((0, 0),),
    ((1, 0), (3, 0), (2, 0), (0, 1)),
    ((1, 1), (3, 1), (2, 1)),
)
PLACE = {b: (g, i) for g, grp in enumerate(GROUPS) for i, b in enumerate(grp)}


def from_z(value, dzh, lz):
    pairs = []
    for zh in range(4):
        for zl in range(2):
            pairs.append((((zh + dzh) % 4) * 2 + (zl ^ lz), zh * 2 + zl))
    return lax.ppermute(value, ("zh", "zl"), pairs)


def other_core(value):
    return lax.ppermute(value, "c", [(0, 1), (1, 0)])


def shape(dims, dtype):
    return jax.ShapeDtypeStruct(dims, dtype)


def call(kernel, out_shape, in_specs, out_specs, grid=(), scratch=(), flops=10**6, nbytes=10**6):
    return pl.pallas_call(
        kernel,
        out_shape=out_shape,
        grid=grid,
        in_specs=in_specs,
        out_specs=out_specs,
        scratch_shapes=scratch,
        compiler_params=pltpu.CompilerParams(vmem_limit_bytes=16 * 1024 * 1024),
        cost_estimate=pl.CostEstimate(flops=flops, bytes_accessed=nbytes, transcendentals=0),
    )


def hbm(dims, dtype):
    return pltpu.HBM(dims, dtype)


def in_hbm(value):
    return pltpu.with_memory_space_constraint(value, pltpu.HBM)


SMEM = pl.BlockSpec(memory_space=pltpu.SMEM)


def whole(dims):
    return pl.BlockSpec(dims, lambda *_: (0,) * len(dims))


def by_x(dims):
    return pl.BlockSpec((1,) + dims, lambda i: (i,) + (0,) * len(dims))


def split3(value):
    hi = value.astype(BF)
    left = value - hi.astype(F32)
    mid = left.astype(BF)
    return [hi, mid, (left - mid.astype(F32)).astype(BF)]


def row(ref_rows, at):
    rows = ref_rows.astype(F32)
    return rows[at : at + 1] + rows[at + 1 : at + 2] + rows[at + 2 : at + 3]


def pack_kernel(tokens, gain, pack, packs):
    values = tokens[...].astype(F32)
    squares = jnp.sum((values * values).T, axis=0, keepdims=True)
    pack[0:BLK, :] = tokens[...]
    extra = split3(gain[...]) + split3(squares)
    tail = jnp.concatenate([e.astype(F32) for e in extra] + [jnp.zeros((10, BLK), F32)], axis=0)
    pack[BLK:PACK, :] = tail.astype(BF)
    for i in range(4):
        packs[i, 0] = pack[...]


def quarter_kernel(ids, w_gate, w_up, cot, p0, p1, p2, p3, turned):
    for i, ref in enumerate((w_gate, w_up, cot)):
        turned[i] = ref[...].astype(F32).T.astype(BF)
        for k, to in enumerate((p0, p1, p2, p3)):
            q = pl.multiple_of(lax.rem(ids[1] - k + 4, 4) * SUB, SUB)
            to[SUB * i : SUB * (i + 1), :] = turned[i, pl.ds(q, SUB), :]


def pre_kernel(parts, with_gain, ids, w, *refs):
    toks = refs[: len(parts)]
    out, sq = refs[len(parts)], refs[len(parts) + 1]
    gabs = refs[len(parts) + 2] if with_gain else None
    x, zh, zl, c = pl.program_id(0), ids[1], ids[3], ids[4]

    @pl.when(x == 0)
    def _():
        out[...] = jnp.zeros_like(out)
        sq[...] = jnp.zeros_like(sq)

    scaled, sums, squares = {}, {}, {}
    for (grp, g), ref in zip(parts, toks):
        for i, (k, l) in enumerate(GROUPS[grp]):
            tail = ref[0, i, BLK:PACK, :]
            if (l, g) not in scaled:
                gain = row(tail, 0)
                at = (zl ^ l) * 2 + (c ^ g)
                wv = w[0, lax.rem(at - zh + 4, 4)]
                scaled[l, g] = (wv.astype(F32) * gain).astype(BF)
                if gabs is not None:
                    gabs[x * 4 + at] = jnp.broadcast_to(gain, (8, BLK))
            sums.setdefault(k, []).append((scaled[l, g], ref[0, i, 0:BLK, :]))
            s = row(tail, 3)
            squares[k] = squares[k] + s if k in squares else s
    for k, pairs in sums.items():
        out[k] += joined(pairs, 1, NT)
        sq[k] += jnp.broadcast_to(squares[k], (8, BLK))


def joined(pairs, axis, dims):
    left = jnp.concatenate([p[0] for p in pairs], axis=1)
    right = jnp.concatenate([p[1] for p in pairs], axis=axis)
    return lax.dot_general(left, right, dims, preferred_element_type=F32)


def pre2_kernel(parts, ids, asc, mask, gabs, *refs):
    toks, out = refs[: len(parts)], refs[len(parts)]
    x, zl, c = pl.program_id(0), ids[3], ids[4]

    @pl.when(x == 0)
    def _():
        out[...] = jnp.zeros_like(out)

    scaled, sums = {}, {}
    for (grp, g), ref in zip(parts, toks):
        for i, (k, l) in enumerate(GROUPS[grp]):
            if (l, g) not in scaled:
                at = (zl ^ l) * 2 + (c ^ g)
                fb = x * 4 + at
                scaled[l, g] = (asc[0, at].astype(F32) * mask_rows(mask[fb]) * gabs[fb][0:1]).astype(BF)
            sums.setdefault(k, []).append((scaled[l, g], ref[0, i, 0:BLK, :]))
    for k, pairs in sums.items():
        out[k] += joined(pairs, 1, NT)


def mask_rows(m):
    return jnp.concatenate(
        [jnp.broadcast_to(m[0:1, :], (SUB, BLK)), jnp.broadcast_to(m[1:2, :], (SUB, BLK))], axis=0
    )


def hidden_grads(pre, r, cot):
    gate = pre[0:SUB] * r
    up = pre[SUB:ROWS] * r
    u = cot.astype(F32)
    inner = KC * (gate + KB * gate * gate * gate)
    t = jnp.tanh(inner)
    act = 0.5 * gate * (1.0 + t)
    slope = 0.5 * (1.0 + t) + 0.5 * gate * (1.0 - t * t) * KC * (1.0 + 3.0 * KB * gate * gate)
    return jnp.concatenate([u * up * slope * r, u * act * r], axis=0).astype(BF)


def outer_terms(parts, d, toks):
    where = {p: ref for p, ref in zip(parts, toks)}
    for l in range(2):
        for g in range(2):
            places = [PLACE[k, l] for k in range(4)]
            pairs = [(d[k], where[grp, g][0, i, 0:BLK, :]) for k, (grp, i) in enumerate(places)]
            yield l, g, joined(pairs, 0, NN)


def outer1_kernel(parts, ids, p0, p1, s0, s1, c0, c1, c2, c3, w, *refs):
    toks, (out, praw, rs, d) = refs[: len(parts)], refs[len(parts) :]
    i, zh, zl, c = pl.program_id(0), ids[1], ids[3], ids[4]
    grp, g = parts[-1]

    @pl.when(i == 0)
    def _():
        praw[...] = p0[...] + p1[...]
        rs[...] = s0[...] + s1[...]

    @pl.when(i < 4)
    def _():
        wv = w[0, lax.rem((zl ^ 1) * 2 + (c ^ g) - zh + 4, 4)].astype(F32)
        scaled = (wv * row(toks[-1][0, 0, BLK:PACK, :], 0)).astype(BF)
        for j, (k, _) in enumerate(GROUPS[grp]):
            praw[k] += lax.dot_general(scaled, toks[-1][0, j, 0:BLK, :], NT, preferred_element_type=F32)
            rs[k] += jnp.broadcast_to(row(toks[-1][0, j, BLK:PACK, :], 3), (8, BLK))

    @pl.when(i == 4)
    def _():
        for k, cot in enumerate((c0, c1, c2, c3)):
            r = lax.rsqrt(rs[k] / (NB * BLK) + 1e-06)
            rs[k] = r
            d[k] = hidden_grads(praw[k], r[0:1], cot[ROWS : ROWS + SUB, :])

    @pl.when(i >= 4)
    def _():
        for l, h, total in outer_terms(parts, d, toks):
            out[0, (zl ^ l) * 2 + (c ^ h)] = total.astype(BF)


def outer2_kernel(parts, radius, ids, totals, praw, rs, pa, c0, c1, c2, c3, w, asc, mask, *refs):
    toks, (out, dgp, d) = refs[: len(parts)], refs[len(parts) :]
    x, zh, zl, c = pl.program_id(0), ids[1], ids[3], ids[4]
    total = jnp.sum(jnp.sum(jnp.sum(totals[...], axis=0), axis=0, keepdims=True), axis=1, keepdims=True)
    f = radius[0] / (jnp.sqrt(total) + 1e-12)

    @pl.when(x == 0)
    def _():
        for k, cot in enumerate((c0, c1, c2, c3)):
            d[k] = hidden_grads(praw[k] + f * pa[k], rs[k][0:1], cot[ROWS : ROWS + SUB, :])

    for l, g, total in outer_terms(parts, d, toks):
        at = (zl ^ l) * 2 + (c ^ g)
        out[0, lax.rem(at - zh + 4, 4)] = total.astype(BF)
        fb = x * 4 + at
        by_w = jnp.sum(w[0, lax.rem(at - zh + 4, 4)].astype(F32) * total, axis=0, keepdims=True)
        by_asc = asc[0, at].astype(F32) * total
        m = mask[fb]
        by_gate = m[0:1] * jnp.sum(by_asc[0:SUB], axis=0, keepdims=True)
        by_up = m[1:2] * jnp.sum(by_asc[SUB:ROWS], axis=0, keepdims=True)
        dgp[fb] = by_w + f * (by_gate + by_up)


def ascent_kernel(ids, terms, gabs, mask, asc, part):
    acc = jnp.zeros((8, BLK), F32)
    for h in range(4):
        fb = ids[0] * 4 + h
        total = terms[0, h].astype(F32)
        for j in range(1, 4):
            total = total + terms[j, h].astype(F32)
        low = (total * gabs[fb][0:1]).astype(BF)
        asc[h] = low
        wide = low.astype(F32)
        acc = acc + jnp.sum((mask_rows(mask[fb]) * wide * wide).reshape(ROWS // 8, 8, BLK), axis=0)
    acc = acc[:, 0:128] + acc[:, 128:256]
    for i in range(16):
        part[i] = acc


def final_kernel(ids, gabs, b0, b1, b2, b3, gate, up, tg, tu):
    g = gabs[ids[0] * 4 + ids[1]][0:1]
    for k, ref in enumerate((b0, b1, b2, b3)):
        q = pl.multiple_of(lax.rem(ids[1] - k + 4, 4) * SUB, SUB)
        tg[pl.ds(q, SUB), :] = ref[0:SUB, :].astype(F32) * g
        tu[pl.ds(q, SUB), :] = ref[SUB:ROWS, :].astype(F32) * g
    gate[...] = tg[...].T
    up[...] = tu[...].T


def spread(value, axes):
    n = 16
    return lax.all_to_all(jnp.broadcast_to(value[None], (n,) + value.shape), axes, 0, 0, tiled=True)


def body(tokens, norm_gain, w_gate, w_up, cotangent, decay_mask, radius):
    ids = jnp.stack([lax.axis_index(n) for n in NAMES]).astype(jnp.int32)
    mask = decay_mask.astype(F32).reshape(2, NB, BLK).transpose(1, 0, 2)

    piece = hbm((3 * SUB, BLK), BF)
    pack, packs = call(
        pack_kernel,
        (hbm((PACK, BLK), BF), hbm((4, 1, PACK, BLK), BF)),
        [whole((BLK, BLK)), whole((1, BLK))],
        (whole((PACK, BLK)), whole((4, 1, PACK, BLK))),
    )(in_hbm(tokens), in_hbm(norm_gain[None, :]))
    pieces = call(
        quarter_kernel,
        (piece,) * 4,
        [SMEM] + [whole((BLK, 4 * SUB))] * 3,
        (whole(piece.shape),) * 4,
        scratch=[pltpu.VMEM((3, 4 * SUB, BLK), BF)],
    )(ids, in_hbm(w_gate), in_hbm(w_up), in_hbm(cotangent))

    def after(value, *others):
        return lax.optimization_barrier((value,) + others)[0]

    def over_x(value):
        return lax.all_to_all(jnp.broadcast_to(value[None], (4,) + value.shape), "x", 0, 0, tiled=True)

    mids = [from_z(pack, k, 0) for k in (1, 3, 2)]
    near = from_z(pack, 0, 1)
    own_x = lax.all_to_all(packs, "x", 0, 0, tiled=True)
    pieces = [pieces[0]] + [from_z(pieces[k], k, 0) for k in range(1, 4)]
    part_w = jnp.stack([p[:ROWS] for p in pieces])
    mid_x = over_x(after(jnp.stack(mids + [near]), own_x, pieces[0]))
    far = from_z(jnp.stack(mids), 0, 1)
    weights = in_hbm(lax.all_gather(part_w, "y", axis=0, tiled=False))
    far_x = over_x(after(far, part_w, mid_x))
    mine = [in_hbm(v) for v in (own_x, after(mid_x, far))]
    toks = {(grp, g): in_hbm(other_core(v)) if g else v for grp, v in enumerate(mine) for g in range(2)}

    pshape, sshape, gshape = shape((4, ROWS, BLK), F32), shape((4, 8, BLK), F32), shape((NB, 8, BLK), F32)
    wspec = by_x((4, ROWS, BLK))

    def tok_spec(grp):
        return by_x((len(GROUPS[grp]), PACK, BLK))

    def pre(parts, with_gain):
        outs = [hbm(pshape.shape, F32) if with_gain else pshape, sshape] + ([gshape] if with_gain else [])
        blocks = sum(len(GROUPS[p[0]]) for p in parts)
        return call(
            functools.partial(pre_kernel, parts, with_gain),
            outs,
            [SMEM, wspec] + [tok_spec(p[0]) for p in parts],
            [whole(s.shape) for s in outs],
            (4,),
            flops=blocks * 4 * 2 * ROWS * BLK * BLK,
            nbytes=blocks * 4 * 2 * PACK * BLK,
        )(ids, weights, *[toks[p] for p in parts])

    p0, s0, gabs = pre(tuple((grp, g) for g in range(2) for grp in (0, 1)), True)
    far_x = after(far_x, p0)
    toks[2, 0], toks[2, 1] = far_x, other_core(far_x)
    p1, s1 = pre(((2, 0),), False)
    parts = tuple((grp, g) for g in range(2) for grp in range(len(GROUPS)))
    tok_specs = [by_x((len(GROUPS[p[0]]), BLK, BLK)) for p in parts]
    tok_refs = [toks[p] for p in parts]
    cost = {"flops": 64 * 2 * ROWS * BLK * BLK, "nbytes": 12 * 10**6}
    oshape = hbm((4, 4, ROWS, BLK), BF)
    pspec, sspec = whole(pshape.shape), whole(sshape.shape)
    pieces = [in_hbm(p) for p in pieces]
    dscratch = [pltpu.VMEM((4, ROWS, BLK), BF)]
    def late(dims):
        return pl.BlockSpec((1,) + dims, lambda i: (jnp.maximum(i - 4, 0),) + (0,) * len(dims))

    late_specs = [late((len(GROUPS[p[0]]), BLK, BLK)) for p in parts[:-1]]
    both_spec = pl.BlockSpec((1, len(GROUPS[2]), PACK, BLK), lambda i: (lax.rem(i, 4), 0, 0, 0))
    early_w = pl.BlockSpec((1, 4, ROWS, BLK), lambda i: (jnp.minimum(i, 3), 0, 0, 0))
    out1, praw, rs = call(
        functools.partial(outer1_kernel, parts),
        (oshape, hbm(pshape.shape, F32), hbm(sshape.shape, F32)),
        [SMEM] + [pspec] * 2 + [sspec] * 2 + [whole(piece.shape)] * 4 + [early_w] + late_specs + [both_spec],
        (late((4, ROWS, BLK)), pspec, sspec),
        (8,),
        dscratch,
        **cost,
    )(ids, p0, p1, s0, s1, *pieces, weights, *tok_refs)
    terms = lax.all_to_all(out1, "y", 0, 0, tiled=True)
    asc, part = call(
        ascent_kernel,
        (hbm((4, ROWS, BLK), BF), hbm((16, 8, 128), F32)),
        [SMEM, whole(oshape.shape), whole(gshape.shape), whole((NB, 2, BLK))],
        (whole((4, ROWS, BLK)), whole((16, 8, 128))),
    )(ids, terms, gabs, mask)
    ascs = in_hbm(lax.all_gather(asc, "y", axis=0, tiled=False))
    part = lax.all_to_all(part, MP, 0, 0, tiled=True)
    part = spread(jnp.sum(part, axis=0), DP)
    pa = call(
        functools.partial(pre2_kernel, parts),
        hbm(pshape.shape, F32),
        [SMEM, wspec, whole((NB, 2, BLK)), whole(gshape.shape)] + tok_specs,
        whole(pshape.shape),
        (4,),
        **cost,
    )(ids, ascs, mask, gabs, *tok_refs)
    out2, dgp = call(
        functools.partial(outer2_kernel, parts),
        (oshape, hbm((NB, 1, BLK), F32)),
        [SMEM, SMEM, whole((16, 8, 128)), pspec, sspec, pspec] + [whole(piece.shape)] * 4 + [wspec, wspec, whole((NB, 2, BLK))] + tok_specs,
        (by_x((4, ROWS, BLK)), whole((NB, 1, BLK))),
        (4,),
        dscratch,
        **cost,
    )(radius, ids, after(part, pa), in_hbm(praw), in_hbm(rs), in_hbm(pa), *pieces, weights, ascs, mask, *tok_refs)
    sums = lax.psum_scatter(out2, "y", scatter_dimension=0, tiled=False)
    dg = jnp.sum(lax.all_to_all(dgp, MP, 0, 0, tiled=True), axis=0)
    dg = spread(dg, DP)
    sums = after(sums, dg)
    grad_gain = jnp.sum(dg.reshape(16, BLK), axis=0)
    sums = [sums[0]] + [from_z(sums[k], 4 - k, 0) for k in range(1, 4)]
    out = hbm((BLK, 4 * SUB), F32)
    grad_gate, grad_up = call(
        final_kernel,
        (out, out),
        [SMEM, whole(gshape.shape)] + [whole((ROWS, BLK))] * 4,
        (whole((BLK, 4 * SUB)), whole((BLK, 4 * SUB))),
        scratch=[pltpu.VMEM((4 * SUB, BLK), F32)] * 2,
    )(ids, gabs, *sums)
    return grad_gain, grad_gate, grad_up


def solution(mesh):
    fine = Mesh(mesh.devices.reshape(SIZES), NAMES)
    both = P(DP, MP)
    return jax.shard_map(
        body,
        mesh=fine,
        in_specs=(both, P(MP), both, both, both, P(), P()),
        out_specs=(P(MP), both, both),
        check_vma=False,
    )
```
